32 devices in a mesh: tile: 8 (over y, x, core), crm: 4 (over z).
Axes of the slice: x: 2, y: 2, z: 4, core: 2. Of those that a mesh axis runs over, the one named last changes fastest.
Arguments:
- thermal_anomaly: float32 [72, 8192], P(None, ('tile', 'crm')), may hold values from -6 to 6
- vapour_anomaly: float32 [72, 8192], P(None, ('tile', 'crm')), may hold values from -6 to 6
- periodic_flow_velocity: float32 [72, 8192], P(None, ('tile', 'crm')), may hold values from -0.8 to 0.8
- processor_assignment: int32 [8192], P(('tile', 'crm')), may hold values from 0 to 31, as said below
- thermal_disturbance: float32 [50, 32, 8192], P(None, None, ('tile', 'crm')), may hold values from -8 to 8
- layer_index_downscale: float32 [50, 72], replicated, may hold values from -0.75 to 0.75
- layer_index_upscale: float32 [72, 50], replicated, may hold values from -0.875 to 0.875
Outputs:
- thermal_after_step: float32 [72, 8192], P(None, ('tile', 'crm'))
- vapour_after_step: float32 [72, 8192], P(None, ('tile', 'crm'))
- cloud_water: float32 [72, 8192], P(None, ('tile', 'crm'))
The draws below stay inside these ranges and needn't reach their ends.
Inputs may be any that keep to these rules, and one draw needn't show every extreme that they name: `processor_assignment`: the 256 columns of each device go exactly 8 to each owner device; owners are numbered in the order of tile, then crm.
All inputs are finite; a program needn't handle non-finite values.
Results may differ from the reference program's by a relative error of at most 0.0003.
Values sent between devices are 32-bit elements; how exact they have to be, the bound alone decides.
No kernel may reach another device: no remote copies, remote signals or barrier semaphores. Data moves between devices by JAX's collectives and lax.ppermute only.
A program may use at most 64 MiB of HBM per device.

```python
import jax
import jax.numpy as jnp
from jax import lax

VERTICAL_LAYERS = 72
CZ = 50
CX = 32
SUBSTEPS = 10
COL_DEV = 256
GRID_POINT_TOTAL = 8192


def draw_processor_assignment(key, part):
    devices = GRID_POINT_TOTAL // COL_DEV
    base = jnp.arange(COL_DEV, dtype=jnp.int32) % devices
    keys = jax.random.split(jax.random.fold_in(key, 7), devices)

    def shuffle_block(block_key):
        return jax.random.permutation(block_key, base)
    return jax.vmap(shuffle_block)(keys).reshape(GRID_POINT_TOTAL).astype(jnp.int32)


def draw_thermal_disturbance(key, part):
    full_shape = (CZ, CX, GRID_POINT_TOTAL)
    return jax.random.uniform(jax.random.fold_in(key, 17), full_shape, jnp.float32, -8.0, 8.0)


def shard_levels(stream_key, dims, cuts, smallest, top_value):
    def one(dim, parts):
        steps = jax.random.uniform(jax.random.fold_in(jax.random.fold_in(stream_key, 6), dim), (parts,), jnp.float32, smallest / len(cuts), top_value / len(cuts))
        return jnp.repeat(jnp.exp(steps), dims[dim] // parts).reshape((-1,) + (1,) * (len(dims) - dim - 1))

    gain = one(*cuts[0])
    for cut in cuts[1:]:
        gain = gain * one(*cut)
    return gain


def noise(rng, extent, spread, most, cuts=(), kind=jnp.bfloat16):
    entries = spread * jax.random.normal(rng, extent, jnp.float32)
    if cuts:
        entries = entries * shard_levels(rng, extent, cuts, -0.22, 0.18)
    return jnp.clip(entries, -most, most).astype(kind)


def setup_inputs(seed: int = 0) -> dict:
    seeds = jax.random.split(jax.random.key(seed), 8)
    return {
        "thermal_anomaly": noise(seeds[0], (VERTICAL_LAYERS, GRID_POINT_TOTAL), 1.0, 6.0, ((1, 32),), jnp.float32),
        "vapour_anomaly": noise(seeds[1], (VERTICAL_LAYERS, GRID_POINT_TOTAL), 1.0, 6.0, ((1, 32),), jnp.float32),
        "periodic_flow_velocity": jnp.clip(jax.random.uniform(seeds[2], (VERTICAL_LAYERS, GRID_POINT_TOTAL), jnp.float32, -0.8, 0.8) * shard_levels(seeds[2], (VERTICAL_LAYERS, GRID_POINT_TOTAL), ((1, 32),), -0.4, 0.0), -0.8, 0.8),
        "processor_assignment": draw_processor_assignment(jax.random.fold_in(seeds[7], 71), 0),
        "thermal_disturbance": draw_thermal_disturbance(jax.random.fold_in(seeds[7], 71), 0),
        "layer_index_downscale": noise(seeds[5], (CZ, VERTICAL_LAYERS), VERTICAL_LAYERS ** -0.5, 0.75, (), jnp.float32),
        "layer_index_upscale": noise(seeds[6], (VERTICAL_LAYERS, CZ), CZ ** -0.5, 0.875, (), jnp.float32),
    }


loop_diff = 0.35
mix_along = 0.35
mix_vertical = 0.1
cond_rate = 0.1
latent_heat = 1.5
max_speed = 0.8


def motion_rate_change(field_in, periodic_flow_velocity):
    ahead = jnp.roll(field_in, -1, axis=1)
    behind = jnp.roll(field_in, 1, axis=1)
    return -periodic_flow_velocity * (ahead - behind) * 0.5 + loop_diff * (ahead - 2.0 * field_in + behind)


def transport(field_in, advect_speed):
    eastward = jnp.roll(field_in, -1, axis=1)
    westward = jnp.roll(field_in, 1, axis=1)
    level_above = jnp.concatenate([field_in[1:], field_in[-1:]], axis=0)
    level_below = jnp.concatenate([field_in[:1], field_in[:-1]], axis=0)
    return (field_in - advect_speed * (eastward - westward) * 0.5
            + mix_along * (eastward - 2.0 * field_in + westward)
            + mix_vertical * (level_above - 2.0 * field_in + level_below))


def cloud_model(profiles, thermal_disturbance):
    temp_prof, water_prof, wind_prof, force_temp, force_water = profiles[0], profiles[1], profiles[2], profiles[3], profiles[4]
    advect_speed = (max_speed * jnp.tanh(wind_prof))[:, None, :]
    theta_state = temp_prof[:, None, :] + thermal_disturbance
    water_state = jnp.broadcast_to(water_prof[:, None, :], thermal_disturbance.shape).astype(jnp.float32)

    def substep(step_index, carry):
        theta_old, water_old = carry
        condense = cond_rate * jax.nn.softplus(water_old - 0.5 * theta_old)
        theta_new = transport(theta_old, advect_speed) + force_temp[:, None, :] / SUBSTEPS + latent_heat * condense
        water_new = transport(water_old, advect_speed) + force_water[:, None, :] / SUBSTEPS - condense
        return (theta_new, water_new)

    theta_state, water_state = lax.fori_loop(0, SUBSTEPS, substep, (theta_state, water_state))
    delta_temp = jnp.mean(theta_state, axis=1) - temp_prof
    delta_water = jnp.mean(water_state, axis=1) - water_prof
    cloud_mean = jnp.mean(jax.nn.softplus(water_state - 0.5 * theta_state), axis=1)
    return jnp.stack([delta_temp, delta_water, cloud_mean])


def reference(thermal_anomaly, vapour_anomaly, periodic_flow_velocity, processor_assignment, thermal_disturbance, layer_index_downscale, layer_index_upscale):
    carried_heat = motion_rate_change(thermal_anomaly, periodic_flow_velocity)
    carried_vapour = motion_rate_change(vapour_anomaly, periodic_flow_velocity)
    prognostic_variables = jnp.stack([thermal_anomaly, vapour_anomaly, periodic_flow_velocity, carried_heat, carried_vapour])
    devices = GRID_POINT_TOTAL // COL_DEV
    per_peer = COL_DEV // devices
    blocks = prognostic_variables.reshape(5, VERTICAL_LAYERS, devices, COL_DEV).transpose(2, 0, 1, 3)
    owners_all = processor_assignment.reshape(devices, COL_DEV)

    def one_home(inputs):
        home, block, owners = inputs
        onehot = (owners[:, None] == jnp.arange(devices, dtype=jnp.int32)[None, :]).astype(jnp.int32)
        rank_here = jnp.sum((jnp.cumsum(onehot, axis=0).astype(jnp.int32) - 1) * onehot, axis=1).astype(jnp.int32)
        slots = (owners * COL_DEV + home * per_peer + rank_here).astype(jnp.int32)
        local_noise = jnp.take(thermal_disturbance, slots, axis=2)
        profiles = jnp.einsum('zl,flc->fzc', layer_index_downscale, block, precision=lax.Precision.HIGHEST)
        result = cloud_model(profiles, local_noise)
        return jnp.einsum('lz,fzc->flc', layer_index_upscale, result, precision=lax.Precision.HIGHEST)

    resolved_results = lax.map(one_home, (jnp.arange(devices, dtype=jnp.int32), blocks, owners_all))
    resolved_results = resolved_results.transpose(1, 2, 0, 3).reshape(3, VERTICAL_LAYERS, GRID_POINT_TOTAL)
    thermal_after_step = thermal_anomaly + carried_heat + resolved_results[0]
    vapour_after_step = vapour_anomaly + carried_vapour + resolved_results[1]
    return thermal_after_step, vapour_after_step, resolved_results[2]
```

```python
import functools

import numpy as np

import jax
import jax.numpy as jnp
from jax import lax
from jax.experimental import pallas as pl
from jax.experimental.pallas import tpu as pltpu
from jax.sharding import PartitionSpec as P

SUBSTEPS = 10

loop_diff = 0.35
mix_along = 0.35
mix_vertical = 0.1
cond_rate = 0.1
latent_heat = 1.5
max_speed = 0.8

AXES = ("tile", "crm")
LOG2E = 1.4426950408889634
LN2 = 0.6931471805599453
SUB = 8
LANE = 128
HI = lax.Precision.HIGHEST
VMEM = pl.BlockSpec(memory_space=pltpu.VMEM)


def up_to(n, m):
    return -(-n // m) * m


def edges(block):
    count = lax.axis_size(AXES)
    forward = [(i, (i + 1) % count) for i in range(count)]
    backward = [(t, s) for s, t in forward]
    low = lax.ppermute(block[:, :, -1:], AXES, forward)
    high = lax.ppermute(block[:, :, :1], AXES, backward)
    return low, high


def ring_mean_operator(levels):
    f = np.eye(levels)
    east = west = f
    above = np.concatenate([f[1:], f[-1:]], axis=0)
    below = np.concatenate([f[:1], f[:-1]], axis=0)
    return (
        f
        + mix_along * (east - 2.0 * f + west)
        + mix_vertical * (above - 2.0 * f + below)
    )


def mean_operators(levels):
    v = ring_mean_operator(levels)
    power = np.eye(levels)
    total = np.zeros((levels, levels))
    for _ in range(SUBSTEPS):
        total = total + power
        power = v @ power
    return power, total / SUBSTEPS


def split3(x):
    a = x.astype(jnp.bfloat16)
    r = x - a.astype(jnp.float32)
    b = r.astype(jnp.bfloat16)
    c = (r - b.astype(jnp.float32)).astype(jnp.bfloat16)
    return a, b, c


def dot(a, b, ca, cb, precision=None):
    return lax.dot_general(
        a, b, (((ca,), (cb,)), ((), ())), precision=precision, preferred_element_type=jnp.float32
    )


def advection(f, v, low, high):
    cols = f.shape[1]
    lane = lax.broadcasted_iota(jnp.int32, f.shape, 1)
    ahead = jnp.where(lane == cols - 1, high, pltpu.roll(f, cols - 1, 1))
    behind = jnp.where(lane == 0, low, pltpu.roll(f, 1, 1))
    return -v * (ahead - behind) * 0.5 + loop_diff * (ahead - 2.0 * f + behind)


def onehot(pos_row, cols):
    place = lax.broadcasted_iota(jnp.int32, (cols, cols), 0)
    return jnp.where(place == pos_row, 1.0, 0.0).astype(jnp.bfloat16)


def pack_kernel(devices, t_ref, q_ref, v_ref, own_ref, low_ref, high_ref,
                out_ref, pos_ref, advt_ref, advq_ref, s_ref):
    nl, cols = t_ref.shape
    own = own_ref[...]
    who = lax.broadcasted_iota(jnp.int32, (devices, cols), 0)
    mine = jnp.where(who == own, 1.0, 0.0)
    before = lax.broadcasted_iota(jnp.int32, (cols, cols), 0) < lax.broadcasted_iota(
        jnp.int32, (cols, cols), 1
    )
    tri = jnp.where(before, 1.0, 0.0).astype(jnp.bfloat16)
    ranks = dot(mine.astype(jnp.bfloat16), tri, 1, 0)
    rank = jnp.sum(ranks * mine, axis=0, keepdims=True)
    pos = own * (cols // devices) + rank.astype(jnp.int32)
    pos_ref[...] = pos
    sel = onehot(pos, cols)

    t = t_ref[...]
    q = q_ref[...]
    v = v_ref[...]
    advt = advection(t, v, low_ref[0], high_ref[0])
    advq = advection(q, v, low_ref[1], high_ref[1])
    advt_ref[...] = advt
    advq_ref[...] = advq
    s_ref[0:nl, :] = q - 0.5 * t
    s_ref[nl:2 * nl, :] = v
    s_ref[2 * nl:3 * nl, :] = advq - 0.5 * advt
    rest = s_ref.shape[0] - 3 * nl
    if rest:
        s_ref[3 * nl:, :] = jnp.zeros((rest, cols), jnp.float32)
    a, b, c = split3(s_ref[...])
    out_ref[...] = dot(sel, a, 1, 1) + dot(sel, b, 1, 1) + dot(sel, c, 1, 1)


def softplus2(f):
    return jnp.maximum(f, jnp.log2(1.0 + jnp.exp2(jnp.minimum(f, 100.0))))


def cloud_kernel(zp, r_ref, td_ref, down_ref, mean_ref, out_ref,
                 d_ref, raw_ref, east_ref, west_ref, force_ref, val_ref):
    cz, cx, cols = td_ref.shape
    nl = down_ref.shape[1]
    width = r_ref.shape[1]
    groups = cx // SUB
    tiles = cols // LANE

    down = jnp.concatenate(
        [down_ref[...], jnp.zeros((cz, width - nl), jnp.float32)], axis=1
    )
    down = jnp.concatenate([down, jnp.zeros((zp - cz, width), jnp.float32)], axis=0)
    g = jnp.concatenate(
        [down, pltpu.roll(down, nl, 1), pltpu.roll(down, 2 * nl, 1)], axis=0
    )
    prof = dot(g, r_ref[...], 1, 1, HI)
    d0 = prof[0:zp]
    speed = max_speed * jnp.tanh(prof[zp:2 * zp])
    fd = prof[2 * zp:3 * zp]
    east_ref[...] = mix_along - 0.5 * speed
    west_ref[...] = mix_along + 0.5 * speed
    force_ref[...] = fd * (LOG2E / SUBSTEPS)
    val_ref[zp:2 * zp, :] = d0
    val_ref[2 * zp:3 * zp, :] = fd

    def lanes(k):
        return pl.ds(k * LANE, LANE)

    def row(ref, z, k):
        return jnp.broadcast_to(ref[pl.ds(z, 1), lanes(k)], (SUB, LANE))

    val_ref[0:zp, :] = jnp.zeros((zp, cols), jnp.float32)
    val_ref[3 * zp:, :] = jnp.zeros((val_ref.shape[0] - 3 * zp, cols), jnp.float32)

    for k in range(tiles):
        for z in range(cz):
            base = row(val_ref, zp + z, k) * LOG2E
            total = None
            raw = raw_ref.at[k * cz + z]
            raw[...] = td_ref[z, :, lanes(k)]
            for i in range(groups):
                td = raw[pl.ds(i, SUB, stride=groups), :]
                total = td if total is None else total + td
                d_ref[k, z, i] = base - (0.5 * LOG2E) * td
            val_ref[pl.ds(z, 1), lanes(k)] = jnp.sum(total, axis=0, keepdims=True) * (1.0 / cx)
    val_ref[zp:2 * zp, :] = d0 - 0.5 * val_ref[0:zp, :]

    drain = cond_rate * (1.0 + 0.5 * latent_heat)
    keep = 1.0 - 2.0 * mix_along - 2.0 * mix_vertical

    def step(_, carry):
        for k in range(tiles):
            prev = cur = [d_ref[k, 0, i] for i in range(groups)]
            for z in range(cz):
                nxt = [d_ref[k, z + 1, i] for i in range(groups)] if z + 1 < cz else cur
                ea = row(east_ref, z, k)
                we = row(west_ref, z, k)
                fo = row(force_ref, z, k)
                for i in range(groups):
                    f = cur[i]
                    east = cur[i + 1] if i + 1 < groups else pltpu.roll(cur[0], SUB - 1, 0)
                    west = cur[i - 1] if i else pltpu.roll(cur[-1], 1, 0)
                    new = (
                        keep * f
                        + mix_vertical * (prev[i] + nxt[i])
                        + ea * east
                        + we * west
                        + fo
                        - drain * softplus2(f)
                    )
                    d_ref[k, z, i] = new
                prev, cur = cur, nxt
        return carry

    lax.fori_loop(0, SUBSTEPS, step, 0)

    for k in range(tiles):
        for z in range(cz):
            total = cloud = None
            for i in range(groups):
                f = d_ref[k, z, i]
                c = softplus2(f)
                total = f if total is None else total + f
                cloud = c if cloud is None else cloud + c
            val_ref[pl.ds(3 * zp + z, 1), lanes(k)] = jnp.sum(
                total, axis=0, keepdims=True
            ) * (LN2 / cx)
            val_ref[pl.ds(4 * zp + z, 1), lanes(k)] = jnp.sum(
                cloud, axis=0, keepdims=True
            ) * (LN2 / cx)
    out_ref[...] = dot(val_ref[...], mean_ref[...], 0, 0, HI)


def finish_kernel(zp, r_ref, pos_ref, t_ref, q_ref, advt_ref, advq_ref, down_ref, up_ref,
                  lin_ref, to_ref, qo_ref, co_ref):
    nl, cols = t_ref.shape
    cz = down_ref.shape[0]
    width = r_ref.shape[1]
    down = down_ref[...]
    up = up_ref[...]
    tc = dot(down, t_ref[...], 1, 0, HI)
    qc = dot(down, q_ref[...], 1, 0, HI)
    ft = dot(down, advt_ref[...], 1, 0, HI)
    fq = dot(down, advq_ref[...], 1, 0, HI)
    lin = lin_ref[...]
    ls = dot(lin[0], tc, 1, 0, HI) + dot(lin[1], ft, 1, 0, HI)
    lq = dot(lin[0], qc, 1, 0, HI) + dot(lin[1], fq, 1, 0, HI)
    sel = onehot(pos_ref[...], cols)
    a, b, c = split3(r_ref[...])
    u = dot(a, sel, 0, 0) + dot(b, sel, 0, 0) + dot(c, sel, 0, 0)
    heat = dot(up, ls + u[0:cz], 1, 0, HI)
    moist = dot(up, lq - u[zp:zp + cz], 1, 0, HI)
    to_ref[...] = t_ref[...] + advt_ref[...] + heat
    qo_ref[...] = q_ref[...] + advq_ref[...] + moist
    co_ref[...] = dot(up, u[2 * zp:2 * zp + cz], 1, 0, HI)


def local(
    thermal_anomaly,
    vapour_anomaly,
    periodic_flow_velocity,
    processor_assignment,
    thermal_disturbance,
    layer_index_downscale,
    layer_index_upscale,
):
    nl, cols = thermal_anomaly.shape
    cz, cx, _ = thermal_disturbance.shape
    devices = lax.axis_size(AXES)
    per = cols // devices
    zp = up_to(cz, SUB)
    f32 = jnp.float32
    width = up_to(3 * nl, LANE)
    back = up_to(3 * zp, LANE)

    low, high = edges(jnp.stack([thermal_anomaly, vapour_anomaly]))
    field = jax.ShapeDtypeStruct((nl, cols), f32)
    out, pos, advt, advq = pl.pallas_call(
        functools.partial(pack_kernel, devices),
        out_shape=(
            jax.ShapeDtypeStruct((cols, width), f32),
            jax.ShapeDtypeStruct((1, cols), jnp.int32),
            field,
            field,
        ),
        in_specs=[VMEM] * 6,
        out_specs=(VMEM,) * 4,
        scratch_shapes=[pltpu.VMEM((width, cols), f32)],
        name="pack",
    )(
        thermal_anomaly,
        vapour_anomaly,
        periodic_flow_velocity,
        processor_assignment.reshape(1, cols),
        low,
        high,
    )
    r1 = lax.all_to_all(
        out.reshape(devices, per, width), AXES, split_axis=0, concat_axis=0, tiled=True
    ).reshape(cols, width)

    power, total = mean_operators(cz)
    release = cond_rate * (1.0 + 0.5 * latent_heat) / cond_rate
    mean = np.zeros((5 * zp, back))
    z_part = np.zeros((5 * zp, cz))
    z_part[zp:zp + cz] = power.T / release
    z_part[2 * zp:2 * zp + cz] = total.T / release
    z_part[3 * zp:3 * zp + cz] = -np.eye(cz) / release
    mean[0:cz, 0:cz] = power.T
    mean[:, 0:cz] += latent_heat * z_part
    mean[:, zp:zp + cz] = z_part
    mean[4 * zp:4 * zp + cz, 2 * zp:2 * zp + cz] = np.eye(cz)

    tiles = cols // LANE
    vals = pl.pallas_call(
        functools.partial(cloud_kernel, zp),
        out_shape=jax.ShapeDtypeStruct((cols, back), f32),
        in_specs=[VMEM] * 4,
        out_specs=VMEM,
        scratch_shapes=[
            pltpu.VMEM((tiles, cz, cx // SUB, SUB, LANE), f32),
            pltpu.VMEM((tiles * cz, cx, LANE), f32),
            pltpu.VMEM((zp, cols), f32),
            pltpu.VMEM((zp, cols), f32),
            pltpu.VMEM((zp, cols), f32),
            pltpu.VMEM((5 * zp, cols), f32),
        ],
        name="cloud",
    )(r1, thermal_disturbance, layer_index_downscale, jnp.asarray(mean, f32))
    r2 = lax.all_to_all(
        vals.reshape(devices, per, back), AXES, split_axis=0, concat_axis=0, tiled=True
    ).reshape(cols, back)

    lin = np.stack([power - np.eye(cz), total])
    return pl.pallas_call(
        functools.partial(finish_kernel, zp),
        out_shape=(field,) * 3,
        in_specs=[VMEM] * 9,
        out_specs=(VMEM,) * 3,
        name="finish",
    )(
        r2,
        pos,
        thermal_anomaly,
        vapour_anomaly,
        advt,
        advq,
        layer_index_downscale,
        layer_index_upscale,
        jnp.asarray(lin, f32),
    )


def solution(mesh):
    in_specs = (
        P(None, AXES),
        P(None, AXES),
        P(None, AXES),
        P(AXES),
        P(None, None, AXES),
        P(),
        P(),
    )
    out_specs = (P(None, AXES), P(None, AXES), P(None, AXES))
    return jax.shard_map(local, mesh=mesh, in_specs=in_specs, out_specs=out_specs, check_vma=False)
```

```python
import functools

import numpy as np

import jax
import jax.numpy as jnp
from jax import lax
from jax.experimental import pallas as pl
from jax.experimental.pallas import tpu as pltpu
from jax.sharding import PartitionSpec as P

SUBSTEPS = 10

loop_diff = 0.35
mix_along = 0.35
mix_vertical = 0.1
cond_rate = 0.1
latent_heat = 1.5
max_speed = 0.8

AXES = ("tile", "crm")
LOG2E = 1.4426950408889634
LN2 = 0.6931471805599453
SUB = 8
LANE = 128
HI = lax.Precision.HIGH
VMEM = pl.BlockSpec(memory_space=pltpu.VMEM)
ANY = pl.BlockSpec(memory_space=pl.ANY)


def up_to(n, m):
    return -(-n // m) * m


def edges(block):
    count = lax.axis_size(AXES)
    forward = [(i, (i + 1) % count) for i in range(count)]
    backward = [(t, s) for s, t in forward]
    low = lax.ppermute(block[:, :, -1:], AXES, forward)
    high = lax.ppermute(block[:, :, :1], AXES, backward)
    return low, high


def ring_mean_operator(levels):
    f = np.eye(levels)
    east = west = f
    above = np.concatenate([f[1:], f[-1:]], axis=0)
    below = np.concatenate([f[:1], f[:-1]], axis=0)
    return (
        f
        + mix_along * (east - 2.0 * f + west)
        + mix_vertical * (above - 2.0 * f + below)
    )


def mean_operators(levels):
    v = ring_mean_operator(levels)
    power = np.eye(levels)
    total = np.zeros((levels, levels))
    for _ in range(SUBSTEPS):
        total = total + power
        power = v @ power
    return power, total / SUBSTEPS


def split(x):
    a = x.astype(jnp.bfloat16)
    return a, (x - a.astype(jnp.float32)).astype(jnp.bfloat16)


def dot(a, b, ca, cb, precision=None):
    return lax.dot_general(
        a, b, (((ca,), (cb,)), ((), ())), precision=precision, preferred_element_type=jnp.float32
    )


def advection(f, v, low, high):
    cols = f.shape[1]
    lane = lax.broadcasted_iota(jnp.int32, f.shape, 1)
    ahead = jnp.where(lane == cols - 1, high, pltpu.roll(f, cols - 1, 1))
    behind = jnp.where(lane == 0, low, pltpu.roll(f, 1, 1))
    return -v * (ahead - behind) * 0.5 + loop_diff * (ahead - 2.0 * f + behind)


def onehot(pos_row, cols):
    place = lax.broadcasted_iota(jnp.int32, (cols, cols), 0)
    return jnp.where(place == pos_row, 1.0, 0.0).astype(jnp.bfloat16)


CARRIED = (
    (0, 1, 0), (0, 0, 0), (0, 0, 1), (0, 1, 1),
    (1, 0, 0), (1, 1, 0), (1, 0, 1), (1, 1, 1),
)


def row_of(field, half, end):
    return CARRIED.index((field, half, end))


def halves(levels):
    first = up_to(-(-levels // 2), SUB)
    return first, levels - first


def carries(levels, per, width):
    first, second = halves(levels)
    return per >= len(CARRIED) and 3 * levels + first <= width and second < first


def pack_kernel(devices, carry, *refs):
    t_ref, q_ref, v_ref, own_ref = refs[:4]
    low_ref, high_ref = (None, None) if carry else refs[4:6]
    out_ref, pos_ref, s_ref = refs[-3:]
    nl, cols = t_ref.shape
    width = s_ref.shape[0]
    per = cols // devices
    own = own_ref[...]
    who = lax.broadcasted_iota(jnp.int32, (devices, cols), 0)
    mine = jnp.where(who == own, 1.0, 0.0)
    before = lax.broadcasted_iota(jnp.int32, (cols, cols), 0) < lax.broadcasted_iota(
        jnp.int32, (cols, cols), 1
    )
    tri = jnp.where(before, 1.0, 0.0).astype(jnp.bfloat16)
    ranks = dot(mine.astype(jnp.bfloat16), tri, 1, 0)
    rank = jnp.sum(ranks * mine, axis=0, keepdims=True)
    pos = own * per + rank.astype(jnp.int32)
    pos_ref[...] = pos
    sel = onehot(pos, cols)

    t = t_ref[...]
    x = q_ref[...] - 0.5 * t
    v = v_ref[...]
    if carry:
        low = high = jnp.zeros((nl, 1), jnp.float32)
    else:
        low = low_ref[1] - 0.5 * low_ref[0]
        high = high_ref[1] - 0.5 * high_ref[0]
    s_ref[0:nl, :] = x
    s_ref[nl:2 * nl, :] = v
    s_ref[2 * nl:3 * nl, :] = advection(x, v, low, high)
    rest = width - 3 * nl
    if rest:
        s_ref[3 * nl:, :] = jnp.zeros((rest, cols), jnp.float32)
    if carry:
        first, second = halves(nl)
        lane = lax.broadcasted_iota(jnp.int32, (1, cols), 1)
        s_ref[3 * nl + second:3 * nl + second + 1, :] = jnp.where(
            (lane == 0) | (lane == cols - 1), 1.0, 0.0
        )
    a, b = split(s_ref[...])
    out = dot(sel, a, 1, 1) + dot(sel, b, 1, 1)
    if carry:
        fill = jnp.zeros((first - second, cols), jnp.float32)
        parts = []
        for f in (x, t):
            parts += [f[:first], jnp.concatenate([f[first:], fill], axis=0)]
        parts = jnp.concatenate(parts, axis=1)
        shape = (SUB, parts.shape[1])
        want = jnp.full(shape, -1, jnp.int32)
        row = lax.broadcasted_iota(jnp.int32, shape, 0)
        for r, (field, half, end) in enumerate(CARRIED):
            want = jnp.where(row == r, (2 * field + half) * cols + end * (cols - 1), want)
        pick = jnp.where(lax.broadcasted_iota(jnp.int32, shape, 1) == want, 1.0, 0.0).astype(
            jnp.bfloat16
        )
        a, b = split(parts)
        ends = dot(pick, a, 1, 1) + dot(pick, b, 1, 1)
        ends = jnp.concatenate([ends, jnp.zeros((SUB, width - first), jnp.float32)], axis=1)
        ends = pltpu.roll(ends, 3 * nl, 1)
        out = (out.reshape(devices, per, width) + ends[None]).reshape(cols, width)
    out_ref[...] = out


def softplus2(f):
    return jnp.maximum(f, jnp.log2(1.0 + jnp.exp2(jnp.minimum(f, 100.0))))


def cloud_kernel(devices, carry, r_ref, td_ref, down_ref, mean_ref, out_ref,
                 d_ref, raw_ref, east_ref, west_ref, force_ref, val_ref, part_ref, mean_buf,
                 td_sem, mean_sem):
    cz, cx, cols = td_ref.shape
    nl = down_ref.shape[1]
    zp = east_ref.shape[0]
    width = r_ref.shape[1]
    per = cols // devices
    groups = cx // SUB
    tiles = cols // LANE
    chunk = -(-cz // td_sem.shape[1])

    def lanes(k):
        return pl.ds(k * LANE, LANE)

    def td_copy(k, c):
        levels = pl.ds(c * chunk, min(chunk, cz - c * chunk))
        return pltpu.make_async_copy(
            td_ref.at[levels, :, lanes(k)], raw_ref.at[k, levels], td_sem.at[k, c]
        )

    for k in range(tiles):
        for c in range(td_sem.shape[1]):
            td_copy(k, c).start()
    mean_copy = pltpu.make_async_copy(mean_ref, mean_buf, mean_sem)
    mean_copy.start()

    down = jnp.concatenate(
        [down_ref[...], jnp.zeros((cz, width - nl), jnp.float32)], axis=1
    )
    down = jnp.concatenate([down, jnp.zeros((zp - cz, width), jnp.float32)], axis=0)
    g = [down, pltpu.roll(down, nl, 1), pltpu.roll(down, 2 * nl, 1)]
    if carry:
        first, second = halves(nl)
        shape = (nl + first, width)
        row = lax.broadcasted_iota(jnp.int32, shape, 0)
        to = jnp.where(row < nl, row + nl, row + 2 * nl)
        g.append(jnp.where(lax.broadcasted_iota(jnp.int32, shape, 1) == to, 1.0, 0.0))
    prof = dot(jnp.concatenate(g, axis=0), r_ref[...], 1, 1, HI)
    d0 = prof[0:zp]
    speed = max_speed * jnp.tanh(prof[zp:2 * zp])
    fd = prof[2 * zp:3 * zp]
    if carry:
        v = prof[3 * zp:3 * zp + nl]
        ends = prof[3 * zp + nl:3 * zp + nl + first]
        flag = ends[second:second + 1] > 0.5
        place = lax.rem(lax.broadcasted_iota(jnp.int32, (1, cols), 1), per)

        def neighbour(end, at):
            step = per if at == 0 else -per
            shift = lambda half: (step + at - row_of(0, half, end)) % cols
            return jnp.concatenate(
                [pltpu.roll(ends, shift(0), 1), pltpu.roll(ends, shift(1), 1)[:second]], axis=0
            )

        behind = neighbour(1, 0) * (loop_diff + 0.5 * v)
        ahead = neighbour(0, per - 1) * (loop_diff - 0.5 * v)
        halo = jnp.where(flag & (place == 0), behind, 0.0) + jnp.where(
            flag & (place == per - 1), ahead, 0.0
        )
        fd = fd + dot(down[:, :nl], halo, 1, 0, HI)
    east_ref[...] = mix_along - 0.5 * speed
    west_ref[...] = mix_along + 0.5 * speed
    force_ref[...] = fd * (LOG2E / SUBSTEPS)
    val_ref[zp:2 * zp, :] = d0
    val_ref[2 * zp:3 * zp, :] = fd

    def row_at(ref, z, k):
        return jnp.broadcast_to(ref[pl.ds(z, 1), lanes(k)], (SUB, LANE))

    zeros = jnp.zeros((SUB, LANE), jnp.float32)
    for n in range(part_ref.shape[0]):
        for z in range(cz, zp):
            part_ref[n, pl.ds(z * SUB, SUB), :] = zeros

    def fold(n, k, base, scale):
        total = part_ref[n, pl.ds(0, zp, stride=SUB), :]
        for s in range(1, SUB):
            total = total + part_ref[n, pl.ds(s, zp, stride=SUB), :]
        val_ref[pl.ds(base, zp), lanes(k)] = total * scale

    slot = [0] + [SUB * (i + 1) for i in range(1, groups)]
    last = slot[-1]

    def put(k, z, i, new):
        d_ref[k, z, pl.ds(slot[i], SUB), :] = new
        if i == 0:
            d_ref[k, z, pl.ds(SUB, SUB), :] = new
        if i == groups - 1:
            d_ref[k, z, pl.ds(last + SUB, SUB), :] = new

    for k in range(tiles):
        for z in range(cz):
            if z % chunk == 0:
                td_copy(k, z // chunk).wait()
            base = row_at(val_ref, zp + z, k) * LOG2E
            total = None
            for i in range(groups):
                td = raw_ref[k, z, pl.ds(i, SUB, stride=groups), :]
                total = td if total is None else total + td
                put(k, z, i, base - (0.5 * LOG2E) * td)
            part_ref[k, pl.ds(z * SUB, SUB), :] = total
        fold(k, k, 0, 1.0 / cx)

    drain = cond_rate * (1.0 + 0.5 * latent_heat)

    def step(_, carry):
        for k in range(tiles):
            prev = cur = [d_ref[k, 0, pl.ds(slot[i], SUB), :] for i in range(groups)]
            for z in range(cz):
                nxt = cur
                if z + 1 < cz:
                    nxt = [d_ref[k, z + 1, pl.ds(slot[i], SUB), :] for i in range(groups)]
                ea = row_at(east_ref, z, k)
                we = row_at(west_ref, z, k)
                fo = row_at(force_ref, z, k)
                ring = [d_ref[k, z, pl.ds(last + SUB - 1, SUB), :]] + cur
                ring = ring + [d_ref[k, z, pl.ds(1, SUB), :]]
                for i in range(groups):
                    f = cur[i]
                    new = (
                        mix_vertical * ((prev[i] + f) + nxt[i])
                        + ea * ring[i + 2]
                        + we * ring[i]
                        + fo
                        - drain * softplus2(f)
                    )
                    put(k, z, i, new)
                prev, cur = cur, nxt
        return carry

    lax.fori_loop(0, SUBSTEPS, step, 0)

    for k in range(tiles):
        for z in range(cz):
            total = cloud = None
            for i in range(groups):
                f = d_ref[k, z, pl.ds(slot[i], SUB), :]
                c = softplus2(f)
                total = f if total is None else total + f
                cloud = c if cloud is None else cloud + c
            part_ref[2 * k, pl.ds(z * SUB, SUB), :] = total
            part_ref[2 * k + 1, pl.ds(z * SUB, SUB), :] = cloud
        fold(2 * k, k, 3 * zp, LN2 / cx)
        fold(2 * k + 1, k, 4 * zp, LN2 / cx)
    val_ref[zp:2 * zp, :] = val_ref[zp:2 * zp, :] - 0.5 * val_ref[0:zp, :]
    mean_copy.wait()
    out_ref[...] = dot(val_ref[...], mean_buf[...], 0, 0, HI)


def base_kernel(devices, carry, *refs):
    t_ref, q_ref, v_ref, down_ref, up_ref, lin_ref, after_ref, r_ref = refs[:8]
    high_ref = None if carry else refs[8]
    to_ref, qo_ref = refs[-2:]
    del after_ref
    nl, cols = t_ref.shape
    per = cols // devices
    if carry:
        first, second = halves(nl)
        me = lax.axis_index(AXES)

        def ends(device, end):
            start = pl.multiple_of(device * per, SUB)
            block = r_ref[pl.ds(start, SUB), :]
            block = pltpu.roll(block, block.shape[1] - 3 * nl, 1)[:, :LANE].T
            x, t = [
                jnp.concatenate(
                    [
                        block[:first, row_of(field, 0, end):row_of(field, 0, end) + 1],
                        block[:second, row_of(field, 1, end):row_of(field, 1, end) + 1],
                    ],
                    axis=0,
                )
                for field in (0, 1)
            ]
            return t, x + 0.5 * t

        low = ends(lax.rem(me + devices - 1, devices), 1)
        high = ends(lax.rem(me + 1, devices), 0)
    else:
        low = (r_ref[0], r_ref[1])
        high = (high_ref[0], high_ref[1])
    v = v_ref[...]
    t = t_ref[...]
    q = q_ref[...]
    advt = advection(t, v, low[0], high[0])
    advq = advection(q, v, low[1], high[1])
    prof = dot(down_ref[...], jnp.concatenate([t, q, advt, advq], axis=1), 1, 0, HI)
    lin = lin_ref[...]
    gain = dot(lin[0], prof[:, :2 * cols], 1, 0, HI) + dot(lin[1], prof[:, 2 * cols:], 1, 0, HI)
    gain = dot(up_ref[...], gain, 1, 0, HI)
    to_ref[...] = t + advt + gain[:, :cols]
    qo_ref[...] = q + advq + gain[:, cols:]


def finish_kernel(zp, r_ref, pos_ref, up_ref, tb_ref, qb_ref, to_ref, qo_ref, co_ref):
    nl, cols = tb_ref.shape
    cz = up_ref.shape[1]
    width = r_ref.shape[1]
    up = jnp.concatenate([up_ref[...], jnp.zeros((nl, width - cz), jnp.float32)], axis=1)
    up = jnp.concatenate([up, -pltpu.roll(up, zp, 1), pltpu.roll(up, 2 * zp, 1)], axis=0)
    sel = onehot(pos_ref[...], cols)
    a, b = split(dot(up, r_ref[...], 1, 1, HI))
    out = dot(a, sel, 1, 0) + dot(b, sel, 1, 0)
    to_ref[...] = tb_ref[...] + out[0:nl]
    qo_ref[...] = qb_ref[...] + out[nl:2 * nl]
    co_ref[...] = out[2 * nl:3 * nl]


def local(
    thermal_anomaly,
    vapour_anomaly,
    periodic_flow_velocity,
    processor_assignment,
    thermal_disturbance,
    layer_index_downscale,
    layer_index_upscale,
):
    nl, cols = thermal_anomaly.shape
    cz, cx, _ = thermal_disturbance.shape
    devices = lax.axis_size(AXES)
    per = cols // devices
    zp = up_to(cz, SUB)
    f32 = jnp.float32
    width = up_to(3 * nl, LANE)
    back = up_to(3 * zp, LANE)
    field = jax.ShapeDtypeStruct((nl, cols), f32)
    carry = carries(nl, per, width)

    fields = (thermal_anomaly, vapour_anomaly, periodic_flow_velocity)
    ends = () if carry else edges(jnp.stack(fields[:2]))
    out, pos = pl.pallas_call(
        functools.partial(pack_kernel, devices, carry),
        out_shape=(
            jax.ShapeDtypeStruct((cols, width), f32),
            jax.ShapeDtypeStruct((1, cols), jnp.int32),
        ),
        in_specs=[VMEM] * (4 + len(ends)),
        out_specs=(VMEM,) * 2,
        scratch_shapes=[pltpu.VMEM((width, cols), f32)],
        compiler_params=pltpu.CompilerParams(vmem_limit_bytes=VMEM_PACK),
        name="pack",
    )(*fields, processor_assignment.reshape(1, cols), *ends)

    def exchange(blocks):
        shape = blocks.shape
        blocks = blocks.reshape(devices, per, shape[1])
        return lax.all_to_all(blocks, AXES, split_axis=0, concat_axis=0, tiled=True).reshape(shape)

    r1 = exchange(out)

    power, total = mean_operators(cz)
    release = 1.0 + 0.5 * latent_heat
    mean = np.zeros((5 * zp, back))
    z_part = np.zeros((5 * zp, cz))
    z_part[zp:zp + cz] = power.T / release
    z_part[2 * zp:2 * zp + cz] = total.T / release
    z_part[3 * zp:3 * zp + cz] = -np.eye(cz) / release
    mean[0:cz, 0:cz] = power.T
    mean[:, 0:cz] += latent_heat * z_part
    mean[:, zp:zp + cz] = z_part
    mean[4 * zp:4 * zp + cz, 2 * zp:2 * zp + cz] = np.eye(cz)

    tiles = cols // LANE
    groups = cx // SUB
    vals = pl.pallas_call(
        functools.partial(cloud_kernel, devices, carry),
        out_shape=jax.ShapeDtypeStruct((cols, back), f32),
        in_specs=[VMEM, ANY, VMEM, ANY],
        out_specs=VMEM,
        scratch_shapes=[
            pltpu.VMEM((tiles, cz, SUB * (groups + 2), LANE), f32),
            pltpu.VMEM((tiles, cz, cx, LANE), f32),
            pltpu.VMEM((zp, cols), f32),
            pltpu.VMEM((zp, cols), f32),
            pltpu.VMEM((zp, cols), f32),
            pltpu.VMEM((5 * zp, cols), f32),
            pltpu.VMEM((2 * tiles, zp * SUB, LANE), f32),
            pltpu.VMEM((5 * zp, back), f32),
            pltpu.SemaphoreType.DMA((tiles, 5)),
            pltpu.SemaphoreType.DMA,
        ],
        compiler_params=pltpu.CompilerParams(vmem_limit_bytes=VMEM_CLOUD),
        name="cloud",
    )(r1, thermal_disturbance, layer_index_downscale, jnp.asarray(mean, f32))
    r2 = exchange(vals)

    lin = np.stack([power - np.eye(cz), total])
    halo = (r1,) if carry else ends
    base = pl.pallas_call(
        functools.partial(base_kernel, devices, carry),
        out_shape=(field,) * 2,
        in_specs=[VMEM] * 6 + [ANY] + [VMEM] * len(halo),
        out_specs=(VMEM,) * 2,
        compiler_params=pltpu.CompilerParams(vmem_limit_bytes=VMEM_PACK),
        cost_estimate=pl.CostEstimate(flops=10**8, bytes_accessed=10**6, transcendentals=0),
        name="base",
    )(*fields, layer_index_downscale, layer_index_upscale, jnp.asarray(lin, f32), vals, *halo)
    return pl.pallas_call(
        functools.partial(finish_kernel, zp),
        out_shape=(field,) * 3,
        in_specs=[VMEM] * 5,
        out_specs=(VMEM,) * 3,
        compiler_params=pltpu.CompilerParams(vmem_limit_bytes=VMEM_PACK),
        name="finish",
    )(r2, pos, layer_index_upscale, *base)


VMEM_PACK = 16 * 2**20
VMEM_CLOUD = 24 * 2**20


def solution(mesh):
    in_specs = (
        P(None, AXES),
        P(None, AXES),
        P(None, AXES),
        P(AXES),
        P(None, None, AXES),
        P(),
        P(),
    )
    out_specs = (P(None, AXES), P(None, AXES), P(None, AXES))
    return jax.shard_map(local, mesh=mesh, in_specs=in_specs, out_specs=out_specs, check_vma=False)
```

```python
import functools

import numpy as np

import jax
import jax.numpy as jnp
from jax import lax
from jax.experimental import pallas as pl
from jax.experimental.pallas import tpu as pltpu
from jax.sharding import PartitionSpec as P

SUBSTEPS = 10

loop_diff = 0.35
mix_along = 0.35
mix_vertical = 0.1
cond_rate = 0.1
latent_heat = 1.5
max_speed = 0.8

AXES = ("tile", "crm")
LOG2E = 1.4426950408889634
LN2 = 0.6931471805599453
SUB = 8
LANE = 128
HI = lax.Precision.HIGH
VMEM = pl.BlockSpec(memory_space=pltpu.VMEM)
ANY = pl.BlockSpec(memory_space=pl.ANY)
HBM = pl.BlockSpec(memory_space=pltpu.HBM)


def up_to(n, m):
    return -(-n // m) * m


def edges(block):
    count = lax.axis_size(AXES)
    forward = [(i, (i + 1) % count) for i in range(count)]
    backward = [(t, s) for s, t in forward]
    low = lax.ppermute(block[:, :, -1:], AXES, forward)
    high = lax.ppermute(block[:, :, :1], AXES, backward)
    return low, high


def ring_mean_operator(levels):
    f = np.eye(levels)
    east = west = f
    above = np.concatenate([f[1:], f[-1:]], axis=0)
    below = np.concatenate([f[:1], f[:-1]], axis=0)
    return (
        f
        + mix_along * (east - 2.0 * f + west)
        + mix_vertical * (above - 2.0 * f + below)
    )


def mean_operators(levels):
    v = ring_mean_operator(levels)
    power = np.eye(levels)
    total = np.zeros((levels, levels))
    for _ in range(SUBSTEPS):
        total = total + power
        power = v @ power
    return power, total / SUBSTEPS


def split(x):
    a = x.astype(jnp.bfloat16)
    return a, (x - a.astype(jnp.float32)).astype(jnp.bfloat16)


def dot(a, b, ca, cb, precision=None):
    return lax.dot_general(
        a, b, (((ca,), (cb,)), ((), ())), precision=precision, preferred_element_type=jnp.float32
    )


def advection(f, v, low, high):
    cols = f.shape[1]
    lane = lax.broadcasted_iota(jnp.int32, f.shape, 1)
    ahead = jnp.where(lane == cols - 1, high, pltpu.roll(f, cols - 1, 1))
    behind = jnp.where(lane == 0, low, pltpu.roll(f, 1, 1))
    return -v * (ahead - behind) * 0.5 + loop_diff * (ahead - 2.0 * f + behind)


def onehot(pos_row, cols):
    place = lax.broadcasted_iota(jnp.int32, (cols, cols), 0)
    return jnp.where(place == pos_row, 1.0, 0.0).astype(jnp.bfloat16)


CARRIED = (
    (0, 1, 0), (0, 0, 0), (0, 0, 1), (0, 1, 1),
    (1, 0, 0), (1, 1, 0), (1, 0, 1), (1, 1, 1),
)


def row_of(field, half, end):
    return CARRIED.index((field, half, end))


def halves(levels):
    first = up_to(-(-levels // 2), SUB)
    return first, levels - first


def carries(levels, per, width):
    first, second = halves(levels)
    return per >= len(CARRIED) and 3 * levels + first <= width and second < first


def pack_kernel(devices, carry, *refs):
    low_ref, high_ref = (None, None) if carry else refs[4:6]
    out_ref, pos_ref, s_ref, t_ref, q_ref, v_ref, own_ref, sem = refs[-8:]
    copies = [
        pltpu.make_async_copy(source, target, sem.at[n])
        for n, (source, target) in enumerate(zip(refs[:4], (t_ref, q_ref, v_ref, own_ref)))
    ]
    for n in (3, 0, 1, 2):
        copies[n].start()
    nl, cols = t_ref.shape
    width = s_ref.shape[0]
    per = cols // devices
    copies[3].wait()
    own = own_ref[...]
    who = lax.broadcasted_iota(jnp.int32, (devices, cols), 0)
    mine = jnp.where(who == own, 1.0, 0.0)
    before = lax.broadcasted_iota(jnp.int32, (cols, cols), 0) < lax.broadcasted_iota(
        jnp.int32, (cols, cols), 1
    )
    tri = jnp.where(before, 1.0, 0.0).astype(jnp.bfloat16)
    ranks = dot(mine.astype(jnp.bfloat16), tri, 1, 0)
    rank = jnp.sum(ranks * mine, axis=0, keepdims=True)
    pos = own * per + rank.astype(jnp.int32)
    pos_ref[...] = pos
    sel = onehot(pos, cols)

    for n in range(3):
        copies[n].wait()
    t = t_ref[...]
    x = q_ref[...] - 0.5 * t
    v = v_ref[...]
    if carry:
        low = high = jnp.zeros((nl, 1), jnp.float32)
    else:
        low = low_ref[1] - 0.5 * low_ref[0]
        high = high_ref[1] - 0.5 * high_ref[0]
    s_ref[0:nl, :] = x
    s_ref[nl:2 * nl, :] = v
    s_ref[2 * nl:3 * nl, :] = advection(x, v, low, high)
    rest = width - 3 * nl
    if rest:
        s_ref[3 * nl:, :] = jnp.zeros((rest, cols), jnp.float32)
    if carry:
        first, second = halves(nl)
        lane = lax.broadcasted_iota(jnp.int32, (1, cols), 1)
        s_ref[3 * nl + second:3 * nl + second + 1, :] = jnp.where(
            (lane == 0) | (lane == cols - 1), 1.0, 0.0
        )
    a, b = split(s_ref[...])
    out = dot(sel, a, 1, 1) + dot(sel, b, 1, 1)
    if carry:
        fill = jnp.zeros((first - second, cols), jnp.float32)
        parts = []
        for f in (x, t):
            parts += [f[:first], jnp.concatenate([f[first:], fill], axis=0)]
        parts = jnp.concatenate(parts, axis=1)
        shape = (SUB, parts.shape[1])
        want = jnp.full(shape, -1, jnp.int32)
        row = lax.broadcasted_iota(jnp.int32, shape, 0)
        for r, (field, half, end) in enumerate(CARRIED):
            want = jnp.where(row == r, (2 * field + half) * cols + end * (cols - 1), want)
        pick = jnp.where(lax.broadcasted_iota(jnp.int32, shape, 1) == want, 1.0, 0.0).astype(
            jnp.bfloat16
        )
        a, b = split(parts)
        ends = dot(pick, a, 1, 1) + dot(pick, b, 1, 1)
        ends = jnp.concatenate([ends, jnp.zeros((SUB, width - first), jnp.float32)], axis=1)
        ends = pltpu.roll(ends, 3 * nl, 1)
        out = (out.reshape(devices, per, width) + ends[None]).reshape(cols, width)
    out_ref[...] = out


def softplus2(f):
    return jnp.maximum(f, jnp.log2(1.0 + jnp.exp2(jnp.minimum(f, 100.0))))


def lanes(k):
    return pl.ds(k * LANE, LANE)


def fold(part_ref, out_ref, k, scale):
    levels = out_ref.shape[0]
    total = part_ref[pl.ds(0, levels, stride=SUB), :]
    for s in range(1, SUB):
        total = total + part_ref[pl.ds(s, levels, stride=SUB), :]
    out_ref[:, lanes(k)] = total * scale


def clear_tail(part_ref, cz):
    for n in range(part_ref.shape[0]):
        for z in range(cz * SUB, part_ref.shape[1], SUB):
            part_ref[n, pl.ds(z, SUB), :] = jnp.zeros((SUB, LANE), jnp.float32)


def prep_kernel(carry, td_ref, down_ref, after_ref, start_ref, mean_ref, g_ref,
                raw_ref, part_ref, td_sem):
    del after_ref
    cz, cx, cols = td_ref.shape
    nl = down_ref.shape[1]
    zp = mean_ref.shape[0]
    width = g_ref.shape[1]
    groups = cx // SUB
    tiles = cols // LANE
    chunk = -(-cz // td_sem.shape[1])

    def td_copy(k, c):
        levels = pl.ds(c * chunk, min(chunk, cz - c * chunk))
        return pltpu.make_async_copy(
            td_ref.at[levels, :, lanes(k)], raw_ref.at[k, levels], td_sem.at[k, c]
        )

    for k in range(tiles):
        for c in range(td_sem.shape[1]):
            td_copy(k, c).start()

    down = jnp.concatenate(
        [down_ref[...], jnp.zeros((cz, width - nl), jnp.float32)], axis=1
    )
    down = jnp.concatenate([down, jnp.zeros((zp - cz, width), jnp.float32)], axis=0)
    for n in range(3):
        g_ref[n * zp:(n + 1) * zp, :] = down if n == 0 else pltpu.roll(down, n * nl, 1)
    if carry:
        shape = (g_ref.shape[0] - 3 * zp, width)
        row = lax.broadcasted_iota(jnp.int32, shape, 0)
        to = jnp.where(row < nl, row + nl, row + 2 * nl)
        g_ref[3 * zp:, :] = jnp.where(
            lax.broadcasted_iota(jnp.int32, shape, 1) == to, 1.0, 0.0
        )

    clear_tail(part_ref, cz)
    for k in range(tiles):
        for z in range(cz):
            if z % chunk == 0:
                td_copy(k, z // chunk).wait()
            total = None
            for i in range(groups):
                td = raw_ref[k, z, pl.ds(i, SUB, stride=groups), :]
                total = td if total is None else total + td
                start_ref[k, z, pl.ds(SUB * i, SUB), :] = (-0.5 * LOG2E) * td
            part_ref[k, pl.ds(z * SUB, SUB), :] = total
        fold(part_ref.at[k], mean_ref, k, 1.0 / cx)


def cloud_kernel(devices, carry, nl, r_ref, start_ref, td_mean_ref, g_ref, mean_ref, out_ref,
                 d_ref, east_ref, west_ref, force_ref, val_ref, part_ref, mean_buf, mean_sem):
    tiles, cz, cx, _ = start_ref.shape
    zp, cols = td_mean_ref.shape
    per = cols // devices
    groups = cx // SUB

    mean_copy = pltpu.make_async_copy(mean_ref, mean_buf, mean_sem)
    mean_copy.start()

    prof = dot(g_ref[...], r_ref[...], 1, 1, HI)
    d0 = prof[0:zp]
    speed = max_speed * jnp.tanh(prof[zp:2 * zp])
    fd = prof[2 * zp:3 * zp]
    if carry:
        first, second = halves(nl)
        v = prof[3 * zp:3 * zp + nl]
        ends = prof[3 * zp + nl:3 * zp + nl + first]
        flag = ends[second:second + 1] > 0.5
        place = lax.rem(lax.broadcasted_iota(jnp.int32, (1, cols), 1), per)

        def neighbour(end, at):
            step = per if at == 0 else -per
            shift = lambda half: (step + at - row_of(0, half, end)) % cols
            return jnp.concatenate(
                [pltpu.roll(ends, shift(0), 1), pltpu.roll(ends, shift(1), 1)[:second]], axis=0
            )

        behind = neighbour(1, 0) * (loop_diff + 0.5 * v)
        ahead = neighbour(0, per - 1) * (loop_diff - 0.5 * v)
        halo = jnp.where(flag & (place == 0), behind, 0.0) + jnp.where(
            flag & (place == per - 1), ahead, 0.0
        )
        fd = fd + dot(g_ref[0:zp, 0:nl], halo, 1, 0, HI)
    east_ref[...] = mix_along - 0.5 * speed
    west_ref[...] = mix_along + 0.5 * speed
    force_ref[...] = fd * (LOG2E / SUBSTEPS)
    val_ref[0:zp, :] = td_mean_ref[...]
    val_ref[zp:2 * zp, :] = d0
    val_ref[2 * zp:3 * zp, :] = fd
    clear_tail(part_ref, cz)

    def row_at(ref, z, k):
        return jnp.broadcast_to(ref[pl.ds(z, 1), lanes(k)], (SUB, LANE))

    slot = [0] + [SUB * (i + 1) for i in range(1, groups)]
    last = slot[-1]

    def get(k, z):
        return [d_ref[k, z, pl.ds(slot[i], SUB), :] for i in range(groups)]

    def put(k, z, i, new):
        d_ref[k, z, pl.ds(slot[i], SUB), :] = new
        if i == 0:
            d_ref[k, z, pl.ds(SUB, SUB), :] = new
        if i == groups - 1:
            d_ref[k, z, pl.ds(last + SUB, SUB), :] = new

    for k in range(tiles):
        for z in range(cz):
            base = row_at(val_ref, zp + z, k) * LOG2E
            for i in range(groups):
                put(k, z, i, base + start_ref[k, z, pl.ds(SUB * i, SUB), :])

    drain = cond_rate * (1.0 + 0.5 * latent_heat)

    def step(_, carry):
        for k in range(tiles):
            below = cur = get(k, 0)
            pair = None
            for z in range(cz):
                above = get(k, z + 1) if z + 1 < cz else cur
                if pair is None:
                    pair = [c + a for c, a in zip(cur, above)]
                    column = [p + b for p, b in zip(pair, below)]
                else:
                    column = [p + a for p, a in zip(pair, above)]
                    pair = None
                ea = row_at(east_ref, z, k)
                we = row_at(west_ref, z, k)
                fo = row_at(force_ref, z, k)
                ring = [d_ref[k, z, pl.ds(last + SUB - 1, SUB), :]] + cur
                ring = ring + [d_ref[k, z, pl.ds(1, SUB), :]]
                for i in range(groups):
                    new = (
                        mix_vertical * column[i]
                        + ea * ring[i + 2]
                        + we * ring[i]
                        + fo
                        - drain * softplus2(cur[i])
                    )
                    put(k, z, i, new)
                below, cur = cur, above
        return carry

    lax.fori_loop(0, SUBSTEPS, step, 0)

    for k in range(tiles):
        for z in range(cz):
            total = cloud = None
            for f in get(k, z):
                c = softplus2(f)
                total = f if total is None else total + f
                cloud = c if cloud is None else cloud + c
            part_ref[2 * k, pl.ds(z * SUB, SUB), :] = total
            part_ref[2 * k + 1, pl.ds(z * SUB, SUB), :] = cloud
        fold(part_ref.at[2 * k], val_ref.at[pl.ds(3 * zp, zp)], k, LN2 / cx)
        fold(part_ref.at[2 * k + 1], val_ref.at[pl.ds(4 * zp, zp)], k, LN2 / cx)
    val_ref[zp:2 * zp, :] = val_ref[zp:2 * zp, :] - 0.5 * val_ref[0:zp, :]
    mean_copy.wait()
    out_ref[...] = dot(val_ref[...], mean_buf[...], 0, 0, HI)


def base_kernel(devices, carry, *refs):
    t_ref, q_ref, v_ref, down_ref, up_ref, lin_ref, after_ref, r_ref = refs[:8]
    high_ref = None if carry else refs[8]
    to_ref, qo_ref = refs[-2:]
    del after_ref
    nl, cols = t_ref.shape
    per = cols // devices
    if carry:
        first, second = halves(nl)
        me = lax.axis_index(AXES)

        def ends(device, end):
            start = pl.multiple_of(device * per, SUB)
            block = r_ref[pl.ds(start, SUB), :]
            block = pltpu.roll(block, block.shape[1] - 3 * nl, 1)[:, :LANE].T
            x, t = [
                jnp.concatenate(
                    [
                        block[:first, row_of(field, 0, end):row_of(field, 0, end) + 1],
                        block[:second, row_of(field, 1, end):row_of(field, 1, end) + 1],
                    ],
                    axis=0,
                )
                for field in (0, 1)
            ]
            return t, x + 0.5 * t

        low = ends(lax.rem(me + devices - 1, devices), 1)
        high = ends(lax.rem(me + 1, devices), 0)
    else:
        low = (r_ref[0], r_ref[1])
        high = (high_ref[0], high_ref[1])
    v = v_ref[...]
    t = t_ref[...]
    q = q_ref[...]
    advt = advection(t, v, low[0], high[0])
    advq = advection(q, v, low[1], high[1])
    prof = dot(down_ref[...], jnp.concatenate([t, q, advt, advq], axis=1), 1, 0, HI)
    lin = lin_ref[...]
    gain = dot(lin[0], prof[:, :2 * cols], 1, 0, HI) + dot(lin[1], prof[:, 2 * cols:], 1, 0, HI)
    gain = dot(up_ref[...], gain, 1, 0, HI)
    to_ref[...] = t + advt + gain[:, :cols]
    qo_ref[...] = q + advq + gain[:, cols:]


def finish_kernel(zp, r_ref, pos_ref, up_ref, tb_ref, qb_ref, to_ref, qo_ref, co_ref):
    nl, cols = tb_ref.shape
    cz = up_ref.shape[1]
    width = r_ref.shape[1]
    up = jnp.concatenate([up_ref[...], jnp.zeros((nl, width - cz), jnp.float32)], axis=1)
    up = jnp.concatenate([up, -pltpu.roll(up, zp, 1), pltpu.roll(up, 2 * zp, 1)], axis=0)
    sel = onehot(pos_ref[...], cols)
    a, b = split(dot(up, r_ref[...], 1, 1, HI))
    out = dot(a, sel, 1, 0) + dot(b, sel, 1, 0)
    to_ref[...] = tb_ref[...] + out[0:nl]
    qo_ref[...] = qb_ref[...] + out[nl:2 * nl]
    co_ref[...] = out[2 * nl:3 * nl]


def local(
    thermal_anomaly,
    vapour_anomaly,
    periodic_flow_velocity,
    processor_assignment,
    thermal_disturbance,
    layer_index_downscale,
    layer_index_upscale,
):
    nl, cols = thermal_anomaly.shape
    cz, cx, _ = thermal_disturbance.shape
    devices = lax.axis_size(AXES)
    per = cols // devices
    zp = up_to(cz, SUB)
    f32 = jnp.float32
    width = up_to(3 * nl, LANE)
    back = up_to(3 * zp, LANE)
    field = jax.ShapeDtypeStruct((nl, cols), f32)
    carry = carries(nl, per, width)

    fields = (thermal_anomaly, vapour_anomaly, periodic_flow_velocity)
    ends = () if carry else edges(jnp.stack(fields[:2]))
    out, pos = pl.pallas_call(
        functools.partial(pack_kernel, devices, carry),
        out_shape=(
            jax.ShapeDtypeStruct((cols, width), f32),
            jax.ShapeDtypeStruct((1, cols), jnp.int32),
        ),
        in_specs=[HBM] * 4 + [VMEM] * len(ends),
        out_specs=(VMEM,) * 2,
        scratch_shapes=[
            pltpu.VMEM((width, cols), f32),
            pltpu.VMEM((nl, cols), f32),
            pltpu.VMEM((nl, cols), f32),
            pltpu.VMEM((nl, cols), f32),
            pltpu.VMEM((1, cols), jnp.int32),
            pltpu.SemaphoreType.DMA((4,)),
        ],
        compiler_params=pltpu.CompilerParams(vmem_limit_bytes=VMEM_ALL),
        name="pack",
    )(*fields, processor_assignment.reshape(1, cols), *ends)

    def exchange(blocks):
        shape = blocks.shape
        blocks = blocks.reshape(devices, per, shape[1])
        return lax.all_to_all(blocks, AXES, split_axis=0, concat_axis=0, tiled=True).reshape(shape)

    r1 = exchange(out)

    power, total = mean_operators(cz)
    release = 1.0 + 0.5 * latent_heat
    mean = np.zeros((5 * zp, back))
    z_part = np.zeros((5 * zp, cz))
    z_part[zp:zp + cz] = power.T / release
    z_part[2 * zp:2 * zp + cz] = total.T / release
    z_part[3 * zp:3 * zp + cz] = -np.eye(cz) / release
    mean[0:cz, 0:cz] = power.T
    mean[:, 0:cz] += latent_heat * z_part
    mean[:, zp:zp + cz] = z_part
    mean[4 * zp:4 * zp + cz, 2 * zp:2 * zp + cz] = np.eye(cz)

    tiles = cols // LANE
    groups = cx // SUB
    level_rows = 3 * zp + (nl + halves(nl)[0] if carry else 0)
    prep = pl.pallas_call(
        functools.partial(prep_kernel, carry),
        out_shape=(
            jax.ShapeDtypeStruct((tiles, cz, cx, LANE), f32),
            jax.ShapeDtypeStruct((zp, cols), f32),
            jax.ShapeDtypeStruct((level_rows, width), f32),
        ),
        in_specs=[HBM, VMEM, ANY],
        out_specs=(VMEM,) * 3,
        scratch_shapes=[
            pltpu.VMEM((tiles, cz, cx, LANE), f32),
            pltpu.VMEM((tiles, zp * SUB, LANE), f32),
            pltpu.SemaphoreType.DMA((tiles, 5)),
        ],
        compiler_params=pltpu.CompilerParams(vmem_limit_bytes=VMEM_PACK),
        cost_estimate=pl.CostEstimate(flops=10**8, bytes_accessed=4 * 10**6, transcendentals=0),
        name="prep",
    )(thermal_disturbance, layer_index_downscale, out)
    vals = pl.pallas_call(
        functools.partial(cloud_kernel, devices, carry, nl),
        out_shape=jax.ShapeDtypeStruct((cols, back), f32),
        in_specs=[VMEM] * 4 + [HBM],
        out_specs=VMEM,
        scratch_shapes=[
            pltpu.VMEM((tiles, cz, SUB * (groups + 2), LANE), f32),
            pltpu.VMEM((zp, cols), f32),
            pltpu.VMEM((zp, cols), f32),
            pltpu.VMEM((zp, cols), f32),
            pltpu.VMEM((5 * zp, cols), f32),
            pltpu.VMEM((2 * tiles, zp * SUB, LANE), f32),
            pltpu.VMEM((5 * zp, back), f32),
            pltpu.SemaphoreType.DMA,
        ],
        compiler_params=pltpu.CompilerParams(vmem_limit_bytes=VMEM_CLOUD),
        name="cloud",
    )(r1, *prep, jnp.asarray(mean, f32))
    r2 = exchange(vals)

    lin = np.stack([power - np.eye(cz), total])
    halo = (r1,) if carry else ends
    base = pl.pallas_call(
        functools.partial(base_kernel, devices, carry),
        out_shape=(field,) * 2,
        in_specs=[VMEM] * 6 + [ANY] + [VMEM] * len(halo),
        out_specs=(VMEM,) * 2,
        compiler_params=pltpu.CompilerParams(vmem_limit_bytes=VMEM_PACK),
        cost_estimate=pl.CostEstimate(flops=10**8, bytes_accessed=10**6, transcendentals=0),
        name="base",
    )(*fields, layer_index_downscale, layer_index_upscale, jnp.asarray(lin, f32), vals, *halo)
    return pl.pallas_call(
        functools.partial(finish_kernel, zp),
        out_shape=(field,) * 3,
        in_specs=[VMEM] * 5,
        out_specs=(VMEM,) * 3,
        compiler_params=pltpu.CompilerParams(vmem_limit_bytes=VMEM_PACK),
        name="finish",
    )(r2, pos, layer_index_upscale, *base)


VMEM_ALL = 60 * 1024 * 2**10
VMEM_PACK = 16 * 2**20
VMEM_CLOUD = 24 * 2**20


def solution(mesh):
    in_specs = (
        P(None, AXES),
        P(None, AXES),
        P(None, AXES),
        P(AXES),
        P(None, None, AXES),
        P(),
        P(),
    )
    out_specs = (P(None, AXES), P(None, AXES), P(None, AXES))
    return jax.shard_map(local, mesh=mesh, in_specs=in_specs, out_specs=out_specs, check_vma=False)
```

```python
import functools

import numpy as np

import jax
import jax.numpy as jnp
from jax import lax
from jax.experimental import pallas as pl
from jax.experimental.pallas import tpu as pltpu
from jax.sharding import PartitionSpec as P

SUBSTEPS = 10

loop_diff = 0.35
mix_along = 0.35
mix_vertical = 0.1
cond_rate = 0.1
latent_heat = 1.5
max_speed = 0.8

AXES = ("tile", "crm")
LOG2E = 1.4426950408889634
LN2 = 0.6931471805599453
SUB = 8
LANE = 128
HI = lax.Precision.HIGH
VMEM = pl.BlockSpec(memory_space=pltpu.VMEM)
HBM = pl.BlockSpec(memory_space=pltpu.HBM)


def in_hbm(x):
    return pltpu.with_memory_space_constraint(x, pltpu.HBM)


def up_to(n, m):
    return -(-n // m) * m


def edges(block):
    count = lax.axis_size(AXES)
    forward = [(i, (i + 1) % count) for i in range(count)]
    backward = [(t, s) for s, t in forward]
    low = lax.ppermute(block[:, :, -1:], AXES, forward)
    high = lax.ppermute(block[:, :, :1], AXES, backward)
    return low, high


def ring_mean_operator(levels):
    f = np.eye(levels)
    east = west = f
    above = np.concatenate([f[1:], f[-1:]], axis=0)
    below = np.concatenate([f[:1], f[:-1]], axis=0)
    return (
        f
        + mix_along * (east - 2.0 * f + west)
        + mix_vertical * (above - 2.0 * f + below)
    )


def mean_operators(levels):
    v = ring_mean_operator(levels)
    power = np.eye(levels)
    total = np.zeros((levels, levels))
    for _ in range(SUBSTEPS):
        total = total + power
        power = v @ power
    return power, total / SUBSTEPS


def split(x):
    a = x.astype(jnp.bfloat16)
    return a, (x - a.astype(jnp.float32)).astype(jnp.bfloat16)


def dot(a, b, ca, cb, precision=None):
    return lax.dot_general(
        a, b, (((ca,), (cb,)), ((), ())), precision=precision, preferred_element_type=jnp.float32
    )


def advection(f, v, low, high):
    cols = f.shape[1]
    lane = lax.broadcasted_iota(jnp.int32, f.shape, 1)
    ahead = jnp.where(lane == cols - 1, high, pltpu.roll(f, cols - 1, 1))
    behind = jnp.where(lane == 0, low, pltpu.roll(f, 1, 1))
    return -v * (ahead - behind) * 0.5 + loop_diff * (ahead - 2.0 * f + behind)


def onehot(pos_row, cols):
    place = lax.broadcasted_iota(jnp.int32, (cols, cols), 0)
    return jnp.where(place == pos_row, 1.0, 0.0).astype(jnp.bfloat16)


SLOT = 32
SLOTS = LANE // SLOT


def return_shape(cz, per):
    head = (LANE - 2 * cz) // SUB * SUB
    assert 0 <= head <= cz and cz - head <= SLOT
    return head, per + -(-per // SLOTS)


def slot_onehot(place_row, devices, per, cols):
    row = place_row % per // SLOTS * devices + place_row // per
    rows = -(-per // SLOTS) * devices
    return jnp.where(
        lax.broadcasted_iota(jnp.int32, (rows, cols), 0) == row, 1.0, 0.0
    ).astype(jnp.bfloat16)


CARRIED = (
    (0, 1, 0), (0, 0, 0), (0, 0, 1), (0, 1, 1),
    (1, 0, 0), (1, 1, 0), (1, 0, 1), (1, 1, 1),
)


def row_of(field, half, end):
    return CARRIED.index((field, half, end))


def halves(levels):
    first = up_to(-(-levels // 2), SUB)
    return first, levels - first


def carries(levels, per, width):
    first, second = halves(levels)
    return per >= len(CARRIED) and 3 * levels + first <= width and second < first


def pack_kernel(devices, carry, *refs):
    low_ref, high_ref = (None, None) if carry else refs[4:6]
    out_ref, pos_ref, s_ref, t_ref, q_ref, v_ref, own_ref, sem = refs[-8:]
    copies = [
        pltpu.make_async_copy(source, target, sem.at[n])
        for n, (source, target) in enumerate(zip(refs[:4], (t_ref, q_ref, v_ref, own_ref)))
    ]
    for n in (3, 0, 1, 2):
        copies[n].start()
    nl, cols = t_ref.shape
    width = s_ref.shape[0]
    per = cols // devices
    copies[3].wait()
    own = own_ref[...]
    who = lax.broadcasted_iota(jnp.int32, (devices, cols), 0)
    mine = jnp.where(who == own, 1.0, 0.0)
    before = lax.broadcasted_iota(jnp.int32, (cols, cols), 0) < lax.broadcasted_iota(
        jnp.int32, (cols, cols), 1
    )
    tri = jnp.where(before, 1.0, 0.0).astype(jnp.bfloat16)
    ranks = dot(mine.astype(jnp.bfloat16), tri, 1, 0)
    rank = jnp.sum(ranks * mine, axis=0, keepdims=True)
    pos = own * per + rank.astype(jnp.int32)
    pos_ref[...] = pos
    sel = onehot(pos, cols)

    for n in range(3):
        copies[n].wait()
    t = t_ref[...]
    x = q_ref[...] - 0.5 * t
    v = v_ref[...]
    if carry:
        low = high = jnp.zeros((nl, 1), jnp.float32)
    else:
        low = low_ref[1] - 0.5 * low_ref[0]
        high = high_ref[1] - 0.5 * high_ref[0]
    s_ref[0:nl, :] = x
    s_ref[nl:2 * nl, :] = v
    s_ref[2 * nl:3 * nl, :] = advection(x, v, low, high)
    rest = width - 3 * nl
    if rest:
        s_ref[3 * nl:, :] = jnp.zeros((rest, cols), jnp.float32)
    if carry:
        first, second = halves(nl)
        lane = lax.broadcasted_iota(jnp.int32, (1, cols), 1)
        s_ref[3 * nl + second:3 * nl + second + 1, :] = jnp.where(
            (lane == 0) | (lane == cols - 1), 1.0, 0.0
        )
    a, b = split(s_ref[...])
    out = dot(sel, a, 1, 1) + dot(sel, b, 1, 1)
    if carry:
        fill = jnp.zeros((first - second, cols), jnp.float32)
        parts = []
        for f in (x, t):
            parts += [f[:first], jnp.concatenate([f[first:], fill], axis=0)]
        parts = jnp.concatenate(parts, axis=1)
        shape = (SUB, parts.shape[1])
        want = jnp.full(shape, -1, jnp.int32)
        row = lax.broadcasted_iota(jnp.int32, shape, 0)
        for r, (field, half, end) in enumerate(CARRIED):
            want = jnp.where(row == r, (2 * field + half) * cols + end * (cols - 1), want)
        pick = jnp.where(lax.broadcasted_iota(jnp.int32, shape, 1) == want, 1.0, 0.0).astype(
            jnp.bfloat16
        )
        a, b = split(parts)
        ends = dot(pick, a, 1, 1) + dot(pick, b, 1, 1)
        ends = jnp.concatenate([ends, jnp.zeros((SUB, width - first), jnp.float32)], axis=1)
        ends = pltpu.roll(ends, 3 * nl, 1)
        out = (out.reshape(devices, per, width) + ends[None]).reshape(cols, width)
    out_ref[...] = out


LARGEST = 120.0


def small_softplus2(f):
    return jnp.log2(1.0 + jnp.exp2(f))


def softplus2(f):
    return jnp.maximum(f, jnp.log2(1.0 + jnp.exp2(jnp.minimum(f, 100.0))))


def lanes(k):
    return pl.ds(k * LANE, LANE)


def fold(part_ref, out_ref, k, scale):
    levels = out_ref.shape[0]
    total = part_ref[pl.ds(0, levels, stride=SUB), :]
    for s in range(1, SUB):
        total = total + part_ref[pl.ds(s, levels, stride=SUB), :]
    out_ref[:, lanes(k)] = total * scale


def clear_tail(part_ref, cz):
    for n in range(part_ref.shape[0]):
        for z in range(cz * SUB, part_ref.shape[1], SUB):
            part_ref[n, pl.ds(z, SUB), :] = jnp.zeros((SUB, LANE), jnp.float32)


def prep_kernel(carry, td_ref, down_ref, after_ref, start_ref, mean_ref, g_ref, most_ref,
                raw_ref, part_ref, td_sem):
    del after_ref
    cz, cx, cols = td_ref.shape
    nl = down_ref.shape[1]
    zp = mean_ref.shape[0]
    width = g_ref.shape[1]
    groups = cx // SUB
    tiles = cols // LANE
    chunk = -(-cz // td_sem.shape[1])

    def td_copy(k, c):
        levels = pl.ds(c * chunk, min(chunk, cz - c * chunk))
        return pltpu.make_async_copy(
            td_ref.at[levels, :, lanes(k)], raw_ref.at[k, levels], td_sem.at[k, c]
        )

    for k in range(tiles):
        for c in range(td_sem.shape[1]):
            td_copy(k, c).start()

    down = jnp.concatenate(
        [down_ref[...], jnp.zeros((cz, width - nl), jnp.float32)], axis=1
    )
    down = jnp.concatenate([down, jnp.zeros((zp - cz, width), jnp.float32)], axis=0)
    for n in range(3):
        g_ref[n * zp:(n + 1) * zp, :] = down if n == 0 else pltpu.roll(down, n * nl, 1)
    if carry:
        shape = (g_ref.shape[0] - 3 * zp, width)
        row = lax.broadcasted_iota(jnp.int32, shape, 0)
        to = jnp.where(row < nl, row + nl, row + 2 * nl)
        g_ref[3 * zp:, :] = jnp.where(
            lax.broadcasted_iota(jnp.int32, shape, 1) == to, 1.0, 0.0
        )

    clear_tail(part_ref, cz)
    most = [jnp.zeros((SUB, LANE), jnp.float32)] * groups
    for k in range(tiles):
        for z in range(cz):
            if z % chunk == 0:
                td_copy(k, z // chunk).wait()
            total = None
            for i in range(groups):
                td = raw_ref[k, z, pl.ds(i, SUB, stride=groups), :]
                total = td if total is None else total + td
                first = (-0.5 * LOG2E) * td
                start_ref[k, z, pl.ds(SUB * i, SUB), :] = first
                most[i] = jnp.maximum(most[i], jnp.abs(first))
            part_ref[k, pl.ds(z * SUB, SUB), :] = total
        fold(part_ref.at[k], mean_ref, k, 1.0 / cx)
    most_ref[...] = functools.reduce(jnp.maximum, most)


def cloud_kernel(devices, carry, nl, r_ref, start_ref, td_mean_ref, g_ref, most_ref, mean_ref,
                 out_ref, d_ref, base_ref, east_ref, west_ref, force_ref, val_ref, part_ref):
    tiles, cz, cx, _ = start_ref.shape
    zp, cols = td_mean_ref.shape
    per = cols // devices
    groups = cx // SUB

    prof = dot(g_ref[...], r_ref[...], 1, 1, HI)
    d0 = prof[0:zp]
    speed = max_speed * jnp.tanh(prof[zp:2 * zp])
    fd = prof[2 * zp:3 * zp]
    if carry:
        first, second = halves(nl)
        v = prof[3 * zp:3 * zp + nl]
        ends = prof[3 * zp + nl:3 * zp + nl + first]
        flag = ends[second:second + 1] > 0.5
        place = lax.rem(lax.broadcasted_iota(jnp.int32, (1, cols), 1), per)

        def neighbour(end, at):
            step = per if at == 0 else -per
            shift = lambda half: (step + at - row_of(0, half, end)) % cols
            return jnp.concatenate(
                [pltpu.roll(ends, shift(0), 1), pltpu.roll(ends, shift(1), 1)[:second]], axis=0
            )

        behind = neighbour(1, 0) * (loop_diff + 0.5 * v)
        ahead = neighbour(0, per - 1) * (loop_diff - 0.5 * v)
        halo = jnp.where(flag & (place == 0), behind, 0.0) + jnp.where(
            flag & (place == per - 1), ahead, 0.0
        )
        fd = fd + dot(g_ref[0:zp, 0:nl], halo, 1, 0, HI)
    base_ref[...] = d0 * LOG2E
    east_ref[...] = mix_along - 0.5 * speed
    west_ref[...] = mix_along + 0.5 * speed
    force = fd * (LOG2E / SUBSTEPS)
    force_ref[...] = force
    drain = cond_rate * (1.0 + 0.5 * latent_heat)
    rate = 1.0 - 2.0 * mix_along + max(2.0 * mix_along, max_speed)
    growth = rate**SUBSTEPS
    series = sum(rate**n for n in range(SUBSTEPS))
    bound = growth * (jnp.max(jnp.abs(d0)) * LOG2E + jnp.max(most_ref[...])) + series * (
        jnp.max(jnp.abs(force)) + drain
    )
    val_ref[0:zp, :] = td_mean_ref[...]
    val_ref[zp:2 * zp, :] = d0 - 0.5 * td_mean_ref[...]
    val_ref[2 * zp:3 * zp, :] = fd
    clear_tail(part_ref, cz)

    def row_at(ref, z, k):
        return jnp.broadcast_to(ref[pl.ds(z, 1), lanes(k)], (SUB, LANE))

    slot = [0] + [SUB * (i + 1) for i in range(1, groups)]
    last = slot[-1]

    def get(k, z):
        return [d_ref[k, z, pl.ds(slot[i], SUB), :] for i in range(groups)]

    def put(k, z, i, new):
        d_ref[k, z, pl.ds(slot[i], SUB), :] = new
        if i == 0:
            d_ref[k, z, pl.ds(SUB, SUB), :] = new
        if i == groups - 1:
            d_ref[k, z, pl.ds(last + SUB, SUB), :] = new

    for k in range(tiles):
        for z in range(cz):
            base = row_at(base_ref, z, k)
            for i in range(groups):
                put(k, z, i, base + start_ref[k, z, pl.ds(SUB * i, SUB), :])

    def step(softplus, _, carry):
        for k in range(tiles):
            below = cur = get(k, 0)
            pair = None
            for z in range(cz):
                above = get(k, z + 1) if z + 1 < cz else cur
                if pair is None:
                    pair = [c + a for c, a in zip(cur, above)]
                    column = [p + b for p, b in zip(pair, below)]
                else:
                    column = [p + a for p, a in zip(pair, above)]
                    pair = None
                ea = row_at(east_ref, z, k)
                we = row_at(west_ref, z, k)
                fo = row_at(force_ref, z, k)
                ring = [d_ref[k, z, pl.ds(last + SUB - 1, SUB), :]] + cur
                ring = ring + [d_ref[k, z, pl.ds(1, SUB), :]]
                for i in range(groups):
                    new = (
                        mix_vertical * column[i]
                        + ea * ring[i + 2]
                        + we * ring[i]
                        + fo
                        - drain * softplus(cur[i])
                    )
                    put(k, z, i, new)
                below, cur = cur, above
        return carry

    @pl.when(bound < LARGEST)
    def _():
        lax.fori_loop(0, SUBSTEPS, functools.partial(step, small_softplus2), 0)

    @pl.when(jnp.logical_not(bound < LARGEST))
    def _():
        lax.fori_loop(0, SUBSTEPS, functools.partial(step, softplus2), 0)

    head, rows = return_shape(cz, per)
    cloud_ref = east_ref
    for k in range(tiles):
        for z in range(cz):
            total = cloud = None
            for f in get(k, z):
                c = softplus2(f)
                total = f if total is None else total + f
                cloud = c if cloud is None else cloud + c
            part_ref[2 * k, pl.ds(z * SUB, SUB), :] = total
            part_ref[2 * k + 1, pl.ds(z * SUB, SUB), :] = cloud
        fold(part_ref.at[2 * k], val_ref.at[pl.ds(3 * zp, zp)], k, LN2 / cx)
        fold(part_ref.at[2 * k + 1], cloud_ref, k, LN2 / cx)
        val_ref[4 * zp:, lanes(k)] = cloud_ref[0:head, lanes(k)]
        main = dot(val_ref[:, lanes(k)], mean_ref[...], 0, 0, HI)
        for h in range(LANE // per):
            out_ref[pl.ds((k * (LANE // per) + h) * rows, per), :] = main[h * per:(h + 1) * per]
    left = cloud_ref[head:, :]
    left = jnp.concatenate([left, jnp.zeros((SLOT - left.shape[0], cols), jnp.float32)], axis=0) \
        if left.shape[0] < SLOT else left
    place = lax.broadcasted_iota(jnp.int32, (1, cols), 1)
    part = place % SLOTS
    spread = jnp.concatenate(
        [jnp.where(part == j, left, 0.0) for j in range(SLOTS)], axis=0
    )
    pick = slot_onehot(place, devices, per, cols)
    a, b = split(spread)
    extra = dot(pick, a, 1, 1) + dot(pick, b, 1, 1)
    for i in range(rows - per):
        out_ref[pl.ds(per + i, devices, stride=rows), :] = extra[i * devices:(i + 1) * devices]


def base_kernel(devices, carry, *refs):
    t_ref, q_ref, v_ref, down_ref, up_ref, lin_ref, pos_ref, after_ref, r_ref = refs[:9]
    high_ref = None if carry else refs[9]
    to_ref, qo_ref, level_ref, rest_ref, sel_ref, pick_ref = refs[-6:]
    del after_ref
    nl, cols = t_ref.shape
    cz = up_ref.shape[1]
    per = cols // devices
    head, _ = return_shape(cz, per)
    up = up_ref[...]
    wide = jnp.concatenate([up, jnp.zeros((nl, LANE - cz), jnp.float32)], axis=1)
    lane = lax.broadcasted_iota(jnp.int32, wide.shape, 1)
    level_ref[0:nl, :] = wide
    level_ref[nl:2 * nl, :] = -pltpu.roll(wide, cz, 1)
    level_ref[2 * nl:3 * nl, :] = pltpu.roll(jnp.where(lane < head, wide, 0.0), 2 * cz, 1)
    rest_ref[...] = jnp.where(lane < SLOT, pltpu.roll(wide, LANE - head, 1), 0.0)
    sel_ref[...] = onehot(pos_ref[...], cols)
    pick_ref[...] = slot_onehot(pos_ref[...], devices, per, cols)
    if carry:
        first, second = halves(nl)
        me = lax.axis_index(AXES)

        def ends(device, end):
            start = pl.multiple_of(device * per, SUB)
            block = r_ref[pl.ds(start, SUB), :]
            block = pltpu.roll(block, block.shape[1] - 3 * nl, 1)[:, :LANE].T
            x, t = [
                jnp.concatenate(
                    [
                        block[:first, row_of(field, 0, end):row_of(field, 0, end) + 1],
                        block[:second, row_of(field, 1, end):row_of(field, 1, end) + 1],
                    ],
                    axis=0,
                )
                for field in (0, 1)
            ]
            return t, x + 0.5 * t

        low = ends(lax.rem(me + devices - 1, devices), 1)
        high = ends(lax.rem(me + 1, devices), 0)
    else:
        low = (r_ref[0], r_ref[1])
        high = (high_ref[0], high_ref[1])
    v = v_ref[...]
    t = t_ref[...]
    q = q_ref[...]
    advt = advection(t, v, low[0], high[0])
    advq = advection(q, v, low[1], high[1])
    prof = dot(down_ref[...], jnp.concatenate([t, q, advt, advq], axis=1), 1, 0, HI)
    lin = lin_ref[...]
    gain = dot(lin[0], prof[:, :2 * cols], 1, 0, HI) + dot(lin[1], prof[:, 2 * cols:], 1, 0, HI)
    gain = dot(up, gain, 1, 0, HI)
    to_ref[...] = t + advt + gain[:, :cols]
    qo_ref[...] = q + advq + gain[:, cols:]


def finish_kernel(devices, r_ref, pos_ref, tb_ref, qb_ref, level_ref, rest_ref, sel_ref, pick_ref,
                  to_ref, qo_ref, co_ref):
    nl, cols = tb_ref.shape
    per = cols // devices
    rows = r_ref.shape[0] // devices
    main = jnp.concatenate([r_ref[pl.ds(h * rows, per), :] for h in range(devices)], axis=0)
    extra = jnp.concatenate(
        [r_ref[pl.ds(per + i, devices, stride=rows), :] for i in range(rows - per)], axis=0
    )
    a, b = split(extra)
    extra = dot(a, pick_ref[...], 0, 0) + dot(b, pick_ref[...], 0, 0)
    part = pos_ref[...] % per % SLOTS
    left = jnp.where(part == 0, extra[:SLOT], 0.0)
    for j in range(1, SLOTS):
        left = left + jnp.where(part == j, extra[j * SLOT:(j + 1) * SLOT], 0.0)
    rest = dot(rest_ref[:, 0:SLOT], left, 1, 0, HI)
    a, b = split(dot(level_ref[...], main, 1, 1, HI))
    out = dot(a, sel_ref[...], 1, 0) + dot(b, sel_ref[...], 1, 0)
    to_ref[...] = tb_ref[...] + out[0:nl]
    qo_ref[...] = qb_ref[...] + out[nl:2 * nl]
    co_ref[...] = out[2 * nl:3 * nl] + rest


def local(
    thermal_anomaly,
    vapour_anomaly,
    periodic_flow_velocity,
    processor_assignment,
    thermal_disturbance,
    layer_index_downscale,
    layer_index_upscale,
):
    nl, cols = thermal_anomaly.shape
    cz, cx, _ = thermal_disturbance.shape
    devices = lax.axis_size(AXES)
    per = cols // devices
    zp = up_to(cz, SUB)
    f32 = jnp.float32
    width = up_to(3 * nl, LANE)
    head, rows = return_shape(cz, per)
    field = jax.ShapeDtypeStruct((nl, cols), f32)
    carry = carries(nl, per, width)

    fields = (thermal_anomaly, vapour_anomaly, periodic_flow_velocity)
    ends = () if carry else edges(jnp.stack(fields[:2]))
    out, pos = pl.pallas_call(
        functools.partial(pack_kernel, devices, carry),
        out_shape=(
            jax.ShapeDtypeStruct((cols, width), f32),
            jax.ShapeDtypeStruct((1, cols), jnp.int32),
        ),
        in_specs=[HBM] * 4 + [VMEM] * len(ends),
        out_specs=(VMEM,) * 2,
        scratch_shapes=[
            pltpu.VMEM((width, cols), f32),
            pltpu.VMEM((nl, cols), f32),
            pltpu.VMEM((nl, cols), f32),
            pltpu.VMEM((nl, cols), f32),
            pltpu.VMEM((1, cols), jnp.int32),
            pltpu.SemaphoreType.DMA((4,)),
        ],
        compiler_params=pltpu.CompilerParams(vmem_limit_bytes=VMEM_PACK),
        name="pack",
    )(*[in_hbm(f) for f in (*fields, processor_assignment.reshape(1, cols))], *ends)

    def exchange(blocks, *inner):
        shape = blocks.shape
        blocks = blocks.reshape(devices, *inner)
        return lax.all_to_all(blocks, AXES, split_axis=0, concat_axis=0, tiled=True).reshape(shape)

    r1 = exchange(out, per, width)

    power, total = mean_operators(cz)
    release = 1.0 + 0.5 * latent_heat
    mean = np.zeros((4 * zp + head, LANE))
    z_part = np.zeros((4 * zp + head, cz))
    z_part[zp:zp + cz] = power.T / release
    z_part[2 * zp:2 * zp + cz] = total.T / release
    z_part[3 * zp:3 * zp + cz] = -np.eye(cz) / release
    mean[0:cz, 0:cz] = power.T
    mean[:, 0:cz] += latent_heat * z_part
    mean[:, cz:2 * cz] = z_part
    mean[4 * zp:, 2 * cz:2 * cz + head] = np.eye(head)

    tiles = cols // LANE
    groups = cx // SUB
    level_rows = 3 * zp + (nl + halves(nl)[0] if carry else 0)
    prep = pl.pallas_call(
        functools.partial(prep_kernel, carry),
        out_shape=(
            jax.ShapeDtypeStruct((tiles, cz, cx, LANE), f32),
            jax.ShapeDtypeStruct((zp, cols), f32),
            jax.ShapeDtypeStruct((level_rows, width), f32),
            jax.ShapeDtypeStruct((SUB, LANE), f32),
        ),
        in_specs=[HBM, VMEM, HBM],
        out_specs=(VMEM,) * 4,
        scratch_shapes=[
            pltpu.VMEM((tiles, cz, cx, LANE), f32),
            pltpu.VMEM((tiles, zp * SUB, LANE), f32),
            pltpu.SemaphoreType.DMA((tiles, 5)),
        ],
        compiler_params=pltpu.CompilerParams(vmem_limit_bytes=VMEM_PACK),
        cost_estimate=pl.CostEstimate(flops=10**8, bytes_accessed=4 * 10**6, transcendentals=0),
        name="prep",
    )(in_hbm(thermal_disturbance), layer_index_downscale, in_hbm(out))
    vals = pl.pallas_call(
        functools.partial(cloud_kernel, devices, carry, nl),
        out_shape=jax.ShapeDtypeStruct((devices * rows, LANE), f32),
        in_specs=[VMEM] * 6,
        out_specs=VMEM,
        scratch_shapes=[
            pltpu.VMEM((tiles, cz, SUB * (groups + 2), LANE), f32),
            pltpu.VMEM((zp, cols), f32),
            pltpu.VMEM((zp, cols), f32),
            pltpu.VMEM((zp, cols), f32),
            pltpu.VMEM((zp, cols), f32),
            pltpu.VMEM((4 * zp + head, cols), f32),
            pltpu.VMEM((2 * tiles, zp * SUB, LANE), f32),
        ],
        compiler_params=pltpu.CompilerParams(vmem_limit_bytes=VMEM_CLOUD),
        name="cloud",
    )(r1, *prep, jnp.asarray(mean, f32))
    r2 = exchange(vals, 1, rows * LANE)

    lin = np.stack([power - np.eye(cz), total])
    halo = (r1,) if carry else ends
    base = pl.pallas_call(
        functools.partial(base_kernel, devices, carry),
        out_shape=(
            field,
            field,
            jax.ShapeDtypeStruct((3 * nl, LANE), f32),
            jax.ShapeDtypeStruct((nl, LANE), f32),
            jax.ShapeDtypeStruct((cols, cols), jnp.bfloat16),
            jax.ShapeDtypeStruct((devices * (rows - per), cols), jnp.bfloat16),
        ),
        in_specs=[VMEM] * 7 + [HBM] + [VMEM] * len(halo),
        out_specs=(VMEM,) * 6,
        compiler_params=pltpu.CompilerParams(vmem_limit_bytes=VMEM_PACK),
        cost_estimate=pl.CostEstimate(flops=10**8, bytes_accessed=10**6, transcendentals=0),
        name="base",
    )(*fields, layer_index_downscale, layer_index_upscale, jnp.asarray(lin, f32), pos, in_hbm(vals), *halo)
    return pl.pallas_call(
        functools.partial(finish_kernel, devices),
        out_shape=(field,) * 3,
        in_specs=[VMEM] * 8,
        out_specs=(VMEM,) * 3,
        compiler_params=pltpu.CompilerParams(vmem_limit_bytes=VMEM_PACK),
        name="finish",
    )(r2, pos, *base)


VMEM_PACK = 16 * 2**20
VMEM_CLOUD = 24 * 2**20


def solution(mesh):
    in_specs = (
        P(None, AXES),
        P(None, AXES),
        P(None, AXES),
        P(AXES),
        P(None, None, AXES),
        P(),
        P(),
    )
    out_specs = (P(None, AXES), P(None, AXES), P(None, AXES))
    return jax.shard_map(local, mesh=mesh, in_specs=in_specs, out_specs=out_specs, check_vma=False)
```

```python
import functools

import numpy as np

import jax
import jax.numpy as jnp
from jax import lax
from jax.experimental import pallas as pl
from jax.experimental.pallas import tpu as pltpu
from jax.sharding import PartitionSpec as P

SUBSTEPS = 10

loop_diff = 0.35
mix_along = 0.35
mix_vertical = 0.1
cond_rate = 0.1
latent_heat = 1.5
max_speed = 0.8

AXES = ("tile", "crm")
LOG2E = 1.4426950408889634
LN2 = 0.6931471805599453
SUB = 8
LANE = 128
HI = lax.Precision.HIGH
VMEM = pl.BlockSpec(memory_space=pltpu.VMEM)
HBM = pl.BlockSpec(memory_space=pltpu.HBM)


def in_hbm(x):
    return pltpu.with_memory_space_constraint(x, pltpu.HBM)


def up_to(n, m):
    return -(-n // m) * m


def edges(block):
    count = lax.axis_size(AXES)
    forward = [(i, (i + 1) % count) for i in range(count)]
    backward = [(t, s) for s, t in forward]
    low = lax.ppermute(block[:, :, -1:], AXES, forward)
    high = lax.ppermute(block[:, :, :1], AXES, backward)
    return low, high


def ring_mean_operator(levels):
    f = np.eye(levels)
    east = west = f
    above = np.concatenate([f[1:], f[-1:]], axis=0)
    below = np.concatenate([f[:1], f[:-1]], axis=0)
    return (
        f
        + mix_along * (east - 2.0 * f + west)
        + mix_vertical * (above - 2.0 * f + below)
    )


def mean_operators(levels):
    v = ring_mean_operator(levels)
    power = np.eye(levels)
    total = np.zeros((levels, levels))
    for _ in range(SUBSTEPS):
        total = total + power
        power = v @ power
    return power, total / SUBSTEPS


def split(x):
    a = x.astype(jnp.bfloat16)
    return a, (x - a.astype(jnp.float32)).astype(jnp.bfloat16)


def dot(a, b, ca, cb, precision=None):
    return lax.dot_general(
        a, b, (((ca,), (cb,)), ((), ())), precision=precision, preferred_element_type=jnp.float32
    )


def advection(f, v, low, high):
    cols = f.shape[1]
    lane = lax.broadcasted_iota(jnp.int32, f.shape, 1)
    ahead = jnp.where(lane == cols - 1, high, pltpu.roll(f, cols - 1, 1))
    behind = jnp.where(lane == 0, low, pltpu.roll(f, 1, 1))
    return -v * (ahead - behind) * 0.5 + loop_diff * (ahead - 2.0 * f + behind)


def onehot(pos_row, cols):
    place = lax.broadcasted_iota(jnp.int32, (cols, cols), 0)
    return jnp.where(place == pos_row, 1.0, 0.0).astype(jnp.bfloat16)


SLOT = 32
SLOTS = LANE // SLOT


def return_shape(cz, per):
    head = (LANE - 2 * cz) // SUB * SUB
    assert 0 <= head <= cz and cz - head <= SLOT
    return head, per + -(-per // SLOTS)


def slot_onehot(place_row, devices, per, cols):
    row = place_row % per // SLOTS * devices + place_row // per
    rows = -(-per // SLOTS) * devices
    return jnp.where(
        lax.broadcasted_iota(jnp.int32, (rows, cols), 0) == row, 1.0, 0.0
    ).astype(jnp.bfloat16)


CARRIED = (
    (0, 1, 0), (0, 0, 0), (0, 0, 1), (0, 1, 1),
    (1, 0, 0), (1, 1, 0), (1, 0, 1), (1, 1, 1),
)


def row_of(field, half, end):
    return CARRIED.index((field, half, end))


def halves(levels):
    first = up_to(-(-levels // 2), SUB)
    return first, levels - first


def carries(levels, per, width):
    first, second = halves(levels)
    return per >= len(CARRIED) and 3 * levels + first <= width and second < first


def pack_kernel(devices, carry, *refs):
    low_ref, high_ref = (None, None) if carry else refs[4:6]
    out_ref, pos_ref, s_ref, t_ref, q_ref, v_ref, own_ref, sem = refs[-8:]
    copies = [
        pltpu.make_async_copy(source, target, sem.at[n])
        for n, (source, target) in enumerate(zip(refs[:4], (t_ref, q_ref, v_ref, own_ref)))
    ]
    for n in (3, 0, 1, 2):
        copies[n].start()
    nl, cols = t_ref.shape
    width = s_ref.shape[0]
    per = cols // devices
    copies[3].wait()
    own = own_ref[...]
    who = lax.broadcasted_iota(jnp.int32, (devices, cols), 0)
    mine = jnp.where(who == own, 1.0, 0.0)
    before = lax.broadcasted_iota(jnp.int32, (cols, cols), 0) < lax.broadcasted_iota(
        jnp.int32, (cols, cols), 1
    )
    tri = jnp.where(before, 1.0, 0.0).astype(jnp.bfloat16)
    ranks = dot(mine.astype(jnp.bfloat16), tri, 1, 0)
    rank = jnp.sum(ranks * mine, axis=0, keepdims=True)
    pos = own * per + rank.astype(jnp.int32)
    pos_ref[...] = pos
    sel = onehot(pos, cols)

    for n in range(3):
        copies[n].wait()
    t = t_ref[...]
    x = q_ref[...] - 0.5 * t
    v = v_ref[...]
    if carry:
        low = high = jnp.zeros((nl, 1), jnp.float32)
    else:
        low = low_ref[1] - 0.5 * low_ref[0]
        high = high_ref[1] - 0.5 * high_ref[0]
    s_ref[0:nl, :] = x
    s_ref[nl:2 * nl, :] = v
    s_ref[2 * nl:3 * nl, :] = advection(x, v, low, high)
    rest = width - 3 * nl
    if rest:
        s_ref[3 * nl:, :] = jnp.zeros((rest, cols), jnp.float32)
    if carry:
        first, second = halves(nl)
        lane = lax.broadcasted_iota(jnp.int32, (1, cols), 1)
        s_ref[3 * nl + second:3 * nl + second + 1, :] = jnp.where(
            (lane == 0) | (lane == cols - 1), 1.0, 0.0
        )
    a, b = split(s_ref[...])
    out = dot(sel, a, 1, 1) + dot(sel, b, 1, 1)
    if carry:
        fill = jnp.zeros((first - second, cols), jnp.float32)
        parts = []
        for f in (x, t):
            parts += [f[:first], jnp.concatenate([f[first:], fill], axis=0)]
        parts = jnp.concatenate(parts, axis=1)
        shape = (SUB, parts.shape[1])
        want = jnp.full(shape, -1, jnp.int32)
        row = lax.broadcasted_iota(jnp.int32, shape, 0)
        for r, (field, half, end) in enumerate(CARRIED):
            want = jnp.where(row == r, (2 * field + half) * cols + end * (cols - 1), want)
        pick = jnp.where(lax.broadcasted_iota(jnp.int32, shape, 1) == want, 1.0, 0.0).astype(
            jnp.bfloat16
        )
        a, b = split(parts)
        ends = dot(pick, a, 1, 1) + dot(pick, b, 1, 1)
        ends = jnp.concatenate([ends, jnp.zeros((SUB, width - first), jnp.float32)], axis=1)
        ends = pltpu.roll(ends, 3 * nl, 1)
        out = (out.reshape(devices, per, width) + ends[None]).reshape(cols, width)
    out_ref[...] = out


LARGEST = 120.0


def small_softplus2(f):
    return jnp.log2(1.0 + jnp.exp2(f))


def softplus2(f):
    return jnp.maximum(f, jnp.log2(1.0 + jnp.exp2(jnp.minimum(f, 100.0))))


def lanes(k):
    return pl.ds(k * LANE, LANE)


def fold(part_ref, out_ref, k, scale):
    levels = out_ref.shape[0]
    total = part_ref[pl.ds(0, levels, stride=SUB), :]
    for s in range(1, SUB):
        total = total + part_ref[pl.ds(s, levels, stride=SUB), :]
    out_ref[:, lanes(k)] = total * scale


def clear_tail(part_ref, cz):
    for n in range(part_ref.shape[0]):
        for z in range(cz * SUB, part_ref.shape[1], SUB):
            part_ref[n, pl.ds(z, SUB), :] = jnp.zeros((SUB, LANE), jnp.float32)


def prep_kernel(carry, td_ref, down_ref, after_ref, start_ref, mean_ref, g_ref, most_ref,
                raw_ref, part_ref, td_sem):
    del after_ref
    cz, cx, cols = td_ref.shape
    nl = down_ref.shape[1]
    zp = mean_ref.shape[0]
    width = g_ref.shape[1]
    groups = cx // SUB
    tiles = cols // LANE
    chunk = -(-cz // td_sem.shape[1])

    def td_copy(k, c):
        levels = pl.ds(c * chunk, min(chunk, cz - c * chunk))
        return pltpu.make_async_copy(
            td_ref.at[levels, :, lanes(k)], raw_ref.at[k, levels], td_sem.at[k, c]
        )

    for k in range(tiles):
        for c in range(td_sem.shape[1]):
            td_copy(k, c).start()

    down = jnp.concatenate(
        [down_ref[...], jnp.zeros((cz, width - nl), jnp.float32)], axis=1
    )
    down = jnp.concatenate([down, jnp.zeros((zp - cz, width), jnp.float32)], axis=0)
    for n in range(3):
        g_ref[n * zp:(n + 1) * zp, :] = down if n == 0 else pltpu.roll(down, n * nl, 1)
    if carry:
        shape = (g_ref.shape[0] - 3 * zp, width)
        row = lax.broadcasted_iota(jnp.int32, shape, 0)
        to = jnp.where(row < nl, row + nl, row + 2 * nl)
        g_ref[3 * zp:, :] = jnp.where(
            lax.broadcasted_iota(jnp.int32, shape, 1) == to, 1.0, 0.0
        )

    clear_tail(part_ref, cz)
    most = [jnp.zeros((SUB, LANE), jnp.float32)] * groups
    for k in range(tiles):
        for z in range(cz):
            if z % chunk == 0:
                td_copy(k, z // chunk).wait()
            total = None
            for i in range(groups):
                td = raw_ref[k, z, pl.ds(i, SUB, stride=groups), :]
                total = td if total is None else total + td
                first = (-0.5 * LOG2E) * td
                start_ref[k, z, pl.ds(SUB * i, SUB), :] = first
                most[i] = jnp.maximum(most[i], jnp.abs(first))
            part_ref[k, pl.ds(z * SUB, SUB), :] = total
        fold(part_ref.at[k], mean_ref, k, 1.0 / cx)
    most_ref[...] = functools.reduce(jnp.maximum, most)


def cloud_kernel(devices, carry, nl, r_ref, start_ref, td_mean_ref, g_ref, most_ref, mean_ref, after_ref,
                 out_ref, d_ref, base_ref, east_ref, west_ref, force_ref, val_ref, part_ref):
    del after_ref
    tiles, cz, cx, _ = start_ref.shape
    zp, cols = td_mean_ref.shape
    per = cols // devices
    groups = cx // SUB

    prof = dot(g_ref[...], r_ref[...], 1, 1, HI)
    d0 = prof[0:zp]
    speed = max_speed * jnp.tanh(prof[zp:2 * zp])
    fd = prof[2 * zp:3 * zp]
    if carry:
        first, second = halves(nl)
        v = prof[3 * zp:3 * zp + nl]
        ends = prof[3 * zp + nl:3 * zp + nl + first]
        flag = ends[second:second + 1] > 0.5
        place = lax.rem(lax.broadcasted_iota(jnp.int32, (1, cols), 1), per)

        def neighbour(end, at):
            step = per if at == 0 else -per
            shift = lambda half: (step + at - row_of(0, half, end)) % cols
            return jnp.concatenate(
                [pltpu.roll(ends, shift(0), 1), pltpu.roll(ends, shift(1), 1)[:second]], axis=0
            )

        behind = neighbour(1, 0) * (loop_diff + 0.5 * v)
        ahead = neighbour(0, per - 1) * (loop_diff - 0.5 * v)
        halo = jnp.where(flag & (place == 0), behind, 0.0) + jnp.where(
            flag & (place == per - 1), ahead, 0.0
        )
        fd = fd + dot(g_ref[0:zp, 0:nl], halo, 1, 0, HI)
    base_ref[...] = d0 * LOG2E
    east_ref[...] = mix_along - 0.5 * speed
    west_ref[...] = mix_along + 0.5 * speed
    force = fd * (LOG2E / SUBSTEPS)
    force_ref[...] = force
    drain = cond_rate * (1.0 + 0.5 * latent_heat)
    rate = 1.0 - 2.0 * mix_along + max(2.0 * mix_along, max_speed)
    growth = rate**SUBSTEPS
    series = sum(rate**n for n in range(SUBSTEPS))
    bound = growth * (jnp.max(jnp.abs(d0)) * LOG2E + jnp.max(most_ref[...])) + series * (
        jnp.max(jnp.abs(force)) + drain
    )
    val_ref[0:zp, :] = td_mean_ref[...]
    val_ref[zp:2 * zp, :] = d0 - 0.5 * td_mean_ref[...]
    val_ref[2 * zp:3 * zp, :] = fd
    clear_tail(part_ref, cz)

    def row_at(ref, z, k):
        return jnp.broadcast_to(ref[pl.ds(z, 1), lanes(k)], (SUB, LANE))

    slot = [0] + [SUB * (i + 1) for i in range(1, groups)]
    last = slot[-1]

    def get(k, z):
        return [d_ref[k, z, pl.ds(slot[i], SUB), :] for i in range(groups)]

    def put(k, z, i, new):
        d_ref[k, z, pl.ds(slot[i], SUB), :] = new
        if i == 0:
            d_ref[k, z, pl.ds(SUB, SUB), :] = new
        if i == groups - 1:
            d_ref[k, z, pl.ds(last + SUB, SUB), :] = new

    for k in range(tiles):
        for z in range(cz):
            base = row_at(base_ref, z, k)
            for i in range(groups):
                put(k, z, i, base + start_ref[k, z, pl.ds(SUB * i, SUB), :])

    def step(softplus, _, carry):
        for k in range(tiles):
            below = cur = get(k, 0)
            pair = None
            for z in range(cz):
                above = get(k, z + 1) if z + 1 < cz else cur
                if pair is None:
                    pair = [c + a for c, a in zip(cur, above)]
                    column = [p + b for p, b in zip(pair, below)]
                else:
                    column = [p + a for p, a in zip(pair, above)]
                    pair = None
                ea = row_at(east_ref, z, k)
                we = row_at(west_ref, z, k)
                fo = row_at(force_ref, z, k)
                ring = [d_ref[k, z, pl.ds(last + SUB - 1, SUB), :]] + cur
                ring = ring + [d_ref[k, z, pl.ds(1, SUB), :]]
                for i in range(groups):
                    new = (
                        mix_vertical * column[i]
                        + ea * ring[i + 2]
                        + we * ring[i]
                        + fo
                        - drain * softplus(cur[i])
                    )
                    put(k, z, i, new)
                below, cur = cur, above
        return carry

    @pl.when(bound < LARGEST)
    def _():
        lax.fori_loop(0, SUBSTEPS, functools.partial(step, small_softplus2), 0)

    @pl.when(jnp.logical_not(bound < LARGEST))
    def _():
        lax.fori_loop(0, SUBSTEPS, functools.partial(step, softplus2), 0)

    head, rows = return_shape(cz, per)
    cloud_ref = east_ref
    for k in range(tiles):
        for z in range(cz):
            total = cloud = None
            for f in get(k, z):
                c = softplus2(f)
                total = f if total is None else total + f
                cloud = c if cloud is None else cloud + c
            part_ref[2 * k, pl.ds(z * SUB, SUB), :] = total
            part_ref[2 * k + 1, pl.ds(z * SUB, SUB), :] = cloud
        fold(part_ref.at[2 * k], val_ref.at[pl.ds(3 * zp, zp)], k, LN2 / cx)
        fold(part_ref.at[2 * k + 1], cloud_ref, k, LN2 / cx)
        val_ref[4 * zp:, lanes(k)] = cloud_ref[0:head, lanes(k)]
        main = dot(val_ref[:, lanes(k)], mean_ref[...], 0, 0, HI)
        for h in range(LANE // per):
            out_ref[pl.ds((k * (LANE // per) + h) * rows, per), :] = main[h * per:(h + 1) * per]
    left = cloud_ref[head:, :]
    left = jnp.concatenate([left, jnp.zeros((SLOT - left.shape[0], cols), jnp.float32)], axis=0) \
        if left.shape[0] < SLOT else left
    place = lax.broadcasted_iota(jnp.int32, (1, cols), 1)
    part = place % SLOTS
    spread = jnp.concatenate(
        [jnp.where(part == j, left, 0.0) for j in range(SLOTS)], axis=0
    )
    pick = slot_onehot(place, devices, per, cols)
    a, b = split(spread)
    extra = dot(pick, a, 1, 1) + dot(pick, b, 1, 1)
    for i in range(rows - per):
        out_ref[pl.ds(per + i, devices, stride=rows), :] = extra[i * devices:(i + 1) * devices]


def base_kernel(devices, carry, *refs):
    t_ref, q_ref, v_ref, down_ref, up_ref, lin_ref, pos_ref = refs[:7]
    low_ref, high_ref = (None, None) if carry else refs[7:9]
    to_ref, qo_ref, level_ref, rest_ref, sel_ref, pick_ref, gain_ref = refs[-7:]
    nl, cols = t_ref.shape
    cz = up_ref.shape[1]
    per = cols // devices
    head, _ = return_shape(cz, per)
    up = up_ref[...]
    wide = jnp.concatenate([up, jnp.zeros((nl, LANE - cz), jnp.float32)], axis=1)
    lane = lax.broadcasted_iota(jnp.int32, wide.shape, 1)
    level_ref[0:nl, :] = wide
    level_ref[nl:2 * nl, :] = -pltpu.roll(wide, cz, 1)
    level_ref[2 * nl:3 * nl, :] = pltpu.roll(jnp.where(lane < head, wide, 0.0), 2 * cz, 1)
    rest_ref[...] = jnp.where(lane < SLOT, pltpu.roll(wide, LANE - head, 1), 0.0)
    sel_ref[...] = onehot(pos_ref[...], cols)
    pick_ref[...] = slot_onehot(pos_ref[...], devices, per, cols)
    if carry:
        low = high = (jnp.zeros((nl, 1), jnp.float32),) * 2
    else:
        low = (low_ref[0], low_ref[1])
        high = (high_ref[0], high_ref[1])
    v = v_ref[...]
    t = t_ref[...]
    q = q_ref[...]
    advt = advection(t, v, low[0], high[0])
    advq = advection(q, v, low[1], high[1])
    prof = dot(down_ref[...], jnp.concatenate([t, q, advt, advq], axis=1), 1, 0, HI)
    lin = lin_ref[...]
    gain = dot(lin[0], prof[:, :2 * cols], 1, 0, HI) + dot(lin[1], prof[:, 2 * cols:], 1, 0, HI)
    gain = dot(up, gain, 1, 0, HI)
    to_ref[...] = t + advt + gain[:, :cols]
    qo_ref[...] = q + advq + gain[:, cols:]
    gain_ref[...] = dot(up, dot(lin[1], down_ref[...], 1, 0, HI), 1, 0, HI)


def ends_pick():
    pick = np.zeros((2 * SUB, 2 * LANE))
    for r, (field, half, end) in enumerate(CARRIED):
        row = r + (0 if end else SUB)
        place = half * LANE + (0 if end else 1)
        if field:
            pick[row, place] = 1.0
        pick[row, place + 2] = 0.5 if field else 1.0
    return pick


def halo_part(devices, r_ref, ends_ref, v_ref):
    nl, cols = v_ref.shape
    per = cols // devices
    first, second = halves(nl)
    me = lax.axis_index(AXES)

    def block(device):
        start = pl.multiple_of(device * per, SUB)
        return r_ref[pl.ds(start, SUB), :]

    rows = jnp.concatenate(
        [block(lax.rem(me + devices - 1, devices)), block(lax.rem(me + 1, devices))], axis=0
    )
    rows = pltpu.roll(rows, rows.shape[1] - 3 * nl, 1)[:, :LANE]
    a, b = split(rows)
    pick = ends_ref[...]
    part = dot(a, pick, 0, 0) + dot(b, pick, 0, 0)
    ends = jnp.concatenate([part[:first, :LANE], part[:second, LANE:]], axis=0)
    lane = lax.broadcasted_iota(jnp.int32, ends.shape, 1)
    low = v_ref[:, :LANE]
    high = v_ref[:, cols - LANE:]
    v = jnp.where(
        lane == 0, low, jnp.where(lane == 2, pltpu.roll(low, 2, 1), jnp.where(
            lane == 1, -pltpu.roll(high, 2, 1), -pltpu.roll(high, 4, 1)))
    )
    return (loop_diff + 0.5 * v) * ends


def add_ends(field_ref, out_ref, extra, halo, place):
    cols = field_ref.shape[1]
    lane = lax.broadcasted_iota(jnp.int32, halo.shape, 1)
    start = pltpu.roll(halo, LANE - place, 1) if place else halo
    stop = pltpu.roll(halo, LANE - 2 - place, 1)
    parts = [extra[:, k:k + LANE] for k in range(0, cols, LANE)]
    parts[0] = parts[0] + jnp.where(lane == 0, start, 0.0)
    parts[-1] = parts[-1] + jnp.where(lane == LANE - 1, stop, 0.0)
    for k, part in enumerate(parts):
        out_ref[:, lanes(k)] = field_ref[:, lanes(k)] + part


def finish_kernel(devices, carry, *refs):
    r_ref, pos_ref, tb_ref, qb_ref, level_ref, rest_ref, sel_ref, pick_ref = refs[:8]
    gain_ref, r1_ref, v_ref, ends_ref = refs[8:12] if carry else (None,) * 4
    to_ref, qo_ref, co_ref = refs[-3:]
    nl, cols = tb_ref.shape
    per = cols // devices
    rows = r_ref.shape[0] // devices
    if carry:
        halo = halo_part(devices, r1_ref, ends_ref, v_ref)
        halo = halo + dot(gain_ref[...], halo, 1, 0, HI)
    main = jnp.concatenate([r_ref[pl.ds(h * rows, per), :] for h in range(devices)], axis=0)
    extra = jnp.concatenate(
        [r_ref[pl.ds(per + i, devices, stride=rows), :] for i in range(rows - per)], axis=0
    )
    a, b = split(extra)
    extra = dot(a, pick_ref[...], 0, 0) + dot(b, pick_ref[...], 0, 0)
    part = pos_ref[...] % per % SLOTS
    left = jnp.where(part == 0, extra[:SLOT], 0.0)
    for j in range(1, SLOTS):
        left = left + jnp.where(part == j, extra[j * SLOT:(j + 1) * SLOT], 0.0)
    rest = dot(rest_ref[:, 0:SLOT], left, 1, 0, HI)
    a, b = split(dot(level_ref[...], main, 1, 1, HI))
    out = dot(a, sel_ref[...], 1, 0) + dot(b, sel_ref[...], 1, 0)
    if carry:
        add_ends(tb_ref, to_ref, out[0:nl], halo, 0)
        add_ends(qb_ref, qo_ref, out[nl:2 * nl], halo, 2)
    else:
        to_ref[...] = tb_ref[...] + out[0:nl]
        qo_ref[...] = qb_ref[...] + out[nl:2 * nl]
    co_ref[...] = out[2 * nl:3 * nl] + rest


def local(
    thermal_anomaly,
    vapour_anomaly,
    periodic_flow_velocity,
    processor_assignment,
    thermal_disturbance,
    layer_index_downscale,
    layer_index_upscale,
):
    nl, cols = thermal_anomaly.shape
    cz, cx, _ = thermal_disturbance.shape
    devices = lax.axis_size(AXES)
    per = cols // devices
    zp = up_to(cz, SUB)
    f32 = jnp.float32
    width = up_to(3 * nl, LANE)
    head, rows = return_shape(cz, per)
    field = jax.ShapeDtypeStruct((nl, cols), f32)
    carry = carries(nl, per, width)

    fields = (thermal_anomaly, vapour_anomaly, periodic_flow_velocity)
    ends = () if carry else edges(jnp.stack(fields[:2]))
    out, pos = pl.pallas_call(
        functools.partial(pack_kernel, devices, carry),
        out_shape=(
            jax.ShapeDtypeStruct((cols, width), f32),
            jax.ShapeDtypeStruct((1, cols), jnp.int32),
        ),
        in_specs=[HBM] * 4 + [VMEM] * len(ends),
        out_specs=(VMEM,) * 2,
        scratch_shapes=[
            pltpu.VMEM((width, cols), f32),
            pltpu.VMEM((nl, cols), f32),
            pltpu.VMEM((nl, cols), f32),
            pltpu.VMEM((nl, cols), f32),
            pltpu.VMEM((1, cols), jnp.int32),
            pltpu.SemaphoreType.DMA((4,)),
        ],
        compiler_params=pltpu.CompilerParams(vmem_limit_bytes=VMEM_PACK),
        name="pack",
    )(*[in_hbm(f) for f in (*fields, processor_assignment.reshape(1, cols))], *ends)

    def exchange(blocks, *inner):
        shape = blocks.shape
        blocks = blocks.reshape(devices, *inner)
        return lax.all_to_all(blocks, AXES, split_axis=0, concat_axis=0, tiled=True).reshape(shape)

    r1 = exchange(out, per, width)

    power, total = mean_operators(cz)
    release = 1.0 + 0.5 * latent_heat
    mean = np.zeros((4 * zp + head, LANE))
    z_part = np.zeros((4 * zp + head, cz))
    z_part[zp:zp + cz] = power.T / release
    z_part[2 * zp:2 * zp + cz] = total.T / release
    z_part[3 * zp:3 * zp + cz] = -np.eye(cz) / release
    mean[0:cz, 0:cz] = power.T
    mean[:, 0:cz] += latent_heat * z_part
    mean[:, cz:2 * cz] = z_part
    mean[4 * zp:, 2 * cz:2 * cz + head] = np.eye(head)

    tiles = cols // LANE
    groups = cx // SUB
    level_rows = 3 * zp + (nl + halves(nl)[0] if carry else 0)
    prep = pl.pallas_call(
        functools.partial(prep_kernel, carry),
        out_shape=(
            jax.ShapeDtypeStruct((tiles, cz, cx, LANE), f32),
            jax.ShapeDtypeStruct((zp, cols), f32),
            jax.ShapeDtypeStruct((level_rows, width), f32),
            jax.ShapeDtypeStruct((SUB, LANE), f32),
        ),
        in_specs=[HBM, VMEM, VMEM],
        out_specs=(VMEM,) * 4,
        scratch_shapes=[
            pltpu.VMEM((tiles, cz, cx, LANE), f32),
            pltpu.VMEM((tiles, zp * SUB, LANE), f32),
            pltpu.SemaphoreType.DMA((tiles, 5)),
        ],
        compiler_params=pltpu.CompilerParams(vmem_limit_bytes=VMEM_PACK),
        cost_estimate=pl.CostEstimate(flops=10**8, bytes_accessed=4 * 10**6, transcendentals=0),
        name="prep",
    )(in_hbm(thermal_disturbance), layer_index_downscale, pos)
    lin = np.stack([power - np.eye(cz), total])
    *base, gain = pl.pallas_call(
        functools.partial(base_kernel, devices, carry),
        out_shape=(
            field,
            field,
            jax.ShapeDtypeStruct((3 * nl, LANE), f32),
            jax.ShapeDtypeStruct((nl, LANE), f32),
            jax.ShapeDtypeStruct((cols, cols), jnp.bfloat16),
            jax.ShapeDtypeStruct((devices * (rows - per), cols), jnp.bfloat16),
            jax.ShapeDtypeStruct((nl, nl), f32),
        ),
        in_specs=[VMEM] * (7 + len(ends)),
        out_specs=(VMEM,) * 7,
        compiler_params=pltpu.CompilerParams(vmem_limit_bytes=VMEM_PACK),
        cost_estimate=pl.CostEstimate(flops=10**8, bytes_accessed=10**6, transcendentals=0),
        name="base",
    )(*fields, layer_index_downscale, layer_index_upscale, jnp.asarray(lin, f32), pos, *ends)
    vals = pl.pallas_call(
        functools.partial(cloud_kernel, devices, carry, nl),
        out_shape=jax.ShapeDtypeStruct((devices * rows, LANE), f32),
        in_specs=[VMEM] * 7,
        out_specs=VMEM,
        scratch_shapes=[
            pltpu.VMEM((tiles, cz, SUB * (groups + 2), LANE), f32),
            pltpu.VMEM((zp, cols), f32),
            pltpu.VMEM((zp, cols), f32),
            pltpu.VMEM((zp, cols), f32),
            pltpu.VMEM((zp, cols), f32),
            pltpu.VMEM((4 * zp + head, cols), f32),
            pltpu.VMEM((2 * tiles, zp * SUB, LANE), f32),
        ],
        compiler_params=pltpu.CompilerParams(vmem_limit_bytes=VMEM_CLOUD),
        name="cloud",
    )(r1, *prep, jnp.asarray(mean, f32), gain)
    r2 = exchange(vals, 1, rows * LANE)
    halo = ()
    if carry:
        halo = (gain, r1, periodic_flow_velocity, jnp.asarray(ends_pick(), jnp.bfloat16))
    return pl.pallas_call(
        functools.partial(finish_kernel, devices, carry),
        out_shape=(field,) * 3,
        in_specs=[VMEM] * (8 + len(halo)),
        out_specs=(VMEM,) * 3,
        compiler_params=pltpu.CompilerParams(vmem_limit_bytes=VMEM_PACK),
        name="finish",
    )(r2, pos, *base, *halo)


VMEM_PACK = 16 * 2**20
VMEM_CLOUD = 24 * 2**20


def solution(mesh):
    in_specs = (
        P(None, AXES),
        P(None, AXES),
        P(None, AXES),
        P(AXES),
        P(None, None, AXES),
        P(),
        P(),
    )
    out_specs = (P(None, AXES), P(None, AXES), P(None, AXES))
    return jax.shard_map(local, mesh=mesh, in_specs=in_specs, out_specs=out_specs, check_vma=False)
```

```python
import functools

import numpy as np

import jax
import jax.numpy as jnp
from jax import lax
from jax.experimental import pallas as pl
from jax.experimental.pallas import tpu as pltpu
from jax.sharding import PartitionSpec as P

SUBSTEPS = 10

loop_diff = 0.35
mix_along = 0.35
mix_vertical = 0.1
cond_rate = 0.1
latent_heat = 1.5
max_speed = 0.8

AXES = ("tile", "crm")
LOG2E = 1.4426950408889634
LN2 = 0.6931471805599453
SUB = 8
LANE = 128
HI = lax.Precision.HIGH
VMEM = pl.BlockSpec(memory_space=pltpu.VMEM)
HBM = pl.BlockSpec(memory_space=pltpu.HBM)


def in_hbm(x):
    return pltpu.with_memory_space_constraint(x, pltpu.HBM)


def up_to(n, m):
    return -(-n // m) * m


def edges(block):
    count = lax.axis_size(AXES)
    forward = [(i, (i + 1) % count) for i in range(count)]
    backward = [(t, s) for s, t in forward]
    low = lax.ppermute(block[:, :, -1:], AXES, forward)
    high = lax.ppermute(block[:, :, :1], AXES, backward)
    return low, high


def ring_mean_operator(levels):
    f = np.eye(levels)
    east = west = f
    above = np.concatenate([f[1:], f[-1:]], axis=0)
    below = np.concatenate([f[:1], f[:-1]], axis=0)
    return (
        f
        + mix_along * (east - 2.0 * f + west)
        + mix_vertical * (above - 2.0 * f + below)
    )


def mean_operators(levels):
    v = ring_mean_operator(levels)
    power = np.eye(levels)
    total = np.zeros((levels, levels))
    for _ in range(SUBSTEPS):
        total = total + power
        power = v @ power
    return power, total / SUBSTEPS


def shift_operators(levels):
    drain = cond_rate * (1.0 + 0.5 * latent_heat)
    rest = (1.0 + drain) * np.eye(levels) - ring_mean_operator(levels)
    scale = LOG2E / SUBSTEPS
    return -np.linalg.inv(rest) * scale, -rest / scale


def halved(x):
    a = np.asarray(x, jnp.bfloat16)
    b = np.asarray(x - a.astype(np.float64), jnp.bfloat16)
    return jnp.asarray(a), jnp.asarray(b)


def split(x):
    a = x.astype(jnp.bfloat16)
    return a, (x - a.astype(jnp.float32)).astype(jnp.bfloat16)


def dot3(a, b, ca, cb):
    return dot(a[0], b[0], ca, cb) + dot(a[0], b[1], ca, cb) + dot(a[1], b[0], ca, cb)


def dot(a, b, ca, cb, precision=None):
    return lax.dot_general(
        a, b, (((ca,), (cb,)), ((), ())), precision=precision, preferred_element_type=jnp.float32
    )


def advection(f, v, low, high):
    cols = f.shape[1]
    lane = lax.broadcasted_iota(jnp.int32, f.shape, 1)
    ahead = jnp.where(lane == cols - 1, high, pltpu.roll(f, cols - 1, 1))
    behind = jnp.where(lane == 0, low, pltpu.roll(f, 1, 1))
    return -v * (ahead - behind) * 0.5 + loop_diff * (ahead - 2.0 * f + behind)


def onehot(pos_row, cols):
    place = lax.broadcasted_iota(jnp.int32, (cols, cols), 0)
    return jnp.where(place == pos_row, 1.0, 0.0).astype(jnp.bfloat16)


SLOT = 32
SLOTS = LANE // SLOT


def return_shape(cz, per):
    head = (LANE - 2 * cz) // SUB * SUB
    assert 0 <= head <= cz and cz - head <= SLOT
    return head, per + -(-per // SLOTS)


def slot_onehot(place_row, devices, per, cols):
    row = place_row % per // SLOTS * devices + place_row // per
    rows = -(-per // SLOTS) * devices
    return jnp.where(
        lax.broadcasted_iota(jnp.int32, (rows, cols), 0) == row, 1.0, 0.0
    ).astype(jnp.bfloat16)


CARRIED = (
    (0, 1, 0), (0, 0, 0), (0, 0, 1), (0, 1, 1),
    (1, 0, 0), (1, 1, 0), (1, 0, 1), (1, 1, 1),
)


def row_of(field, half, end):
    return CARRIED.index((field, half, end))


def halves(levels):
    first = up_to(-(-levels // 2), SUB)
    return first, levels - first


def carries(levels, per, width):
    first, second = halves(levels)
    return per >= len(CARRIED) and 3 * levels + first <= width and second < first


def pack_kernel(devices, carry, *refs):
    low_ref, high_ref = (None, None) if carry else refs[4:6]
    out_ref, pos_ref, s_ref, t_ref, q_ref, v_ref, own_ref, sem = refs[-8:]
    copies = [
        pltpu.make_async_copy(source, target, sem.at[n])
        for n, (source, target) in enumerate(zip(refs[:4], (t_ref, q_ref, v_ref, own_ref)))
    ]
    for n in (3, 0, 1, 2):
        copies[n].start()
    nl, cols = t_ref.shape
    width = s_ref.shape[0]
    per = cols // devices
    copies[3].wait()
    own = own_ref[...]
    who = lax.broadcasted_iota(jnp.int32, (devices, cols), 0)
    mine = jnp.where(who == own, 1.0, 0.0)
    before = lax.broadcasted_iota(jnp.int32, (cols, cols), 0) < lax.broadcasted_iota(
        jnp.int32, (cols, cols), 1
    )
    tri = jnp.where(before, 1.0, 0.0).astype(jnp.bfloat16)
    ranks = dot(mine.astype(jnp.bfloat16), tri, 1, 0)
    rank = jnp.sum(ranks * mine, axis=0, keepdims=True)
    pos = own * per + rank.astype(jnp.int32)
    pos_ref[...] = pos
    sel = onehot(pos, cols)

    for n in range(3):
        copies[n].wait()
    t = t_ref[...]
    x = q_ref[...] - 0.5 * t
    v = v_ref[...]
    if carry:
        low = high = jnp.zeros((nl, 1), jnp.float32)
    else:
        low = low_ref[1] - 0.5 * low_ref[0]
        high = high_ref[1] - 0.5 * high_ref[0]
    s_ref[0:nl, :] = x
    s_ref[nl:2 * nl, :] = v
    s_ref[2 * nl:3 * nl, :] = advection(x, v, low, high)
    rest = width - 3 * nl
    if rest:
        s_ref[3 * nl:, :] = jnp.zeros((rest, cols), jnp.float32)
    if carry:
        first, second = halves(nl)
        lane = lax.broadcasted_iota(jnp.int32, (1, cols), 1)
        s_ref[3 * nl + second:3 * nl + second + 1, :] = jnp.where(
            (lane == 0) | (lane == cols - 1), 1.0, 0.0
        )
    a, b = split(s_ref[...])
    out = dot(sel, a, 1, 1) + dot(sel, b, 1, 1)
    if carry:
        fill = jnp.zeros((first - second, cols), jnp.float32)
        parts = []
        for f in (x, t):
            parts += [f[:first], jnp.concatenate([f[first:], fill], axis=0)]
        parts = jnp.concatenate(parts, axis=1)
        shape = (SUB, parts.shape[1])
        want = jnp.full(shape, -1, jnp.int32)
        row = lax.broadcasted_iota(jnp.int32, shape, 0)
        for r, (field, half, end) in enumerate(CARRIED):
            want = jnp.where(row == r, (2 * field + half) * cols + end * (cols - 1), want)
        pick = jnp.where(lax.broadcasted_iota(jnp.int32, shape, 1) == want, 1.0, 0.0).astype(
            jnp.bfloat16
        )
        a, b = split(parts)
        ends = dot(pick, a, 1, 1) + dot(pick, b, 1, 1)
        ends = jnp.concatenate([ends, jnp.zeros((SUB, width - first), jnp.float32)], axis=1)
        ends = pltpu.roll(ends, 3 * nl, 1)
        out = (out.reshape(devices, per, width) + ends[None]).reshape(cols, width)
    out_ref[...] = out


LARGEST = 120.0


def moved_softplus2(small, g, move):
    if small:
        return jnp.log2(move + jnp.exp2(g))
    return move + softplus2(g - move)


def softplus2(f):
    return jnp.maximum(f, jnp.log2(1.0 + jnp.exp2(jnp.minimum(f, 100.0))))


def lanes(k):
    return pl.ds(k * LANE, LANE)


def fold(part_ref, out_ref, k, scale):
    levels = out_ref.shape[0]
    total = part_ref[pl.ds(0, levels, stride=SUB), :]
    for s in range(1, SUB):
        total = total + part_ref[pl.ds(s, levels, stride=SUB), :]
    out_ref[:, lanes(k)] = total * scale


def clear_tail(part_ref, cz):
    for n in range(part_ref.shape[0]):
        for z in range(cz * SUB, part_ref.shape[1], SUB):
            part_ref[n, pl.ds(z, SUB), :] = jnp.zeros((SUB, LANE), jnp.float32)


def prep_kernel(carry, td_ref, down_ref, shift_ref, after_ref, start_ref, mean_ref, most_ref,
                high_ref, low_ref, shift_high_ref, shift_low_ref, raw_ref, part_ref, td_sem):
    del after_ref
    cz, cx, cols = td_ref.shape
    nl = down_ref.shape[1]
    zp = mean_ref.shape[0]
    width = high_ref.shape[1]
    groups = cx // SUB
    tiles = cols // LANE
    chunk = -(-cz // td_sem.shape[1])

    def td_copy(k, c):
        levels = pl.ds(c * chunk, min(chunk, cz - c * chunk))
        return pltpu.make_async_copy(
            td_ref.at[levels, :, lanes(k)], raw_ref.at[k, levels], td_sem.at[k, c]
        )

    for k in range(tiles):
        for c in range(td_sem.shape[1]):
            td_copy(k, c).start()

    def wide(rows):
        rows = jnp.concatenate(
            [rows, jnp.zeros((rows.shape[0], width - nl), jnp.float32)], axis=1
        )
        return jnp.concatenate([rows, jnp.zeros((zp - cz, width), jnp.float32)], axis=0)

    down = wide(down_ref[...])
    shift = wide(dot(shift_ref[...], down_ref[...], 1, 0, lax.Precision.HIGHEST))
    blocks = jnp.concatenate(
        [down, pltpu.roll(down, nl, 1), pltpu.roll(shift, 2 * nl, 1)], axis=0
    )
    a, low_ref[...] = split(blocks)
    offset = high_ref.shape[0] - 3 * zp
    if carry:
        shape = (offset, width)
        row = lax.broadcasted_iota(jnp.int32, shape, 0)
        to = jnp.where(row < nl, row + nl, row + 2 * nl)
        high_ref[0:offset, :] = jnp.where(
            lax.broadcasted_iota(jnp.int32, shape, 1) == to, 1.0, 0.0
        ).astype(jnp.bfloat16)
    high_ref[offset:, :] = a
    shift_high_ref[...], shift_low_ref[...] = split(shift[:, :nl])

    clear_tail(part_ref, cz)
    most = [jnp.zeros((SUB, LANE), jnp.float32)] * groups
    for k in range(tiles):
        for z in range(cz):
            if z % chunk == 0:
                td_copy(k, z // chunk).wait()
            total = None
            for i in range(groups):
                td = raw_ref[k, z, pl.ds(i, SUB, stride=groups), :]
                total = td if total is None else total + td
                first = (-0.5 * LOG2E) * td
                start_ref[k, z, pl.ds(SUB * i, SUB), :] = first
                most[i] = jnp.maximum(most[i], jnp.abs(first))
            part_ref[k, pl.ds(z * SUB, SUB), :] = total
        fold(part_ref.at[k], mean_ref, k, 1.0 / cx)
    most_ref[...] = functools.reduce(jnp.maximum, most)


def cloud_kernel(devices, carry, nl, r_ref, start_ref, td_mean_ref, most_ref, g_high_ref, g_low_ref,
                 shift_high_ref, shift_low_ref, mean_high_ref, mean_low_ref, after_ref, *refs):
    gain_ref, v_ref, ends_ref = (after_ref, *refs[:2]) if carry else (None,) * 3
    out_ref, halo_ref = refs[2:4] if carry else (refs[0], None)
    d_ref, base_ref, east_ref, west_ref, shift_ref, scale_ref, val_ref, part_ref = refs[-8:]
    tiles, cz, cx, _ = start_ref.shape
    zp, cols = td_mean_ref.shape
    per = cols // devices
    groups = cx // SUB

    r = split(r_ref[...])
    offset = g_high_ref.shape[0] - 3 * zp
    prof = dot(g_high_ref[...], r[0], 1, 1) + dot(g_high_ref[...], r[1], 1, 1)
    fine = dot(g_low_ref[...], r[0], 1, 1)
    shift = prof[offset + 2 * zp:] + fine[2 * zp:]
    if carry:
        first, second = halves(nl)
        v = prof[0:nl]
        ends = prof[nl:offset]
        flag = ends[second:second + 1] > 0.5
        place = lax.rem(lax.broadcasted_iota(jnp.int32, (1, cols), 1), per)

        def neighbour(end, at):
            step = per if at == 0 else -per
            shift = lambda half: (step + at - row_of(0, half, end)) % cols
            return jnp.concatenate(
                [pltpu.roll(ends, shift(0), 1), pltpu.roll(ends, shift(1), 1)[:second]], axis=0
            )

        behind = neighbour(1, 0) * (loop_diff + 0.5 * v)
        ahead = neighbour(0, per - 1) * (loop_diff - 0.5 * v)
        halo = jnp.where(flag & (place == 0), behind, 0.0) + jnp.where(
            flag & (place == per - 1), ahead, 0.0
        )
        shift = shift + dot3((shift_high_ref[...], shift_low_ref[...]), split(halo), 1, 0)
    d0 = prof[offset:offset + zp] + fine[0:zp]
    speed = max_speed * jnp.tanh(prof[offset + zp:offset + 2 * zp] + fine[zp:2 * zp])
    base = d0 * LOG2E + shift
    base_ref[...] = base
    east_ref[...] = mix_along - 0.5 * speed
    west_ref[...] = mix_along + 0.5 * speed
    shift_ref[...] = shift
    scale_ref[...] = jnp.exp2(shift)
    drain = cond_rate * (1.0 + 0.5 * latent_heat)
    rate = 1.0 - 2.0 * mix_along + max(2.0 * mix_along, max_speed)
    growth = rate**SUBSTEPS
    series = sum(rate**n for n in range(SUBSTEPS))
    bound = growth * (jnp.max(jnp.abs(base)) + jnp.max(most_ref[...])) + series * drain * (
        jnp.max(jnp.abs(shift)) + 1.0
    )
    val_ref[0:zp, :] = td_mean_ref[...]
    val_ref[zp:2 * zp, :] = d0 - 0.5 * td_mean_ref[...]
    val_ref[2 * zp:3 * zp, :] = shift
    clear_tail(part_ref, cz)

    def row_at(ref, z, k):
        return jnp.broadcast_to(ref[pl.ds(z, 1), lanes(k)], (SUB, LANE))

    slot = [0] + [SUB * (i + 1) for i in range(1, groups)]
    last = slot[-1]

    def get(k, z):
        return [d_ref[k, z, pl.ds(slot[i], SUB), :] for i in range(groups)]

    def put(k, z, i, new):
        d_ref[k, z, pl.ds(slot[i], SUB), :] = new
        if i == 0:
            d_ref[k, z, pl.ds(SUB, SUB), :] = new
        if i == groups - 1:
            d_ref[k, z, pl.ds(last + SUB, SUB), :] = new

    for k in range(tiles):
        for z in range(cz):
            base = row_at(base_ref, z, k)
            for i in range(groups):
                put(k, z, i, base + start_ref[k, z, pl.ds(SUB * i, SUB), :])

    def step(small, _, carry):
        for k in range(tiles):
            below = cur = get(k, 0)
            pair = None
            for z in range(cz):
                above = get(k, z + 1) if z + 1 < cz else cur
                if pair is None:
                    pair = [c + a for c, a in zip(cur, above)]
                    column = [p + b for p, b in zip(pair, below)]
                else:
                    column = [p + a for p, a in zip(pair, above)]
                    pair = None
                ea = row_at(east_ref, z, k)
                we = row_at(west_ref, z, k)
                move = row_at(scale_ref if small else shift_ref, z, k)
                ring = [d_ref[k, z, pl.ds(last + SUB - 1, SUB), :]] + cur
                ring = ring + [d_ref[k, z, pl.ds(1, SUB), :]]
                for i in range(groups):
                    new = (
                        mix_vertical * column[i]
                        + ea * ring[i + 2]
                        + we * ring[i]
                        - drain * moved_softplus2(small, cur[i], move)
                    )
                    put(k, z, i, new)
                below, cur = cur, above
        return carry

    @pl.when(bound < LARGEST)
    def _():
        lax.fori_loop(0, SUBSTEPS, functools.partial(step, True), 0)

    @pl.when(jnp.logical_not(bound < LARGEST))
    def _():
        lax.fori_loop(0, SUBSTEPS, functools.partial(step, False), 0)

    if carry:
        halo = halo_part(devices, r_ref, ends_ref, v_ref)
        halo_ref[...] = halo + dot(gain_ref[...], halo, 1, 0, HI)

    head, rows = return_shape(cz, per)
    cloud_ref = east_ref
    for k in range(tiles):
        for z in range(cz):
            total = cloud = None
            move = row_at(shift_ref, z, k)
            for f in get(k, z):
                f = f - move
                c = softplus2(f)
                total = f if total is None else total + f
                cloud = c if cloud is None else cloud + c
            part_ref[2 * k, pl.ds(z * SUB, SUB), :] = total
            part_ref[2 * k + 1, pl.ds(z * SUB, SUB), :] = cloud
        fold(part_ref.at[2 * k], val_ref.at[pl.ds(3 * zp, zp)], k, LN2 / cx)
        fold(part_ref.at[2 * k + 1], cloud_ref, k, LN2 / cx)
        val_ref[4 * zp:, lanes(k)] = cloud_ref[0:head, lanes(k)]
        main = dot3(split(val_ref[:, lanes(k)]), (mean_high_ref[...], mean_low_ref[...]), 0, 0)
        for h in range(LANE // per):
            out_ref[pl.ds((k * (LANE // per) + h) * rows, per), :] = main[h * per:(h + 1) * per]
    left = cloud_ref[head:, :]
    left = jnp.concatenate([left, jnp.zeros((SLOT - left.shape[0], cols), jnp.float32)], axis=0) \
        if left.shape[0] < SLOT else left
    place = lax.broadcasted_iota(jnp.int32, (1, cols), 1)
    part = place % SLOTS
    spread = jnp.concatenate(
        [jnp.where(part == j, left, 0.0) for j in range(SLOTS)], axis=0
    )
    pick = slot_onehot(place, devices, per, cols)
    a, b = split(spread)
    extra = dot(pick, a, 1, 1) + dot(pick, b, 1, 1)
    for i in range(rows - per):
        out_ref[pl.ds(per + i, devices, stride=rows), :] = extra[i * devices:(i + 1) * devices]


def base_kernel(devices, carry, *refs):
    t_ref, q_ref, v_ref, down_ref, up_ref, lin_ref, pos_ref = refs[:7]
    low_ref, high_ref = (None, None) if carry else refs[7:9]
    to_ref, qo_ref, level_high_ref, level_low_ref, rest_high_ref, rest_low_ref = refs[-9:-3]
    sel_ref, pick_ref, gain_ref = refs[-3:]
    nl, cols = t_ref.shape
    cz = up_ref.shape[1]
    per = cols // devices
    head, _ = return_shape(cz, per)
    up = up_ref[...]
    wide = jnp.concatenate([up, jnp.zeros((nl, LANE - cz), jnp.float32)], axis=1)
    lane = lax.broadcasted_iota(jnp.int32, wide.shape, 1)
    level = jnp.concatenate(
        [
            wide,
            -pltpu.roll(wide, cz, 1),
            pltpu.roll(jnp.where(lane < head, wide, 0.0), 2 * cz, 1),
        ],
        axis=0,
    )
    level_high_ref[...], level_low_ref[...] = split(level)
    rest = jnp.where(lane < SLOT, pltpu.roll(wide, LANE - head, 1), 0.0)
    rest_high_ref[...], rest_low_ref[...] = split(rest[:, 0:SLOT])
    sel_ref[...] = onehot(pos_ref[...], cols)
    pick_ref[...] = slot_onehot(pos_ref[...], devices, per, cols)
    if carry:
        low = high = (jnp.zeros((nl, 1), jnp.float32),) * 2
    else:
        low = (low_ref[0], low_ref[1])
        high = (high_ref[0], high_ref[1])
    v = v_ref[...]
    t = t_ref[...]
    q = q_ref[...]
    advt = advection(t, v, low[0], high[0])
    advq = advection(q, v, low[1], high[1])
    prof = dot(down_ref[...], jnp.concatenate([t, q, advt, advq], axis=1), 1, 0, HI)
    lin = lin_ref[...]
    gain = dot(lin[0], prof[:, :2 * cols], 1, 0, HI) + dot(lin[1], prof[:, 2 * cols:], 1, 0, HI)
    gain = dot(up, gain, 1, 0, HI)
    to_ref[...] = t + advt + gain[:, :cols]
    qo_ref[...] = q + advq + gain[:, cols:]
    gain_ref[...] = dot(up, dot(lin[1], down_ref[...], 1, 0, HI), 1, 0, HI)


def ends_pick():
    pick = np.zeros((2 * SUB, 2 * LANE))
    for r, (field, half, end) in enumerate(CARRIED):
        row = r + (0 if end else SUB)
        place = half * LANE + (0 if end else 1)
        if field:
            pick[row, place] = 1.0
        pick[row, place + 2] = 0.5 if field else 1.0
    return pick


def halo_part(devices, r_ref, ends_ref, v_ref):
    nl, cols = v_ref.shape
    per = cols // devices
    first, second = halves(nl)
    me = lax.axis_index(AXES)

    def block(device):
        start = pl.multiple_of(device * per, SUB)
        return r_ref[pl.ds(start, SUB), :]

    rows = jnp.concatenate(
        [block(lax.rem(me + devices - 1, devices)), block(lax.rem(me + 1, devices))], axis=0
    )
    rows = pltpu.roll(rows, rows.shape[1] - 3 * nl, 1)[:, :LANE]
    a, b = split(rows)
    pick = ends_ref[...]
    part = dot(a, pick, 0, 0) + dot(b, pick, 0, 0)
    ends = jnp.concatenate([part[:first, :LANE], part[:second, LANE:]], axis=0)
    lane = lax.broadcasted_iota(jnp.int32, ends.shape, 1)
    low = v_ref[:, :LANE]
    high = v_ref[:, cols - LANE:]
    v = jnp.where(
        lane == 0, low, jnp.where(lane == 2, pltpu.roll(low, 2, 1), jnp.where(
            lane == 1, -pltpu.roll(high, 2, 1), -pltpu.roll(high, 4, 1)))
    )
    return (loop_diff + 0.5 * v) * ends


def add_ends(field_ref, out_ref, extra, halo, place):
    cols = field_ref.shape[1]
    lane = lax.broadcasted_iota(jnp.int32, halo.shape, 1)
    start = pltpu.roll(halo, LANE - place, 1) if place else halo
    stop = pltpu.roll(halo, LANE - 2 - place, 1)
    parts = [extra[:, k:k + LANE] for k in range(0, cols, LANE)]
    parts[0] = parts[0] + jnp.where(lane == 0, start, 0.0)
    parts[-1] = parts[-1] + jnp.where(lane == LANE - 1, stop, 0.0)
    for k, part in enumerate(parts):
        out_ref[:, lanes(k)] = field_ref[:, lanes(k)] + part


def finish_kernel(devices, carry, *refs):
    r_ref, pos_ref, tb_ref, qb_ref = refs[:4]
    level_high_ref, level_low_ref, rest_high_ref, rest_low_ref, sel_ref, pick_ref = refs[4:10]
    to_ref, qo_ref, co_ref = refs[-3:]
    nl, cols = tb_ref.shape
    per = cols // devices
    rows = r_ref.shape[0] // devices
    main = jnp.concatenate([r_ref[pl.ds(h * rows, per), :] for h in range(devices)], axis=0)
    extra = jnp.concatenate(
        [r_ref[pl.ds(per + i, devices, stride=rows), :] for i in range(rows - per)], axis=0
    )
    a, b = split(extra)
    extra = dot(a, pick_ref[...], 0, 0) + dot(b, pick_ref[...], 0, 0)
    part = pos_ref[...] % per % SLOTS
    left = jnp.where(part == 0, extra[:SLOT], 0.0)
    for j in range(1, SLOTS):
        left = left + jnp.where(part == j, extra[j * SLOT:(j + 1) * SLOT], 0.0)
    rest = dot3((rest_high_ref[...], rest_low_ref[...]), split(left), 1, 0)
    a, b = split(dot3((level_high_ref[...], level_low_ref[...]), split(main), 1, 1))
    out = dot(a, sel_ref[...], 1, 0) + dot(b, sel_ref[...], 1, 0)
    if carry:
        halo = refs[10][...]
        add_ends(tb_ref, to_ref, out[0:nl], halo, 0)
        add_ends(qb_ref, qo_ref, out[nl:2 * nl], halo, 2)
    else:
        to_ref[...] = tb_ref[...] + out[0:nl]
        qo_ref[...] = qb_ref[...] + out[nl:2 * nl]
    co_ref[...] = out[2 * nl:3 * nl] + rest


def local(
    thermal_anomaly,
    vapour_anomaly,
    periodic_flow_velocity,
    processor_assignment,
    thermal_disturbance,
    layer_index_downscale,
    layer_index_upscale,
):
    nl, cols = thermal_anomaly.shape
    cz, cx, _ = thermal_disturbance.shape
    devices = lax.axis_size(AXES)
    per = cols // devices
    zp = up_to(cz, SUB)
    f32 = jnp.float32
    width = up_to(3 * nl, LANE)
    head, rows = return_shape(cz, per)
    field = jax.ShapeDtypeStruct((nl, cols), f32)
    carry = carries(nl, per, width)

    fields = (thermal_anomaly, vapour_anomaly, periodic_flow_velocity)
    ends = () if carry else edges(jnp.stack(fields[:2]))
    out, pos = pl.pallas_call(
        functools.partial(pack_kernel, devices, carry),
        out_shape=(
            jax.ShapeDtypeStruct((cols, width), f32),
            jax.ShapeDtypeStruct((1, cols), jnp.int32),
        ),
        in_specs=[HBM] * 4 + [VMEM] * len(ends),
        out_specs=(VMEM,) * 2,
        scratch_shapes=[
            pltpu.VMEM((width, cols), f32),
            pltpu.VMEM((nl, cols), f32),
            pltpu.VMEM((nl, cols), f32),
            pltpu.VMEM((nl, cols), f32),
            pltpu.VMEM((1, cols), jnp.int32),
            pltpu.SemaphoreType.DMA((4,)),
        ],
        compiler_params=pltpu.CompilerParams(vmem_limit_bytes=VMEM_PACK),
        name="pack",
    )(*[in_hbm(f) for f in (*fields, processor_assignment.reshape(1, cols))], *ends)

    def exchange(blocks, *inner):
        shape = blocks.shape
        blocks = blocks.reshape(devices, *inner)
        return lax.all_to_all(blocks, AXES, split_axis=0, concat_axis=0, tiled=True).reshape(shape)

    r1 = exchange(out, per, width)

    power, total = mean_operators(cz)
    release = 1.0 + 0.5 * latent_heat
    shift, unshift = shift_operators(cz)
    mean = np.zeros((4 * zp + head, LANE))
    z_part = np.zeros((4 * zp + head, cz))
    z_part[zp:zp + cz] = power.T / release
    z_part[2 * zp:2 * zp + cz] = (total @ unshift).T / release
    z_part[3 * zp:3 * zp + cz] = -np.eye(cz) / release
    mean[0:cz, 0:cz] = power.T
    mean[:, 0:cz] += latent_heat * z_part
    mean[:, cz:2 * cz] = z_part
    mean[4 * zp:, 2 * cz:2 * cz + head] = np.eye(head)

    tiles = cols // LANE
    groups = cx // SUB
    level_rows = 3 * zp + (nl + halves(nl)[0] if carry else 0)
    bf16 = jnp.bfloat16
    prep = pl.pallas_call(
        functools.partial(prep_kernel, carry),
        out_shape=(
            jax.ShapeDtypeStruct((tiles, cz, cx, LANE), f32),
            jax.ShapeDtypeStruct((zp, cols), f32),
            jax.ShapeDtypeStruct((SUB, LANE), f32),
            jax.ShapeDtypeStruct((level_rows, width), bf16),
            jax.ShapeDtypeStruct((3 * zp, width), bf16),
            jax.ShapeDtypeStruct((zp, nl), bf16),
            jax.ShapeDtypeStruct((zp, nl), bf16),
        ),
        in_specs=[HBM, VMEM, VMEM, VMEM],
        out_specs=(VMEM,) * 7,
        scratch_shapes=[
            pltpu.VMEM((tiles, cz, cx, LANE), f32),
            pltpu.VMEM((tiles, zp * SUB, LANE), f32),
            pltpu.SemaphoreType.DMA((tiles, 5)),
        ],
        compiler_params=pltpu.CompilerParams(vmem_limit_bytes=VMEM_PACK),
        cost_estimate=pl.CostEstimate(flops=10**8, bytes_accessed=4 * 10**6, transcendentals=0),
        name="prep",
    )(in_hbm(thermal_disturbance), layer_index_downscale, jnp.asarray(shift, f32), pos)
    lin = np.stack([power - np.eye(cz), total])
    *base, gain = pl.pallas_call(
        functools.partial(base_kernel, devices, carry),
        out_shape=(
            field,
            field,
            jax.ShapeDtypeStruct((3 * nl, LANE), bf16),
            jax.ShapeDtypeStruct((3 * nl, LANE), bf16),
            jax.ShapeDtypeStruct((nl, SLOT), bf16),
            jax.ShapeDtypeStruct((nl, SLOT), bf16),
            jax.ShapeDtypeStruct((cols, cols), bf16),
            jax.ShapeDtypeStruct((devices * (rows - per), cols), bf16),
            jax.ShapeDtypeStruct((nl, nl), f32),
        ),
        in_specs=[VMEM] * (7 + len(ends)),
        out_specs=(VMEM,) * 9,
        compiler_params=pltpu.CompilerParams(vmem_limit_bytes=VMEM_PACK),
        cost_estimate=pl.CostEstimate(flops=10**8, bytes_accessed=10**6, transcendentals=0),
        name="base",
    )(*fields, layer_index_downscale, layer_index_upscale, jnp.asarray(lin, f32), pos, *ends)
    halo = (periodic_flow_velocity, jnp.asarray(ends_pick(), bf16)) if carry else ()
    vals, *halo = pl.pallas_call(
        functools.partial(cloud_kernel, devices, carry, nl),
        out_shape=(jax.ShapeDtypeStruct((devices * rows, LANE), f32),)
        + ((jax.ShapeDtypeStruct((nl, LANE), f32),) if carry else ()),
        in_specs=[VMEM] * (11 + len(halo)),
        out_specs=(VMEM,) * (2 if carry else 1),
        scratch_shapes=[
            pltpu.VMEM((tiles, cz, SUB * (groups + 2), LANE), f32),
            pltpu.VMEM((zp, cols), f32),
            pltpu.VMEM((zp, cols), f32),
            pltpu.VMEM((zp, cols), f32),
            pltpu.VMEM((zp, cols), f32),
            pltpu.VMEM((zp, cols), f32),
            pltpu.VMEM((4 * zp + head, cols), f32),
            pltpu.VMEM((2 * tiles, zp * SUB, LANE), f32),
        ],
        compiler_params=pltpu.CompilerParams(vmem_limit_bytes=VMEM_CLOUD),
        name="cloud",
    )(r1, *prep, *halved(mean), gain, *halo)
    r2 = exchange(vals, 1, rows * LANE)
    return pl.pallas_call(
        functools.partial(finish_kernel, devices, carry),
        out_shape=(field,) * 3,
        in_specs=[VMEM] * (10 + len(halo)),
        out_specs=(VMEM,) * 3,
        compiler_params=pltpu.CompilerParams(vmem_limit_bytes=VMEM_PACK),
        name="finish",
    )(r2, pos, *base, *halo)


VMEM_PACK = 16 * 2**20
VMEM_CLOUD = 24 * 2**20


def solution(mesh):
    in_specs = (
        P(None, AXES),
        P(None, AXES),
        P(None, AXES),
        P(AXES),
        P(None, None, AXES),
        P(),
        P(),
    )
    out_specs = (P(None, AXES), P(None, AXES), P(None, AXES))
    return jax.shard_map(local, mesh=mesh, in_specs=in_specs, out_specs=out_specs, check_vma=False)
```

```python
import functools

import numpy as np

import jax
import jax.numpy as jnp
from jax import lax
from jax.experimental import pallas as pl
from jax.experimental.pallas import tpu as pltpu
from jax.sharding import PartitionSpec as P

SUBSTEPS = 10

loop_diff = 0.35
mix_along = 0.35
mix_vertical = 0.1
cond_rate = 0.1
latent_heat = 1.5
max_speed = 0.8

AXES = ("tile", "crm")
LOG2E = 1.4426950408889634
LN2 = 0.6931471805599453
SUB = 8
LANE = 128
HI = lax.Precision.HIGH
VMEM = pl.BlockSpec(memory_space=pltpu.VMEM)
HBM = pl.BlockSpec(memory_space=pltpu.HBM)


def in_hbm(x):
    return pltpu.with_memory_space_constraint(x, pltpu.HBM)


def fetch(sources, targets, sem):
    copies = [
        pltpu.make_async_copy(a, b, sem.at[n]) for n, (a, b) in enumerate(zip(sources, targets))
    ]
    for copy in copies:
        copy.start()
    return copies


def up_to(n, m):
    return -(-n // m) * m


def edges(block):
    count = lax.axis_size(AXES)
    forward = [(i, (i + 1) % count) for i in range(count)]
    backward = [(t, s) for s, t in forward]
    low = lax.ppermute(block[:, :, -1:], AXES, forward)
    high = lax.ppermute(block[:, :, :1], AXES, backward)
    return low, high


def ring_mean_operator(levels):
    f = np.eye(levels)
    east = west = f
    above = np.concatenate([f[1:], f[-1:]], axis=0)
    below = np.concatenate([f[:1], f[:-1]], axis=0)
    return (
        f
        + mix_along * (east - 2.0 * f + west)
        + mix_vertical * (above - 2.0 * f + below)
    )


def mean_operators(levels):
    v = ring_mean_operator(levels)
    power = np.eye(levels)
    total = np.zeros((levels, levels))
    for _ in range(SUBSTEPS):
        total = total + power
        power = v @ power
    return power, total / SUBSTEPS


def shift_operators(levels):
    drain = cond_rate * (1.0 + 0.5 * latent_heat)
    rest = (1.0 + drain) * np.eye(levels) - ring_mean_operator(levels)
    scale = LOG2E / SUBSTEPS
    return -np.linalg.inv(rest) * scale, -rest / scale


def halved(x):
    a = np.asarray(x, jnp.bfloat16)
    b = np.asarray(x - a.astype(np.float64), jnp.bfloat16)
    return jnp.asarray(a), jnp.asarray(b)


def split(x):
    a = x.astype(jnp.bfloat16)
    return a, (x - a.astype(jnp.float32)).astype(jnp.bfloat16)


def dot3(a, b, ca, cb):
    return dot(a[0], b[0], ca, cb) + dot(a[0], b[1], ca, cb) + dot(a[1], b[0], ca, cb)


def dot(a, b, ca, cb, precision=None):
    return lax.dot_general(
        a, b, (((ca,), (cb,)), ((), ())), precision=precision, preferred_element_type=jnp.float32
    )


def advection(f, v, low, high):
    cols = f.shape[1]
    lane = lax.broadcasted_iota(jnp.int32, f.shape, 1)
    ahead = jnp.where(lane == cols - 1, high, pltpu.roll(f, cols - 1, 1))
    behind = jnp.where(lane == 0, low, pltpu.roll(f, 1, 1))
    return -v * (ahead - behind) * 0.5 + loop_diff * (ahead - 2.0 * f + behind)


def onehot(pos_row, cols):
    place = lax.broadcasted_iota(jnp.int32, (cols, cols), 0)
    return jnp.where(place == pos_row, 1.0, 0.0).astype(jnp.bfloat16)


SLOT = 32
SLOTS = LANE // SLOT


def return_shape(cz, per):
    head = (LANE - 2 * cz) // SUB * SUB
    assert 0 <= head <= cz and cz - head <= SLOT
    return head, per + -(-per // SLOTS)


def slot_onehot(place_row, devices, per, cols):
    row = place_row % per // SLOTS * devices + place_row // per
    rows = -(-per // SLOTS) * devices
    return jnp.where(
        lax.broadcasted_iota(jnp.int32, (rows, cols), 0) == row, 1.0, 0.0
    ).astype(jnp.bfloat16)


CARRIED = (
    (0, 1, 0), (0, 0, 0), (0, 0, 1), (0, 1, 1),
    (1, 0, 0), (1, 1, 0), (1, 0, 1), (1, 1, 1),
)


def row_of(field, half, end):
    return CARRIED.index((field, half, end))


def halves(levels):
    first = up_to(-(-levels // 2), SUB)
    return first, levels - first


def carries(levels, per, width):
    first, second = halves(levels)
    return per >= len(CARRIED) and 3 * levels + first <= width and second < first


def pack_kernel(devices, carry, *refs):
    low_ref, high_ref = (None, None) if carry else refs[4:6]
    out_ref, pos_ref, s_ref, t_ref, q_ref, v_ref, own_ref, sem = refs[-8:]
    copies = [
        pltpu.make_async_copy(source, target, sem.at[n])
        for n, (source, target) in enumerate(zip(refs[:4], (t_ref, q_ref, v_ref, own_ref)))
    ]
    for n in (3, 0, 1, 2):
        copies[n].start()
    nl, cols = t_ref.shape
    width = s_ref.shape[0]
    per = cols // devices
    copies[3].wait()
    own = own_ref[...]
    who = lax.broadcasted_iota(jnp.int32, (devices, cols), 0)
    mine = jnp.where(who == own, 1.0, 0.0)
    before = lax.broadcasted_iota(jnp.int32, (cols, cols), 0) < lax.broadcasted_iota(
        jnp.int32, (cols, cols), 1
    )
    tri = jnp.where(before, 1.0, 0.0).astype(jnp.bfloat16)
    ranks = dot(mine.astype(jnp.bfloat16), tri, 1, 0)
    rank = jnp.sum(ranks * mine, axis=0, keepdims=True)
    pos = own * per + rank.astype(jnp.int32)
    pos_ref[...] = pos
    sel = onehot(pos, cols)

    for n in range(3):
        copies[n].wait()
    t = t_ref[...]
    x = q_ref[...] - 0.5 * t
    v = v_ref[...]
    if carry:
        low = high = jnp.zeros((nl, 1), jnp.float32)
    else:
        low = low_ref[1] - 0.5 * low_ref[0]
        high = high_ref[1] - 0.5 * high_ref[0]
    s_ref[0:nl, :] = x
    s_ref[nl:2 * nl, :] = v
    s_ref[2 * nl:3 * nl, :] = advection(x, v, low, high)
    rest = width - 3 * nl
    if rest:
        s_ref[3 * nl:, :] = jnp.zeros((rest, cols), jnp.float32)
    if carry:
        first, second = halves(nl)
        lane = lax.broadcasted_iota(jnp.int32, (1, cols), 1)
        s_ref[3 * nl + second:3 * nl + second + 1, :] = jnp.where(
            (lane == 0) | (lane == cols - 1), 1.0, 0.0
        )
    a, b = split(s_ref[...])
    out = dot(sel, a, 1, 1) + dot(sel, b, 1, 1)
    if carry:
        fill = jnp.zeros((first - second, cols), jnp.float32)
        parts = []
        for f in (x, t):
            parts += [f[:first], jnp.concatenate([f[first:], fill], axis=0)]
        parts = jnp.concatenate(parts, axis=1)
        shape = (SUB, parts.shape[1])
        want = jnp.full(shape, -1, jnp.int32)
        row = lax.broadcasted_iota(jnp.int32, shape, 0)
        for r, (field, half, end) in enumerate(CARRIED):
            want = jnp.where(row == r, (2 * field + half) * cols + end * (cols - 1), want)
        pick = jnp.where(lax.broadcasted_iota(jnp.int32, shape, 1) == want, 1.0, 0.0).astype(
            jnp.bfloat16
        )
        a, b = split(parts)
        ends = dot(pick, a, 1, 1) + dot(pick, b, 1, 1)
        ends = jnp.concatenate([ends, jnp.zeros((SUB, width - first), jnp.float32)], axis=1)
        ends = pltpu.roll(ends, 3 * nl, 1)
        out = (out.reshape(devices, per, width) + ends[None]).reshape(cols, width)
    out_ref[...] = out


LARGEST = 120.0


def moved_softplus2(small, g, move):
    if small:
        return jnp.log2(move + jnp.exp2(g))
    return move + softplus2(g - move)


def softplus2(f):
    return jnp.maximum(f, jnp.log2(1.0 + jnp.exp2(jnp.minimum(f, 100.0))))


def lanes(k):
    return pl.ds(k * LANE, LANE)


def fold(part_ref, levels, scale):
    total = part_ref[pl.ds(0, levels, stride=SUB), :]
    for s in range(1, SUB):
        total = total + part_ref[pl.ds(s, levels, stride=SUB), :]
    return total * scale


def clear_tail(part_ref, cz):
    for n in range(part_ref.shape[0]):
        for z in range(cz * SUB, part_ref.shape[1], SUB):
            part_ref[n, pl.ds(z, SUB), :] = jnp.zeros((SUB, LANE), jnp.float32)


def prep_kernel(carry, td_ref, down_hbm, shift_hbm, after_ref, start_ref, mean_ref, most_ref,
                high_ref, low_ref, shift_high_ref, shift_low_ref, raw_ref, part_ref, down_ref,
                shift_ref, td_sem, sem):
    del after_ref
    cz, cx, cols = td_ref.shape
    nl = down_ref.shape[1]
    zp = mean_ref.shape[0]
    width = high_ref.shape[1]
    groups = cx // SUB
    tiles = cols // LANE
    chunk = -(-cz // td_sem.shape[1])

    def td_copy(k, c):
        levels = pl.ds(c * chunk, min(chunk, cz - c * chunk))
        return pltpu.make_async_copy(
            td_ref.at[levels, :, lanes(k)], raw_ref.at[k, levels], td_sem.at[k, c]
        )

    copies = fetch((down_hbm, shift_hbm), (down_ref, shift_ref), sem)
    for k in range(tiles):
        for c in range(td_sem.shape[1]):
            td_copy(k, c).start()
    for copy in copies:
        copy.wait()

    def wide(rows):
        rows = jnp.concatenate(
            [rows, jnp.zeros((rows.shape[0], width - nl), jnp.float32)], axis=1
        )
        return jnp.concatenate([rows, jnp.zeros((zp - cz, width), jnp.float32)], axis=0)

    down = wide(down_ref[...])
    shift = wide(dot(shift_ref[...], down_ref[...], 1, 0, lax.Precision.HIGHEST))
    blocks = jnp.concatenate(
        [down, pltpu.roll(down, nl, 1), pltpu.roll(shift, 2 * nl, 1)], axis=0
    )
    a, low_ref[...] = split(blocks)
    offset = high_ref.shape[0] - 3 * zp
    if carry:
        shape = (offset, width)
        row = lax.broadcasted_iota(jnp.int32, shape, 0)
        to = jnp.where(row < nl, row + nl, row + 2 * nl)
        high_ref[0:offset, :] = jnp.where(
            lax.broadcasted_iota(jnp.int32, shape, 1) == to, 1.0, 0.0
        ).astype(jnp.bfloat16)
    high_ref[offset:, :] = a
    shift_high_ref[...], shift_low_ref[...] = split(shift[:, :nl])

    clear_tail(part_ref, cz)
    most = [jnp.zeros((SUB, LANE), jnp.float32)] * groups
    for k in range(tiles):
        for z in range(cz):
            if z % chunk == 0:
                td_copy(k, z // chunk).wait()
            total = None
            for i in range(groups):
                td = raw_ref[k, z, pl.ds(i, SUB, stride=groups), :]
                total = td if total is None else total + td
                first = (-0.5 * LOG2E) * td
                start_ref[k, z, pl.ds(SUB * i, SUB), :] = first
                most[i] = jnp.maximum(most[i], jnp.abs(first))
            part_ref[k, pl.ds(z * SUB, SUB), :] = total
        mean_ref[:, lanes(k)] = fold(part_ref.at[k], zp, 1.0 / cx)
    most_ref[...] = functools.reduce(jnp.maximum, most)


def cloud_kernel(devices, carry, nl, r_ref, start_ref, td_mean_ref, most_ref, g_high_ref, g_low_ref,
                 shift_high_ref, shift_low_ref, early_high_ref, early_low_ref,
                 late_high_ref, late_low_ref, after_ref, *refs):
    gain_ref, v_ref, ends_ref = (after_ref, *refs[:2]) if carry else (None,) * 3
    out_ref, halo_ref = refs[2:4] if carry else (refs[0], None)
    d_ref, base_ref, east_ref, west_ref, shift_ref, scale_ref, late_ref, value_ref, part_ref = (
        refs[-9:]
    )
    tiles, cz, cx, _ = start_ref.shape
    zp, cols = td_mean_ref.shape
    per = cols // devices
    groups = cx // SUB

    r = split(r_ref[...])
    offset = g_high_ref.shape[0] - 3 * zp
    prof = dot(g_high_ref[...], r[0], 1, 1) + dot(g_high_ref[...], r[1], 1, 1)
    fine = dot(g_low_ref[...], r[0], 1, 1)
    shift = prof[offset + 2 * zp:] + fine[2 * zp:]
    if carry:
        first, second = halves(nl)
        v = prof[0:nl]
        ends = prof[nl:offset]
        flag = ends[second:second + 1] > 0.5
        place = lax.rem(lax.broadcasted_iota(jnp.int32, (1, cols), 1), per)

        def neighbour(end, at):
            step = per if at == 0 else -per
            shift = lambda half: (step + at - row_of(0, half, end)) % cols
            return jnp.concatenate(
                [pltpu.roll(ends, shift(0), 1), pltpu.roll(ends, shift(1), 1)[:second]], axis=0
            )

        behind = neighbour(1, 0) * (loop_diff + 0.5 * v)
        ahead = neighbour(0, per - 1) * (loop_diff - 0.5 * v)
        halo = jnp.where(flag & (place == 0), behind, 0.0) + jnp.where(
            flag & (place == per - 1), ahead, 0.0
        )
        shift = shift + dot3((shift_high_ref[...], shift_low_ref[...]), split(halo), 1, 0)
    d0 = prof[offset:offset + zp] + fine[0:zp]
    speed = max_speed * jnp.tanh(prof[offset + zp:offset + 2 * zp] + fine[zp:2 * zp])
    base = d0 * LOG2E + shift
    base_ref[...] = base
    east_ref[...] = mix_along - 0.5 * speed
    west_ref[...] = mix_along + 0.5 * speed
    shift_ref[...] = shift
    scale_ref[...] = jnp.exp2(shift)
    drain = cond_rate * (1.0 + 0.5 * latent_heat)
    rate = 1.0 - 2.0 * mix_along + max(2.0 * mix_along, max_speed)
    growth = rate**SUBSTEPS
    series = sum(rate**n for n in range(SUBSTEPS))
    bound = growth * (jnp.max(jnp.abs(base)) + jnp.max(most_ref[...])) + series * drain * (
        jnp.max(jnp.abs(shift)) + 1.0
    )
    value_ref[0:zp, :] = td_mean_ref[...]
    value_ref[zp:2 * zp, :] = d0 - 0.5 * td_mean_ref[...]
    value_ref[2 * zp:, :] = shift
    clear_tail(part_ref, cz)

    def row_at(ref, z, k):
        return jnp.broadcast_to(ref[pl.ds(z, 1), lanes(k)], (SUB, LANE))

    slot = [0] + [SUB * (i + 1) for i in range(1, groups)]
    last = slot[-1]

    def get(k, z):
        return [d_ref[k, z, pl.ds(slot[i], SUB), :] for i in range(groups)]

    def put(k, z, i, new):
        d_ref[k, z, pl.ds(slot[i], SUB), :] = new
        if i == 0:
            d_ref[k, z, pl.ds(SUB, SUB), :] = new
        if i == groups - 1:
            d_ref[k, z, pl.ds(last + SUB, SUB), :] = new

    for k in range(tiles):
        for z in range(cz):
            base = row_at(base_ref, z, k)
            for i in range(groups):
                put(k, z, i, base + start_ref[k, z, pl.ds(SUB * i, SUB), :])

    def step(small, _, carry):
        for k in range(tiles):
            below = cur = get(k, 0)
            pair = None
            for z in range(cz):
                above = get(k, z + 1) if z + 1 < cz else cur
                if pair is None:
                    pair = [c + a for c, a in zip(cur, above)]
                    column = [p + b for p, b in zip(pair, below)]
                else:
                    column = [p + a for p, a in zip(pair, above)]
                    pair = None
                ea = row_at(east_ref, z, k)
                we = row_at(west_ref, z, k)
                move = row_at(scale_ref if small else shift_ref, z, k)
                ring = [d_ref[k, z, pl.ds(last + SUB - 1, SUB), :]] + cur
                ring = ring + [d_ref[k, z, pl.ds(1, SUB), :]]
                for i in range(groups):
                    new = (
                        mix_vertical * column[i]
                        + ea * ring[i + 2]
                        + we * ring[i]
                        - drain * moved_softplus2(small, cur[i], move)
                    )
                    put(k, z, i, new)
                below, cur = cur, above
        return carry

    def finish(small):
        lax.fori_loop(0, SUBSTEPS, functools.partial(step, small), 0)
        head, rows = return_shape(cz, per)
        cloud_ref = east_ref
        for k in range(tiles):
            for z in range(cz):
                total = cloud = None
                move = row_at(scale_ref if small else shift_ref, z, k)
                for f in get(k, z):
                    c = moved_softplus2(small, f, move)
                    total = f if total is None else total + f
                    cloud = c if cloud is None else cloud + c
                part_ref[2 * k, pl.ds(z * SUB, SUB), :] = total
                part_ref[2 * k + 1, pl.ds(z * SUB, SUB), :] = cloud
            early = dot3(
                split(value_ref[:, lanes(k)]), (early_high_ref[...], early_low_ref[...]), 0, 0
            )
            if carry and k == 0:
                halo = halo_part(devices, r_ref, ends_ref, v_ref)
                halo_ref[...] = halo + dot(gain_ref[...], halo, 1, 0, HI)
            moved = LN2 * shift_ref[:, lanes(k)]
            end = fold(part_ref.at[2 * k], zp, LN2 / cx) - moved
            cloud = fold(part_ref.at[2 * k + 1], zp, LN2 / cx) - moved
            late_ref[0:zp, lanes(k)] = end
            late_ref[zp:, lanes(k)] = cloud[0:head]
            cloud_ref[:, lanes(k)] = cloud
            late = dot3(split(late_ref[:, lanes(k)]), (late_high_ref[...], late_low_ref[...]), 0, 0)
            main = early + late
            for h in range(LANE // per):
                out_ref[pl.ds((k * (LANE // per) + h) * rows, per), :] = main[h * per:(h + 1) * per]
        left = cloud_ref[head:, :]
        left = jnp.concatenate([left, jnp.zeros((SLOT - left.shape[0], cols), jnp.float32)], axis=0) \
            if left.shape[0] < SLOT else left
        place = lax.broadcasted_iota(jnp.int32, (1, cols), 1)
        part = place % SLOTS
        spread = jnp.concatenate(
            [jnp.where(part == j, left, 0.0) for j in range(SLOTS)], axis=0
        )
        pick = slot_onehot(place, devices, per, cols)
        a, b = split(spread)
        extra = dot(pick, a, 1, 1) + dot(pick, b, 1, 1)
        for i in range(rows - per):
            out_ref[pl.ds(per + i, devices, stride=rows), :] = extra[i * devices:(i + 1) * devices]

    @pl.when(bound < LARGEST)
    def _():
        finish(True)

    @pl.when(jnp.logical_not(bound < LARGEST))
    def _():
        finish(False)


def base_kernel(devices, carry, *refs):
    pos_ref = refs[6]
    low_ref, high_ref = (None, None) if carry else refs[7:9]
    to_ref, qo_ref, level_high_ref, level_low_ref, rest_high_ref, rest_low_ref = refs[-16:-10]
    sel_ref, pick_ref, gain_ref = refs[-10:-7]
    t_ref, q_ref, v_ref, down_ref, up_ref, lin_ref, sem = refs[-7:]
    copies = fetch(refs[:6], refs[-7:-1], sem)
    nl, cols = t_ref.shape
    cz = up_ref.shape[0]
    per = cols // devices
    head, _ = return_shape(cz, per)
    sel_ref[...] = onehot(pos_ref[...], cols)
    pick_ref[...] = slot_onehot(pos_ref[...], devices, per, cols)
    for copy in copies:
        copy.wait()
    up = up_ref[...].T
    wide = jnp.concatenate([up, jnp.zeros((nl, LANE - cz), jnp.float32)], axis=1)
    lane = lax.broadcasted_iota(jnp.int32, wide.shape, 1)
    level = jnp.concatenate(
        [
            wide,
            -pltpu.roll(wide, cz, 1),
            pltpu.roll(jnp.where(lane < head, wide, 0.0), 2 * cz, 1),
        ],
        axis=0,
    )
    level_high_ref[...], level_low_ref[...] = split(level)
    rest = jnp.where(lane < SLOT, pltpu.roll(wide, LANE - head, 1), 0.0)
    rest_high_ref[...], rest_low_ref[...] = split(rest[:, 0:SLOT])
    if carry:
        low = high = (jnp.zeros((nl, 1), jnp.float32),) * 2
    else:
        low = (low_ref[0], low_ref[1])
        high = (high_ref[0], high_ref[1])
    v = v_ref[...]
    t = t_ref[...]
    q = q_ref[...]
    advt = advection(t, v, low[0], high[0])
    advq = advection(q, v, low[1], high[1])
    prof = dot(down_ref[...], jnp.concatenate([t, q, advt, advq], axis=1), 1, 0, HI)
    lin = lin_ref[...]
    gain = dot(lin[0], prof[:, :2 * cols], 1, 0, HI) + dot(lin[1], prof[:, 2 * cols:], 1, 0, HI)
    gain = dot(up, gain, 1, 0, HI)
    to_ref[...] = t + advt + gain[:, :cols]
    qo_ref[...] = q + advq + gain[:, cols:]
    gain_ref[...] = dot(up, dot(lin[1], down_ref[...], 1, 0, HI), 1, 0, HI)


def ends_pick():
    pick = np.zeros((2 * SUB, 2 * LANE))
    for r, (field, half, end) in enumerate(CARRIED):
        row = r + (0 if end else SUB)
        place = half * LANE + (0 if end else 1)
        if field:
            pick[row, place] = 1.0
        pick[row, place + 2] = 0.5 if field else 1.0
    return pick


def halo_part(devices, r_ref, ends_ref, v_ref):
    nl, cols = v_ref.shape
    per = cols // devices
    first, second = halves(nl)
    me = lax.axis_index(AXES)

    def block(device):
        start = pl.multiple_of(device * per, SUB)
        return r_ref[pl.ds(start, SUB), :]

    rows = jnp.concatenate(
        [block(lax.rem(me + devices - 1, devices)), block(lax.rem(me + 1, devices))], axis=0
    )
    rows = pltpu.roll(rows, rows.shape[1] - 3 * nl, 1)[:, :LANE]
    a, b = split(rows)
    pick = ends_ref[...]
    part = dot(a, pick, 0, 0) + dot(b, pick, 0, 0)
    ends = jnp.concatenate([part[:first, :LANE], part[:second, LANE:]], axis=0)
    lane = lax.broadcasted_iota(jnp.int32, ends.shape, 1)
    low = v_ref[:, :LANE]
    high = v_ref[:, cols - LANE:]
    v = jnp.where(
        lane == 0, low, jnp.where(lane == 2, pltpu.roll(low, 2, 1), jnp.where(
            lane == 1, -pltpu.roll(high, 2, 1), -pltpu.roll(high, 4, 1)))
    )
    return (loop_diff + 0.5 * v) * ends


def add_ends(field_ref, out_ref, extra, halo, place):
    cols = field_ref.shape[1]
    lane = lax.broadcasted_iota(jnp.int32, halo.shape, 1)
    start = pltpu.roll(halo, LANE - place, 1) if place else halo
    stop = pltpu.roll(halo, LANE - 2 - place, 1)
    parts = [extra[:, k:k + LANE] for k in range(0, cols, LANE)]
    parts[0] = parts[0] + jnp.where(lane == 0, start, 0.0)
    parts[-1] = parts[-1] + jnp.where(lane == LANE - 1, stop, 0.0)
    for k, part in enumerate(parts):
        out_ref[:, lanes(k)] = field_ref[:, lanes(k)] + part


def finish_kernel(devices, carry, *refs):
    r_ref, pos_ref, tb_ref, qb_ref = refs[:4]
    level_high_ref, level_low_ref, rest_high_ref, rest_low_ref, sel_ref, pick_ref = refs[4:10]
    to_ref, qo_ref, co_ref = refs[-3:]
    nl, cols = tb_ref.shape
    per = cols // devices
    rows = r_ref.shape[0] // devices
    main = jnp.concatenate([r_ref[pl.ds(h * rows, per), :] for h in range(devices)], axis=0)
    extra = jnp.concatenate(
        [r_ref[pl.ds(per + i, devices, stride=rows), :] for i in range(rows - per)], axis=0
    )
    a, b = split(extra)
    extra = dot(a, pick_ref[...], 0, 0) + dot(b, pick_ref[...], 0, 0)
    part = pos_ref[...] % per % SLOTS
    left = jnp.where(part == 0, extra[:SLOT], 0.0)
    for j in range(1, SLOTS):
        left = left + jnp.where(part == j, extra[j * SLOT:(j + 1) * SLOT], 0.0)
    rest = dot3((rest_high_ref[...], rest_low_ref[...]), split(left), 1, 0)
    a, b = split(dot3((level_high_ref[...], level_low_ref[...]), split(main), 1, 1))
    out = dot(a, sel_ref[...], 1, 0) + dot(b, sel_ref[...], 1, 0)
    if carry:
        halo = refs[10][...]
        add_ends(tb_ref, to_ref, out[0:nl], halo, 0)
        add_ends(qb_ref, qo_ref, out[nl:2 * nl], halo, 2)
    else:
        to_ref[...] = tb_ref[...] + out[0:nl]
        qo_ref[...] = qb_ref[...] + out[nl:2 * nl]
    co_ref[...] = out[2 * nl:3 * nl] + rest


def local(
    thermal_anomaly,
    vapour_anomaly,
    periodic_flow_velocity,
    processor_assignment,
    thermal_disturbance,
    layer_index_downscale,
    layer_index_upscale,
):
    nl, cols = thermal_anomaly.shape
    cz, cx, _ = thermal_disturbance.shape
    devices = lax.axis_size(AXES)
    per = cols // devices
    zp = up_to(cz, SUB)
    f32 = jnp.float32
    width = up_to(3 * nl, LANE)
    head, rows = return_shape(cz, per)
    field = jax.ShapeDtypeStruct((nl, cols), f32)
    carry = carries(nl, per, width)

    fields = (thermal_anomaly, vapour_anomaly, periodic_flow_velocity)
    ends = () if carry else edges(jnp.stack(fields[:2]))
    out, pos = pl.pallas_call(
        functools.partial(pack_kernel, devices, carry),
        out_shape=(
            jax.ShapeDtypeStruct((cols, width), f32),
            jax.ShapeDtypeStruct((1, cols), jnp.int32),
        ),
        in_specs=[HBM] * 4 + [VMEM] * len(ends),
        out_specs=(VMEM,) * 2,
        scratch_shapes=[
            pltpu.VMEM((width, cols), f32),
            pltpu.VMEM((nl, cols), f32),
            pltpu.VMEM((nl, cols), f32),
            pltpu.VMEM((nl, cols), f32),
            pltpu.VMEM((1, cols), jnp.int32),
            pltpu.SemaphoreType.DMA((4,)),
        ],
        compiler_params=pltpu.CompilerParams(vmem_limit_bytes=VMEM_PACK),
        name="pack",
    )(*[in_hbm(f) for f in (*fields, processor_assignment.reshape(1, cols))], *ends)

    def exchange(blocks, *inner):
        shape = blocks.shape
        blocks = blocks.reshape(devices, *inner)
        return lax.all_to_all(blocks, AXES, split_axis=0, concat_axis=0, tiled=True).reshape(shape)

    r1 = exchange(out, per, width)

    power, total = mean_operators(cz)
    release = 1.0 + 0.5 * latent_heat
    shift, unshift = shift_operators(cz)
    mean = np.zeros((4 * zp + head, LANE))
    z_part = np.zeros((4 * zp + head, cz))
    z_part[zp:zp + cz] = power.T / release
    z_part[2 * zp:2 * zp + cz] = (total @ unshift).T / release
    z_part[3 * zp:3 * zp + cz] = -np.eye(cz) / release
    mean[0:cz, 0:cz] = power.T
    mean[:, 0:cz] += latent_heat * z_part
    mean[:, cz:2 * cz] = z_part
    mean[4 * zp:, 2 * cz:2 * cz + head] = np.eye(head)

    tiles = cols // LANE
    groups = cx // SUB
    level_rows = 3 * zp + (nl + halves(nl)[0] if carry else 0)
    bf16 = jnp.bfloat16
    prep = pl.pallas_call(
        functools.partial(prep_kernel, carry),
        out_shape=(
            jax.ShapeDtypeStruct((tiles, cz, cx, LANE), f32),
            jax.ShapeDtypeStruct((zp, cols), f32),
            jax.ShapeDtypeStruct((SUB, LANE), f32),
            jax.ShapeDtypeStruct((level_rows, width), bf16),
            jax.ShapeDtypeStruct((3 * zp, width), bf16),
            jax.ShapeDtypeStruct((zp, nl), bf16),
            jax.ShapeDtypeStruct((zp, nl), bf16),
        ),
        in_specs=[HBM, HBM, HBM, VMEM],
        out_specs=(VMEM,) * 7,
        scratch_shapes=[
            pltpu.VMEM((tiles, cz, cx, LANE), f32),
            pltpu.VMEM((tiles, zp * SUB, LANE), f32),
            pltpu.VMEM((cz, nl), f32),
            pltpu.VMEM((cz, cz), f32),
            pltpu.SemaphoreType.DMA((tiles, 5)),
            pltpu.SemaphoreType.DMA((2,)),
        ],
        compiler_params=pltpu.CompilerParams(vmem_limit_bytes=VMEM_PACK),
        cost_estimate=pl.CostEstimate(flops=10**8, bytes_accessed=4 * 10**6, transcendentals=0),
        name="prep",
    )(
        in_hbm(thermal_disturbance),
        in_hbm(layer_index_downscale),
        in_hbm(jnp.asarray(shift, f32)),
        pos,
    )
    lin = np.stack([power - np.eye(cz), total])
    *base, gain = pl.pallas_call(
        functools.partial(base_kernel, devices, carry),
        out_shape=(
            field,
            field,
            jax.ShapeDtypeStruct((3 * nl, LANE), bf16),
            jax.ShapeDtypeStruct((3 * nl, LANE), bf16),
            jax.ShapeDtypeStruct((nl, SLOT), bf16),
            jax.ShapeDtypeStruct((nl, SLOT), bf16),
            jax.ShapeDtypeStruct((cols, cols), bf16),
            jax.ShapeDtypeStruct((devices * (rows - per), cols), bf16),
            jax.ShapeDtypeStruct((nl, nl), f32),
        ),
        in_specs=[HBM] * 6 + [VMEM] * (1 + len(ends)),
        out_specs=(VMEM,) * 9,
        scratch_shapes=[
            pltpu.VMEM((nl, cols), f32),
            pltpu.VMEM((nl, cols), f32),
            pltpu.VMEM((nl, cols), f32),
            pltpu.VMEM((cz, nl), f32),
            pltpu.VMEM((cz, nl), f32),
            pltpu.VMEM((2, cz, cz), f32),
            pltpu.SemaphoreType.DMA((6,)),
        ],
        compiler_params=pltpu.CompilerParams(vmem_limit_bytes=VMEM_PACK),
        cost_estimate=pl.CostEstimate(flops=10**8, bytes_accessed=10**6, transcendentals=0),
        name="base",
    )(
        *[
            in_hbm(x)
            for x in (
                *fields,
                layer_index_downscale,
                layer_index_upscale.T,
                jnp.asarray(lin, f32),
            )
        ],
        pos,
        *ends,
    )
    halo = (periodic_flow_velocity, jnp.asarray(ends_pick(), bf16)) if carry else ()
    vals, *halo = pl.pallas_call(
        functools.partial(cloud_kernel, devices, carry, nl),
        out_shape=(jax.ShapeDtypeStruct((devices * rows, LANE), f32),)
        + ((jax.ShapeDtypeStruct((nl, LANE), f32),) if carry else ()),
        in_specs=[VMEM] * (13 + len(halo)),
        out_specs=(VMEM,) * (2 if carry else 1),
        scratch_shapes=[
            pltpu.VMEM((tiles, cz, SUB * (groups + 2), LANE), f32),
            pltpu.VMEM((zp, cols), f32),
            pltpu.VMEM((zp, cols), f32),
            pltpu.VMEM((zp, cols), f32),
            pltpu.VMEM((zp, cols), f32),
            pltpu.VMEM((zp, cols), f32),
            pltpu.VMEM((zp + head, cols), f32),
            pltpu.VMEM((3 * zp, cols), f32),
            pltpu.VMEM((2 * tiles, zp * SUB, LANE), f32),
        ],
        compiler_params=pltpu.CompilerParams(vmem_limit_bytes=VMEM_CLOUD),
        name="cloud",
    )(r1, *prep, *halved(mean[:3 * zp]), *halved(mean[3 * zp:]), gain, *halo)
    r2 = exchange(vals, 1, rows * LANE)
    return pl.pallas_call(
        functools.partial(finish_kernel, devices, carry),
        out_shape=(field,) * 3,
        in_specs=[VMEM] * (10 + len(halo)),
        out_specs=(VMEM,) * 3,
        compiler_params=pltpu.CompilerParams(vmem_limit_bytes=VMEM_PACK),
        name="finish",
    )(r2, pos, *base, *halo)


VMEM_PACK = 16 * 2**20
VMEM_CLOUD = 24 * 2**20


def solution(mesh):
    in_specs = (
        P(None, AXES),
        P(None, AXES),
        P(None, AXES),
        P(AXES),
        P(None, None, AXES),
        P(),
        P(),
    )
    out_specs = (P(None, AXES), P(None, AXES), P(None, AXES))
    return jax.shard_map(local, mesh=mesh, in_specs=in_specs, out_specs=out_specs, check_vma=False)
```

```python
import functools

import numpy as np

import jax
import jax.numpy as jnp
from jax import lax
from jax.experimental import pallas as pl
from jax.experimental.pallas import tpu as pltpu
from jax.sharding import PartitionSpec as P

SUBSTEPS = 10

loop_diff = 0.35
mix_along = 0.35
mix_vertical = 0.1
cond_rate = 0.1
latent_heat = 1.5
max_speed = 0.8

AXES = ("tile", "crm")
LOG2E = 1.4426950408889634
LN2 = 0.6931471805599453
SUB = 8
LANE = 128
HI = lax.Precision.HIGH
VMEM = pl.BlockSpec(memory_space=pltpu.VMEM)
HBM = pl.BlockSpec(memory_space=pltpu.HBM)


def in_hbm(x):
    return pltpu.with_memory_space_constraint(x, pltpu.HBM)


def fetch(sources, targets, sem):
    copies = [
        pltpu.make_async_copy(a, b, sem.at[n]) for n, (a, b) in enumerate(zip(sources, targets))
    ]
    for copy in copies:
        copy.start()
    return copies


def up_to(n, m):
    return -(-n // m) * m


def edges(block):
    count = lax.axis_size(AXES)
    forward = [(i, (i + 1) % count) for i in range(count)]
    backward = [(t, s) for s, t in forward]
    low = lax.ppermute(block[:, :, -1:], AXES, forward)
    high = lax.ppermute(block[:, :, :1], AXES, backward)
    return low, high


def ring_mean_operator(levels):
    f = np.eye(levels)
    east = west = f
    above = np.concatenate([f[1:], f[-1:]], axis=0)
    below = np.concatenate([f[:1], f[:-1]], axis=0)
    return (
        f
        + mix_along * (east - 2.0 * f + west)
        + mix_vertical * (above - 2.0 * f + below)
    )


def mean_operators(levels):
    v = ring_mean_operator(levels)
    power = np.eye(levels)
    total = np.zeros((levels, levels))
    for _ in range(SUBSTEPS):
        total = total + power
        power = v @ power
    return power, total / SUBSTEPS


def shift_operators(levels):
    drain = cond_rate * (1.0 + 0.5 * latent_heat)
    rest = (1.0 + drain) * np.eye(levels) - ring_mean_operator(levels)
    scale = LOG2E / SUBSTEPS
    return -np.linalg.inv(rest) * scale, -rest / scale


def halved(x):
    a = np.asarray(x, jnp.bfloat16)
    b = np.asarray(x - a.astype(np.float64), jnp.bfloat16)
    return jnp.asarray(a), jnp.asarray(b)


def split(x):
    a = x.astype(jnp.bfloat16)
    return a, (x - a.astype(jnp.float32)).astype(jnp.bfloat16)


def dot3(a, b, ca, cb):
    return dot(a[0], b[0], ca, cb) + dot(a[0], b[1], ca, cb) + dot(a[1], b[0], ca, cb)


def dot(a, b, ca, cb, precision=None):
    return lax.dot_general(
        a, b, (((ca,), (cb,)), ((), ())), precision=precision, preferred_element_type=jnp.float32
    )


def advection(f, v, low, high):
    cols = f.shape[1]
    lane = lax.broadcasted_iota(jnp.int32, f.shape, 1)
    ahead = jnp.where(lane == cols - 1, high, pltpu.roll(f, cols - 1, 1))
    behind = jnp.where(lane == 0, low, pltpu.roll(f, 1, 1))
    return -v * (ahead - behind) * 0.5 + loop_diff * (ahead - 2.0 * f + behind)


def onehot(pos_row, cols):
    place = lax.broadcasted_iota(jnp.int32, (cols, cols), 0)
    return jnp.where(place == pos_row, 1.0, 0.0).astype(jnp.bfloat16)


SLOT = 32
SLOTS = LANE // SLOT


def return_shape(cz, per):
    head = (LANE - 2 * cz) // SUB * SUB
    assert 0 <= head <= cz and cz - head <= SLOT
    return head, per + -(-per // SLOTS)


def slot_onehot(place_row, devices, per, cols):
    row = place_row % per // SLOTS * devices + place_row // per
    rows = -(-per // SLOTS) * devices
    return jnp.where(
        lax.broadcasted_iota(jnp.int32, (rows, cols), 0) == row, 1.0, 0.0
    ).astype(jnp.bfloat16)


CARRIED = (
    (0, 1, 0), (0, 0, 0), (0, 0, 1), (0, 1, 1),
    (1, 0, 0), (1, 1, 0), (1, 0, 1), (1, 1, 1),
)


def row_of(field, half, end):
    return CARRIED.index((field, half, end))


def halves(levels):
    first = up_to(-(-levels // 2), SUB)
    return first, levels - first


def carries(levels, per, width):
    first, second = halves(levels)
    return per >= len(CARRIED) and 3 * levels + first <= width and second < first


def pack_kernel(devices, carry, *refs):
    low_ref, high_ref = (None, None) if carry else refs[4:6]
    out_ref, pos_ref, s_ref, t_ref, q_ref, v_ref, own_ref, sem = refs[-8:]
    copies = [
        pltpu.make_async_copy(source, target, sem.at[n])
        for n, (source, target) in enumerate(zip(refs[:4], (t_ref, q_ref, v_ref, own_ref)))
    ]
    for n in (3, 0, 1, 2):
        copies[n].start()
    nl, cols = t_ref.shape
    width = s_ref.shape[0]
    per = cols // devices
    copies[3].wait()
    own = own_ref[...]
    who = lax.broadcasted_iota(jnp.int32, (devices, cols), 0)
    mine = jnp.where(who == own, 1.0, 0.0)
    before = lax.broadcasted_iota(jnp.int32, (cols, cols), 0) < lax.broadcasted_iota(
        jnp.int32, (cols, cols), 1
    )
    tri = jnp.where(before, 1.0, 0.0).astype(jnp.bfloat16)
    ranks = dot(mine.astype(jnp.bfloat16), tri, 1, 0)
    rank = jnp.sum(ranks * mine, axis=0, keepdims=True)
    pos = own * per + rank.astype(jnp.int32)
    pos_ref[...] = pos
    sel = onehot(pos, cols)

    for n in range(3):
        copies[n].wait()
    t = t_ref[...]
    x = q_ref[...] - 0.5 * t
    v = v_ref[...]
    if carry:
        low = high = jnp.zeros((nl, 1), jnp.float32)
    else:
        low = low_ref[1] - 0.5 * low_ref[0]
        high = high_ref[1] - 0.5 * high_ref[0]
    s_ref[0:nl, :] = x
    s_ref[nl:2 * nl, :] = v
    s_ref[2 * nl:3 * nl, :] = advection(x, v, low, high)
    rest = width - 3 * nl
    if rest:
        s_ref[3 * nl:, :] = jnp.zeros((rest, cols), jnp.float32)
    if carry:
        first, second = halves(nl)
        lane = lax.broadcasted_iota(jnp.int32, (1, cols), 1)
        s_ref[3 * nl + second:3 * nl + second + 1, :] = jnp.where(
            (lane == 0) | (lane == cols - 1), 1.0, 0.0
        )
    a, b = split(s_ref[...])
    out = dot(sel, a, 1, 1) + dot(sel, b, 1, 1)
    if carry:
        fill = jnp.zeros((first - second, cols), jnp.float32)
        parts = []
        for f in (x, t):
            parts += [f[:first], jnp.concatenate([f[first:], fill], axis=0)]
        parts = jnp.concatenate(parts, axis=1)
        shape = (SUB, parts.shape[1])
        want = jnp.full(shape, -1, jnp.int32)
        row = lax.broadcasted_iota(jnp.int32, shape, 0)
        for r, (field, half, end) in enumerate(CARRIED):
            want = jnp.where(row == r, (2 * field + half) * cols + end * (cols - 1), want)
        pick = jnp.where(lax.broadcasted_iota(jnp.int32, shape, 1) == want, 1.0, 0.0).astype(
            jnp.bfloat16
        )
        a, b = split(parts)
        ends = dot(pick, a, 1, 1) + dot(pick, b, 1, 1)
        ends = jnp.concatenate([ends, jnp.zeros((SUB, width - first), jnp.float32)], axis=1)
        ends = pltpu.roll(ends, 3 * nl, 1)
        out = (out.reshape(devices, per, width) + ends[None]).reshape(cols, width)
    out_ref[...] = out


LARGEST = 60.0


def moved_softplus2(small, g, move):
    if small:
        return jnp.log2(move + jnp.exp2(g))
    return move + softplus2(g - move)


def moved_sum(small, parts, move):
    if not small:
        return [moved_softplus2(small, g, move) for g in parts]
    powers = [move + jnp.exp2(g) for g in parts]
    pairs = [a * b for a, b in zip(powers[::2], powers[1::2])] + powers[len(powers) // 2 * 2:]
    return [jnp.log2(p) for p in pairs]


def softplus2(f):
    return jnp.maximum(f, jnp.log2(1.0 + jnp.exp2(jnp.minimum(f, 100.0))))


def lanes(k):
    return pl.ds(k * LANE, LANE)


def fold(part_ref, levels, scale):
    total = part_ref[pl.ds(0, levels, stride=SUB), :]
    for s in range(1, SUB):
        total = total + part_ref[pl.ds(s, levels, stride=SUB), :]
    return total * scale


def clear_tail(part_ref, cz):
    for n in range(part_ref.shape[0]):
        for z in range(cz * SUB, part_ref.shape[1], SUB):
            part_ref[n, pl.ds(z, SUB), :] = jnp.zeros((SUB, LANE), jnp.float32)


def prep_kernel(carry, td_ref, down_hbm, shift_hbm, after_ref, start_ref, mean_ref, most_ref,
                high_ref, low_ref, shift_high_ref, shift_low_ref, raw_ref, part_ref, down_ref,
                shift_ref, td_sem, sem):
    del after_ref
    cz, cx, cols = td_ref.shape
    nl = down_ref.shape[1]
    zp = mean_ref.shape[0]
    width = high_ref.shape[1]
    groups = cx // SUB
    tiles = cols // LANE
    chunk = -(-cz // td_sem.shape[1])

    def td_copy(k, c):
        levels = pl.ds(c * chunk, min(chunk, cz - c * chunk))
        return pltpu.make_async_copy(
            td_ref.at[levels, :, lanes(k)], raw_ref.at[k, levels], td_sem.at[k, c]
        )

    copies = fetch((down_hbm, shift_hbm), (down_ref, shift_ref), sem)
    for k in range(tiles):
        for c in range(td_sem.shape[1]):
            td_copy(k, c).start()
    for copy in copies:
        copy.wait()

    def wide(rows):
        rows = jnp.concatenate(
            [rows, jnp.zeros((rows.shape[0], width - nl), jnp.float32)], axis=1
        )
        return jnp.concatenate([rows, jnp.zeros((zp - cz, width), jnp.float32)], axis=0)

    down = wide(down_ref[...])
    shift = wide(dot(shift_ref[...], down_ref[...], 1, 0, lax.Precision.HIGHEST))
    blocks = jnp.concatenate(
        [down, pltpu.roll(down, nl, 1), pltpu.roll(shift, 2 * nl, 1)], axis=0
    )
    a, low_ref[...] = split(blocks)
    offset = high_ref.shape[0] - 3 * zp
    if carry:
        shape = (offset, width)
        row = lax.broadcasted_iota(jnp.int32, shape, 0)
        to = jnp.where(row < nl, row + nl, row + 2 * nl)
        high_ref[0:offset, :] = jnp.where(
            lax.broadcasted_iota(jnp.int32, shape, 1) == to, 1.0, 0.0
        ).astype(jnp.bfloat16)
    high_ref[offset:, :] = a
    shift_high_ref[...], shift_low_ref[...] = split(shift[:, :nl])

    clear_tail(part_ref, cz)
    most = [jnp.zeros((SUB, LANE), jnp.float32)] * groups
    for k in range(tiles):
        for z in range(cz):
            if z % chunk == 0:
                td_copy(k, z // chunk).wait()
            total = None
            for i in range(groups):
                td = raw_ref[k, z, pl.ds(i, SUB, stride=groups), :]
                total = td if total is None else total + td
                first = (-0.5 * LOG2E) * td
                start_ref[k, z, pl.ds(SUB * i, SUB), :] = first
                most[i] = jnp.maximum(most[i], jnp.abs(first))
            part_ref[k, pl.ds(z * SUB, SUB), :] = total
        mean_ref[:, lanes(k)] = fold(part_ref.at[k], zp, 1.0 / cx)
    most_ref[...] = functools.reduce(jnp.maximum, most)


def cloud_kernel(devices, carry, nl, r_ref, start_ref, td_mean_ref, most_ref, g_high_ref, g_low_ref,
                 shift_high_ref, shift_low_ref, early_high_ref, early_low_ref,
                 late_high_ref, late_low_ref, after_ref, *refs):
    gain_ref, v_ref, ends_ref = (after_ref, *refs[:2]) if carry else (None,) * 3
    out_ref, halo_ref = refs[2:4] if carry else (refs[0], None)
    d_ref, base_ref, east_ref, west_ref, shift_ref, scale_ref, late_ref, value_ref, part_ref = (
        refs[-9:]
    )
    tiles, cz, cx, _ = start_ref.shape
    zp, cols = td_mean_ref.shape
    per = cols // devices
    groups = cx // SUB

    r = split(r_ref[...])
    offset = g_high_ref.shape[0] - 3 * zp
    prof = dot(g_high_ref[...], r[0], 1, 1) + dot(g_high_ref[...], r[1], 1, 1)
    fine = dot(g_low_ref[...], r[0], 1, 1)
    shift = prof[offset + 2 * zp:] + fine[2 * zp:]
    if carry:
        first, second = halves(nl)
        v = prof[0:nl]
        ends = prof[nl:offset]
        flag = ends[second:second + 1] > 0.5
        place = lax.rem(lax.broadcasted_iota(jnp.int32, (1, cols), 1), per)

        def neighbour(end, at):
            step = per if at == 0 else -per
            shift = lambda half: (step + at - row_of(0, half, end)) % cols
            return jnp.concatenate(
                [pltpu.roll(ends, shift(0), 1), pltpu.roll(ends, shift(1), 1)[:second]], axis=0
            )

        behind = neighbour(1, 0) * (loop_diff + 0.5 * v)
        ahead = neighbour(0, per - 1) * (loop_diff - 0.5 * v)
        halo = jnp.where(flag & (place == 0), behind, 0.0) + jnp.where(
            flag & (place == per - 1), ahead, 0.0
        )
        shift = shift + dot3((shift_high_ref[...], shift_low_ref[...]), split(halo), 1, 0)
    d0 = prof[offset:offset + zp] + fine[0:zp]
    speed = max_speed * jnp.tanh(prof[offset + zp:offset + 2 * zp] + fine[zp:2 * zp])
    base = d0 * LOG2E + shift
    base_ref[...] = base
    east_ref[...] = mix_along - 0.5 * speed
    west_ref[...] = mix_along + 0.5 * speed
    shift_ref[...] = shift
    scale_ref[...] = jnp.exp2(shift)
    drain = cond_rate * (1.0 + 0.5 * latent_heat)
    rate = 1.0 - 2.0 * mix_along + max(2.0 * mix_along, max_speed)
    growth = rate**SUBSTEPS
    series = sum(rate**n for n in range(SUBSTEPS))
    bound = growth * (jnp.max(jnp.abs(base)) + jnp.max(most_ref[...])) + series * drain * (
        jnp.max(jnp.abs(shift)) + 1.0
    )
    value_ref[0:zp, :] = td_mean_ref[...]
    value_ref[zp:2 * zp, :] = d0 - 0.5 * td_mean_ref[...]
    value_ref[2 * zp:, :] = shift
    clear_tail(part_ref, cz)

    def row_at(ref, z, k):
        return jnp.broadcast_to(ref[pl.ds(z, 1), lanes(k)], (SUB, LANE))

    slot = [0] + [SUB * (i + 1) for i in range(1, groups)]
    last = slot[-1]

    def get(k, z):
        return [d_ref[k, z, pl.ds(slot[i], SUB), :] for i in range(groups)]

    def put(k, z, i, new):
        d_ref[k, z, pl.ds(slot[i], SUB), :] = new
        if i == 0:
            d_ref[k, z, pl.ds(SUB, SUB), :] = new
        if i == groups - 1:
            d_ref[k, z, pl.ds(last + SUB, SUB), :] = new

    for k in range(tiles):
        for z in range(cz):
            base = row_at(base_ref, z, k)
            for i in range(groups):
                put(k, z, i, base + start_ref[k, z, pl.ds(SUB * i, SUB), :])

    def step(small, _, carry):
        for k in range(tiles):
            below = cur = get(k, 0)
            pair = None
            for z in range(cz):
                above = get(k, z + 1) if z + 1 < cz else cur
                if pair is None:
                    pair = [c + a for c, a in zip(cur, above)]
                    column = [p + b for p, b in zip(pair, below)]
                else:
                    column = [p + a for p, a in zip(pair, above)]
                    pair = None
                ea = row_at(east_ref, z, k)
                we = row_at(west_ref, z, k)
                move = row_at(scale_ref if small else shift_ref, z, k)
                ring = [d_ref[k, z, pl.ds(last + SUB - 1, SUB), :]] + cur
                ring = ring + [d_ref[k, z, pl.ds(1, SUB), :]]
                for i in range(groups):
                    new = (
                        mix_vertical * column[i]
                        + ea * ring[i + 2]
                        + we * ring[i]
                        - drain * moved_softplus2(small, cur[i], move)
                    )
                    put(k, z, i, new)
                below, cur = cur, above
        return carry

    def finish(small):
        lax.fori_loop(0, SUBSTEPS, functools.partial(step, small), 0)
        head, rows = return_shape(cz, per)
        cloud_ref = east_ref
        early = [None] * tiles

        def sums(k):
            for z in range(cz):
                total = cloud = None
                move = row_at(scale_ref if small else shift_ref, z, k)
                for c in moved_sum(small, get(k, z), move):
                    cloud = c if cloud is None else cloud + c
                for f in get(k, z):
                    total = f if total is None else total + f
                part_ref[2 * k, pl.ds(z * SUB, SUB), :] = total
                part_ref[2 * k + 1, pl.ds(z * SUB, SUB), :] = cloud

        def known(k):
            early[k] = dot3(
                split(value_ref[:, lanes(k)]), (early_high_ref[...], early_low_ref[...]), 0, 0
            )

        def ends_part():
            if carry:
                halo = halo_part(devices, r_ref, ends_ref, v_ref)
                halo_ref[...] = halo + dot(gain_ref[...], halo, 1, 0, HI)

        def close(k):
            moved = LN2 * shift_ref[:, lanes(k)]
            end = fold(part_ref.at[2 * k], zp, LN2 / cx) - moved
            cloud = fold(part_ref.at[2 * k + 1], zp, LN2 / cx) - moved
            late_ref[0:zp, lanes(k)] = end
            late_ref[zp:, lanes(k)] = cloud[0:head]
            cloud_ref[:, lanes(k)] = cloud
            late = dot3(split(late_ref[:, lanes(k)]), (late_high_ref[...], late_low_ref[...]), 0, 0)
            main = early[k] + late
            for h in range(LANE // per):
                out_ref[pl.ds((k * (LANE // per) + h) * rows, per), :] = main[h * per:(h + 1) * per]

        for k in range(tiles):
            sums(k)
            if k == 0:
                for n in range(tiles):
                    known(n)
            if k == 1:
                ends_part()
            close(k)
        left = cloud_ref[head:, :]
        left = jnp.concatenate([left, jnp.zeros((SLOT - left.shape[0], cols), jnp.float32)], axis=0) \
            if left.shape[0] < SLOT else left
        place = lax.broadcasted_iota(jnp.int32, (1, cols), 1)
        part = place % per % SLOTS
        spread = jnp.concatenate(
            [jnp.where(part == j, left, 0.0) for j in range(SLOTS)], axis=0
        )
        pick = slot_onehot(place, devices, per, cols)
        a, b = split(spread)
        extra = dot(pick, a, 1, 1) + dot(pick, b, 1, 1)
        for i in range(rows - per):
            out_ref[pl.ds(per + i, devices, stride=rows), :] = extra[i * devices:(i + 1) * devices]

    @pl.when(bound < LARGEST)
    def _():
        finish(True)

    @pl.when(jnp.logical_not(bound < LARGEST))
    def _():
        finish(False)


def base_kernel(devices, carry, *refs):
    pos_ref = refs[6]
    low_ref, high_ref = (None, None) if carry else refs[7:9]
    to_ref, qo_ref, level_high_ref, level_low_ref, rest_high_ref, rest_low_ref = refs[-16:-10]
    sel_ref, pick_ref, gain_ref = refs[-10:-7]
    t_ref, q_ref, v_ref, down_ref, up_ref, lin_ref, sem = refs[-7:]
    copies = fetch(refs[:6], refs[-7:-1], sem)
    nl, cols = t_ref.shape
    cz = up_ref.shape[0]
    per = cols // devices
    head, _ = return_shape(cz, per)
    sel_ref[...] = onehot(pos_ref[...], cols)
    pick_ref[...] = slot_onehot(pos_ref[...], devices, per, cols)
    for copy in copies:
        copy.wait()
    up = up_ref[...].T
    wide = jnp.concatenate([up, jnp.zeros((nl, LANE - cz), jnp.float32)], axis=1)
    lane = lax.broadcasted_iota(jnp.int32, wide.shape, 1)
    level = jnp.concatenate(
        [
            wide,
            -pltpu.roll(wide, cz, 1),
            pltpu.roll(jnp.where(lane < head, wide, 0.0), 2 * cz, 1),
        ],
        axis=0,
    )
    level_high_ref[...], level_low_ref[...] = split(level)
    rest = jnp.where(lane < SLOT, pltpu.roll(wide, LANE - head, 1), 0.0)
    rest_high_ref[...], rest_low_ref[...] = split(rest[:, 0:SLOT])
    if carry:
        low = high = (jnp.zeros((nl, 1), jnp.float32),) * 2
    else:
        low = (low_ref[0], low_ref[1])
        high = (high_ref[0], high_ref[1])
    v = v_ref[...]
    t = t_ref[...]
    q = q_ref[...]
    advt = advection(t, v, low[0], high[0])
    advq = advection(q, v, low[1], high[1])
    prof = dot(down_ref[...], jnp.concatenate([t, q, advt, advq], axis=1), 1, 0, HI)
    lin = lin_ref[...]
    gain = dot(lin[0], prof[:, :2 * cols], 1, 0, HI) + dot(lin[1], prof[:, 2 * cols:], 1, 0, HI)
    gain = dot(up, gain, 1, 0, HI)
    to_ref[...] = t + advt + gain[:, :cols]
    qo_ref[...] = q + advq + gain[:, cols:]
    gain_ref[...] = dot(up, dot(lin[1], down_ref[...], 1, 0, HI), 1, 0, HI)


def ends_pick():
    pick = np.zeros((2 * SUB, 2 * LANE))
    for r, (field, half, end) in enumerate(CARRIED):
        row = r + (0 if end else SUB)
        place = half * LANE + (0 if end else 1)
        if field:
            pick[row, place] = 1.0
        pick[row, place + 2] = 0.5 if field else 1.0
    return pick


def halo_part(devices, r_ref, ends_ref, v_ref):
    nl, cols = v_ref.shape
    per = cols // devices
    first, second = halves(nl)
    me = lax.axis_index(AXES)

    def block(device):
        start = pl.multiple_of(device * per, SUB)
        return r_ref[pl.ds(start, SUB), :]

    rows = jnp.concatenate(
        [block(lax.rem(me + devices - 1, devices)), block(lax.rem(me + 1, devices))], axis=0
    )
    rows = pltpu.roll(rows, rows.shape[1] - 3 * nl, 1)[:, :LANE]
    a, b = split(rows)
    pick = ends_ref[...]
    part = dot(a, pick, 0, 0) + dot(b, pick, 0, 0)
    ends = jnp.concatenate([part[:first, :LANE], part[:second, LANE:]], axis=0)
    lane = lax.broadcasted_iota(jnp.int32, ends.shape, 1)
    low = v_ref[:, :LANE]
    high = v_ref[:, cols - LANE:]
    v = jnp.where(
        lane == 0, low, jnp.where(lane == 2, pltpu.roll(low, 2, 1), jnp.where(
            lane == 1, -pltpu.roll(high, 2, 1), -pltpu.roll(high, 4, 1)))
    )
    return (loop_diff + 0.5 * v) * ends


def add_ends(field_ref, out_ref, extra, halo, place):
    cols = field_ref.shape[1]
    lane = lax.broadcasted_iota(jnp.int32, halo.shape, 1)
    start = pltpu.roll(halo, LANE - place, 1) if place else halo
    stop = pltpu.roll(halo, LANE - 2 - place, 1)
    parts = [extra[:, k:k + LANE] for k in range(0, cols, LANE)]
    parts[0] = parts[0] + jnp.where(lane == 0, start, 0.0)
    parts[-1] = parts[-1] + jnp.where(lane == LANE - 1, stop, 0.0)
    for k, part in enumerate(parts):
        out_ref[:, lanes(k)] = field_ref[:, lanes(k)] + part


def finish_kernel(devices, carry, *refs):
    r_ref, pos_ref, tb_ref, qb_ref = refs[:4]
    level_high_ref, level_low_ref, rest_high_ref, rest_low_ref, sel_ref, pick_ref = refs[4:10]
    to_ref, qo_ref, co_ref = refs[-3:]
    nl, cols = tb_ref.shape
    per = cols // devices
    rows = r_ref.shape[0] // devices
    main = jnp.concatenate([r_ref[pl.ds(h * rows, per), :] for h in range(devices)], axis=0)
    extra = jnp.concatenate(
        [r_ref[pl.ds(per + i, devices, stride=rows), :] for i in range(rows - per)], axis=0
    )
    a, b = split(extra)
    extra = dot(a, pick_ref[...], 0, 0) + dot(b, pick_ref[...], 0, 0)
    part = pos_ref[...] % per % SLOTS
    left = jnp.where(part == 0, extra[:SLOT], 0.0)
    for j in range(1, SLOTS):
        left = left + jnp.where(part == j, extra[j * SLOT:(j + 1) * SLOT], 0.0)
    rest = dot3((rest_high_ref[...], rest_low_ref[...]), split(left), 1, 0)
    a, b = split(dot3((level_high_ref[...], level_low_ref[...]), split(main), 1, 1))
    out = dot(a, sel_ref[...], 1, 0) + dot(b, sel_ref[...], 1, 0)
    if carry:
        halo = refs[10][...]
        add_ends(tb_ref, to_ref, out[0:nl], halo, 0)
        add_ends(qb_ref, qo_ref, out[nl:2 * nl], halo, 2)
    else:
        to_ref[...] = tb_ref[...] + out[0:nl]
        qo_ref[...] = qb_ref[...] + out[nl:2 * nl]
    co_ref[...] = out[2 * nl:3 * nl] + rest


def local(
    thermal_anomaly,
    vapour_anomaly,
    periodic_flow_velocity,
    processor_assignment,
    thermal_disturbance,
    layer_index_downscale,
    layer_index_upscale,
):
    nl, cols = thermal_anomaly.shape
    cz, cx, _ = thermal_disturbance.shape
    devices = lax.axis_size(AXES)
    per = cols // devices
    zp = up_to(cz, SUB)
    f32 = jnp.float32
    width = up_to(3 * nl, LANE)
    head, rows = return_shape(cz, per)
    field = jax.ShapeDtypeStruct((nl, cols), f32)
    carry = carries(nl, per, width)

    fields = (thermal_anomaly, vapour_anomaly, periodic_flow_velocity)
    ends = () if carry else edges(jnp.stack(fields[:2]))
    out, pos = pl.pallas_call(
        functools.partial(pack_kernel, devices, carry),
        out_shape=(
            jax.ShapeDtypeStruct((cols, width), f32),
            jax.ShapeDtypeStruct((1, cols), jnp.int32),
        ),
        in_specs=[HBM] * 4 + [VMEM] * len(ends),
        out_specs=(VMEM,) * 2,
        scratch_shapes=[
            pltpu.VMEM((width, cols), f32),
            pltpu.VMEM((nl, cols), f32),
            pltpu.VMEM((nl, cols), f32),
            pltpu.VMEM((nl, cols), f32),
            pltpu.VMEM((1, cols), jnp.int32),
            pltpu.SemaphoreType.DMA((4,)),
        ],
        compiler_params=pltpu.CompilerParams(vmem_limit_bytes=VMEM_PACK),
        name="pack",
    )(*[in_hbm(f) for f in (*fields, processor_assignment.reshape(1, cols))], *ends)

    def exchange(blocks, *inner):
        shape = blocks.shape
        blocks = blocks.reshape(devices, *inner)
        return lax.all_to_all(blocks, AXES, split_axis=0, concat_axis=0, tiled=True).reshape(shape)

    r1 = exchange(out, per, width)

    power, total = mean_operators(cz)
    release = 1.0 + 0.5 * latent_heat
    shift, unshift = shift_operators(cz)
    mean = np.zeros((4 * zp + head, LANE))
    z_part = np.zeros((4 * zp + head, cz))
    z_part[zp:zp + cz] = power.T / release
    z_part[2 * zp:2 * zp + cz] = (total @ unshift).T / release
    z_part[3 * zp:3 * zp + cz] = -np.eye(cz) / release
    mean[0:cz, 0:cz] = power.T
    mean[:, 0:cz] += latent_heat * z_part
    mean[:, cz:2 * cz] = z_part
    mean[4 * zp:, 2 * cz:2 * cz + head] = np.eye(head)

    tiles = cols // LANE
    groups = cx // SUB
    level_rows = 3 * zp + (nl + halves(nl)[0] if carry else 0)
    bf16 = jnp.bfloat16
    prep = pl.pallas_call(
        functools.partial(prep_kernel, carry),
        out_shape=(
            jax.ShapeDtypeStruct((tiles, cz, cx, LANE), f32),
            jax.ShapeDtypeStruct((zp, cols), f32),
            jax.ShapeDtypeStruct((SUB, LANE), f32),
            jax.ShapeDtypeStruct((level_rows, width), bf16),
            jax.ShapeDtypeStruct((3 * zp, width), bf16),
            jax.ShapeDtypeStruct((zp, nl), bf16),
            jax.ShapeDtypeStruct((zp, nl), bf16),
        ),
        in_specs=[HBM, HBM, HBM, VMEM],
        out_specs=(VMEM,) * 7,
        scratch_shapes=[
            pltpu.VMEM((tiles, cz, cx, LANE), f32),
            pltpu.VMEM((tiles, zp * SUB, LANE), f32),
            pltpu.VMEM((cz, nl), f32),
            pltpu.VMEM((cz, cz), f32),
            pltpu.SemaphoreType.DMA((tiles, 5)),
            pltpu.SemaphoreType.DMA((2,)),
        ],
        compiler_params=pltpu.CompilerParams(vmem_limit_bytes=VMEM_PACK),
        cost_estimate=pl.CostEstimate(flops=10**8, bytes_accessed=4 * 10**6, transcendentals=0),
        name="prep",
    )(
        in_hbm(thermal_disturbance),
        in_hbm(layer_index_downscale),
        in_hbm(jnp.asarray(shift, f32)),
        pos,
    )
    lin = np.stack([power - np.eye(cz), total])
    *base, gain = pl.pallas_call(
        functools.partial(base_kernel, devices, carry),
        out_shape=(
            field,
            field,
            jax.ShapeDtypeStruct((3 * nl, LANE), bf16),
            jax.ShapeDtypeStruct((3 * nl, LANE), bf16),
            jax.ShapeDtypeStruct((nl, SLOT), bf16),
            jax.ShapeDtypeStruct((nl, SLOT), bf16),
            jax.ShapeDtypeStruct((cols, cols), bf16),
            jax.ShapeDtypeStruct((devices * (rows - per), cols), bf16),
            jax.ShapeDtypeStruct((nl, nl), f32),
        ),
        in_specs=[HBM] * 6 + [VMEM] * (1 + len(ends)),
        out_specs=(VMEM,) * 9,
        scratch_shapes=[
            pltpu.VMEM((nl, cols), f32),
            pltpu.VMEM((nl, cols), f32),
            pltpu.VMEM((nl, cols), f32),
            pltpu.VMEM((cz, nl), f32),
            pltpu.VMEM((cz, nl), f32),
            pltpu.VMEM((2, cz, cz), f32),
            pltpu.SemaphoreType.DMA((6,)),
        ],
        compiler_params=pltpu.CompilerParams(vmem_limit_bytes=VMEM_PACK),
        cost_estimate=pl.CostEstimate(flops=10**8, bytes_accessed=10**6, transcendentals=0),
        name="base",
    )(
        *[
            in_hbm(x)
            for x in (
                *fields,
                layer_index_downscale,
                layer_index_upscale.T,
                jnp.asarray(lin, f32),
            )
        ],
        pos,
        *ends,
    )
    halo = (periodic_flow_velocity, jnp.asarray(ends_pick(), bf16)) if carry else ()
    vals, *halo = pl.pallas_call(
        functools.partial(cloud_kernel, devices, carry, nl),
        out_shape=(jax.ShapeDtypeStruct((devices * rows, LANE), f32),)
        + ((jax.ShapeDtypeStruct((nl, LANE), f32),) if carry else ()),
        in_specs=[VMEM] * (13 + len(halo)),
        out_specs=(VMEM,) * (2 if carry else 1),
        scratch_shapes=[
            pltpu.VMEM((tiles, cz, SUB * (groups + 2), LANE), f32),
            pltpu.VMEM((zp, cols), f32),
            pltpu.VMEM((zp, cols), f32),
            pltpu.VMEM((zp, cols), f32),
            pltpu.VMEM((zp, cols), f32),
            pltpu.VMEM((zp, cols), f32),
            pltpu.VMEM((zp + head, cols), f32),
            pltpu.VMEM((3 * zp, cols), f32),
            pltpu.VMEM((2 * tiles, zp * SUB, LANE), f32),
        ],
        compiler_params=pltpu.CompilerParams(vmem_limit_bytes=VMEM_CLOUD),
        name="cloud",
    )(r1, *prep, *halved(mean[:3 * zp]), *halved(mean[3 * zp:]), gain, *halo)
    r2 = exchange(vals, 1, rows * LANE)
    return pl.pallas_call(
        functools.partial(finish_kernel, devices, carry),
        out_shape=(field,) * 3,
        in_specs=[VMEM] * (10 + len(halo)),
        out_specs=(VMEM,) * 3,
        compiler_params=pltpu.CompilerParams(vmem_limit_bytes=VMEM_PACK),
        name="finish",
    )(r2, pos, *base, *halo)


VMEM_PACK = 16 * 2**20
VMEM_CLOUD = 24 * 2**20


def solution(mesh):
    in_specs = (
        P(None, AXES),
        P(None, AXES),
        P(None, AXES),
        P(AXES),
        P(None, None, AXES),
        P(),
        P(),
    )
    out_specs = (P(None, AXES), P(None, AXES), P(None, AXES))
    return jax.shard_map(local, mesh=mesh, in_specs=in_specs, out_specs=out_specs, check_vma=False)
```

```python
import functools

import numpy as np

import jax
import jax.numpy as jnp
from jax import lax
from jax.experimental import pallas as pl
from jax.experimental.pallas import tpu as pltpu
from jax.sharding import PartitionSpec as P

SUBSTEPS = 10

loop_diff = 0.35
mix_along = 0.35
mix_vertical = 0.1
cond_rate = 0.1
latent_heat = 1.5
max_speed = 0.8

AXES = ("tile", "crm")
LOG2E = 1.4426950408889634
LN2 = 0.6931471805599453
SUB = 8
LANE = 128
HI = lax.Precision.HIGH
VMEM = pl.BlockSpec(memory_space=pltpu.VMEM)
HBM = pl.BlockSpec(memory_space=pltpu.HBM)


def in_hbm(x):
    return pltpu.with_memory_space_constraint(x, pltpu.HBM)


def fetch(sources, targets, sem):
    copies = [
        pltpu.make_async_copy(a, b, sem.at[n]) for n, (a, b) in enumerate(zip(sources, targets))
    ]
    for copy in copies:
        copy.start()
    return copies


def up_to(n, m):
    return -(-n // m) * m


def edges(block):
    count = lax.axis_size(AXES)
    forward = [(i, (i + 1) % count) for i in range(count)]
    backward = [(t, s) for s, t in forward]
    low = lax.ppermute(block[:, :, -1:], AXES, forward)
    high = lax.ppermute(block[:, :, :1], AXES, backward)
    return low, high


def ring_mean_operator(levels):
    f = np.eye(levels)
    east = west = f
    above = np.concatenate([f[1:], f[-1:]], axis=0)
    below = np.concatenate([f[:1], f[:-1]], axis=0)
    return (
        f
        + mix_along * (east - 2.0 * f + west)
        + mix_vertical * (above - 2.0 * f + below)
    )


def mean_operators(levels):
    v = ring_mean_operator(levels)
    power = np.eye(levels)
    total = np.zeros((levels, levels))
    for _ in range(SUBSTEPS):
        total = total + power
        power = v @ power
    return power, total / SUBSTEPS


def shift_operators(levels):
    drain = cond_rate * (1.0 + 0.5 * latent_heat)
    rest = (1.0 + drain) * np.eye(levels) - ring_mean_operator(levels)
    scale = LOG2E / SUBSTEPS
    return -np.linalg.inv(rest) * scale, -rest / scale


def halved(x):
    a = np.asarray(x, jnp.bfloat16)
    b = np.asarray(x - a.astype(np.float64), jnp.bfloat16)
    return jnp.asarray(a), jnp.asarray(b)


def split(x):
    a = x.astype(jnp.bfloat16)
    return a, (x - a.astype(jnp.float32)).astype(jnp.bfloat16)


def dot3(a, b, ca, cb):
    return dot(a[0], b[0], ca, cb) + dot(a[0], b[1], ca, cb) + dot(a[1], b[0], ca, cb)


def dot(a, b, ca, cb, precision=None):
    return lax.dot_general(
        a, b, (((ca,), (cb,)), ((), ())), precision=precision, preferred_element_type=jnp.float32
    )


def advection(f, v, low, high):
    cols = f.shape[1]
    lane = lax.broadcasted_iota(jnp.int32, f.shape, 1)
    ahead = jnp.where(lane == cols - 1, high, pltpu.roll(f, cols - 1, 1))
    behind = jnp.where(lane == 0, low, pltpu.roll(f, 1, 1))
    return -v * (ahead - behind) * 0.5 + loop_diff * (ahead - 2.0 * f + behind)


def onehot(pos_row, cols):
    place = lax.broadcasted_iota(jnp.int32, (cols, cols), 0)
    return jnp.where(place == pos_row, 1.0, 0.0).astype(jnp.bfloat16)


SLOT = 32
SLOTS = LANE // SLOT


def return_shape(cz, per):
    head = (LANE - 2 * cz) // SUB * SUB
    assert 0 <= head <= cz and cz - head <= SLOT
    return head, per + -(-per // SLOTS)


def slot_onehot(place_row, devices, per, cols):
    row = place_row % per // SLOTS * devices + place_row // per
    rows = -(-per // SLOTS) * devices
    return jnp.where(
        lax.broadcasted_iota(jnp.int32, (rows, cols), 0) == row, 1.0, 0.0
    ).astype(jnp.bfloat16)


CARRIED = (
    (0, 1, 0), (0, 0, 0), (0, 0, 1), (0, 1, 1),
    (1, 0, 0), (1, 1, 0), (1, 0, 1), (1, 1, 1),
)


def row_of(field, half, end):
    return CARRIED.index((field, half, end))


def halves(levels):
    first = up_to(-(-levels // 2), SUB)
    return first, levels - first


def carries(levels, per, width):
    first, second = halves(levels)
    return per >= len(CARRIED) and 3 * levels + first <= width and second < first


def pack_kernel(devices, carry, *refs):
    low_ref, high_ref = (None, None) if carry else refs[4:6]
    out_ref, pos_ref, s_ref, t_ref, q_ref, v_ref, own_ref, sem = refs[-8:]
    copies = [
        pltpu.make_async_copy(source, target, sem.at[n])
        for n, (source, target) in enumerate(zip(refs[:4], (t_ref, q_ref, v_ref, own_ref)))
    ]
    for n in (3, 0, 1, 2):
        copies[n].start()
    nl, cols = t_ref.shape
    width = s_ref.shape[0]
    per = cols // devices
    copies[3].wait()
    own = own_ref[...]
    who = lax.broadcasted_iota(jnp.int32, (devices, cols), 0)
    mine = jnp.where(who == own, 1.0, 0.0)
    before = lax.broadcasted_iota(jnp.int32, (cols, cols), 0) < lax.broadcasted_iota(
        jnp.int32, (cols, cols), 1
    )
    tri = jnp.where(before, 1.0, 0.0).astype(jnp.bfloat16)
    ranks = dot(mine.astype(jnp.bfloat16), tri, 1, 0)
    rank = jnp.sum(ranks * mine, axis=0, keepdims=True)
    pos = own * per + rank.astype(jnp.int32)
    pos_ref[...] = pos
    sel = onehot(pos, cols)

    for n in range(3):
        copies[n].wait()
    t = t_ref[...]
    x = q_ref[...] - 0.5 * t
    v = v_ref[...]
    if carry:
        low = high = jnp.zeros((nl, 1), jnp.float32)
    else:
        low = low_ref[1] - 0.5 * low_ref[0]
        high = high_ref[1] - 0.5 * high_ref[0]
    s_ref[0:nl, :] = x
    s_ref[nl:2 * nl, :] = v
    s_ref[2 * nl:3 * nl, :] = advection(x, v, low, high)
    rest = width - 3 * nl
    if rest:
        s_ref[3 * nl:, :] = jnp.zeros((rest, cols), jnp.float32)
    if carry:
        first, second = halves(nl)
        lane = lax.broadcasted_iota(jnp.int32, (1, cols), 1)
        s_ref[3 * nl + second:3 * nl + second + 1, :] = jnp.where(
            (lane == 0) | (lane == cols - 1), 1.0, 0.0
        )
    a, b = split(s_ref[...])
    out = dot(sel, a, 1, 1) + dot(sel, b, 1, 1)
    if carry:
        fill = jnp.zeros((first - second, cols), jnp.float32)
        parts = []
        for f in (x, t):
            parts += [f[:first], jnp.concatenate([f[first:], fill], axis=0)]
        parts = jnp.concatenate(parts, axis=1)
        shape = (SUB, parts.shape[1])
        want = jnp.full(shape, -1, jnp.int32)
        row = lax.broadcasted_iota(jnp.int32, shape, 0)
        for r, (field, half, end) in enumerate(CARRIED):
            want = jnp.where(row == r, (2 * field + half) * cols + end * (cols - 1), want)
        pick = jnp.where(lax.broadcasted_iota(jnp.int32, shape, 1) == want, 1.0, 0.0).astype(
            jnp.bfloat16
        )
        a, b = split(parts)
        ends = dot(pick, a, 1, 1) + dot(pick, b, 1, 1)
        ends = jnp.concatenate([ends, jnp.zeros((SUB, width - first), jnp.float32)], axis=1)
        ends = pltpu.roll(ends, 3 * nl, 1)
        out = (out.reshape(devices, per, width) + ends[None]).reshape(cols, width)
    out_ref[...] = out


LARGEST = 60.0


def moved_softplus2(small, g, move):
    if small:
        return jnp.log2(move + jnp.exp2(g))
    return move + softplus2(g - move)


def moved_sum(small, parts, move):
    if not small:
        return [moved_softplus2(small, g, move) for g in parts]
    powers = [move + jnp.exp2(g) for g in parts]
    pairs = [a * b for a, b in zip(powers[::2], powers[1::2])] + powers[len(powers) // 2 * 2:]
    return [jnp.log2(p) for p in pairs]


def softplus2(f):
    return jnp.maximum(f, jnp.log2(1.0 + jnp.exp2(jnp.minimum(f, 100.0))))


def lanes(k):
    return pl.ds(k * LANE, LANE)


def fold(part_ref, levels, scale):
    total = part_ref[pl.ds(0, levels, stride=SUB), :]
    for s in range(1, SUB):
        total = total + part_ref[pl.ds(s, levels, stride=SUB), :]
    return total * scale


def clear_tail(part_ref, cz):
    for n in range(part_ref.shape[0]):
        for z in range(cz * SUB, part_ref.shape[1], SUB):
            part_ref[n, pl.ds(z, SUB), :] = jnp.zeros((SUB, LANE), jnp.float32)


def prep_kernel(carry, td_ref, down_hbm, shift_hbm, after_ref, start_ref, mean_ref, most_ref,
                high_ref, low_ref, shift_high_ref, shift_low_ref, raw_ref, part_ref, down_ref,
                shift_ref, td_sem, sem):
    del after_ref
    cz, cx, cols = td_ref.shape
    nl = down_ref.shape[1]
    zp = mean_ref.shape[0]
    width = high_ref.shape[1]
    groups = cx // SUB
    tiles = cols // LANE
    chunk = -(-cz // td_sem.shape[1])

    def td_copy(k, c):
        levels = pl.ds(c * chunk, min(chunk, cz - c * chunk))
        return pltpu.make_async_copy(
            td_ref.at[levels, :, lanes(k)], raw_ref.at[k, levels], td_sem.at[k, c]
        )

    copies = fetch((down_hbm, shift_hbm), (down_ref, shift_ref), sem)
    for k in range(tiles):
        for c in range(td_sem.shape[1]):
            td_copy(k, c).start()
    for copy in copies:
        copy.wait()

    def wide(rows):
        rows = jnp.concatenate(
            [rows, jnp.zeros((rows.shape[0], width - nl), jnp.float32)], axis=1
        )
        return jnp.concatenate([rows, jnp.zeros((zp - cz, width), jnp.float32)], axis=0)

    down = wide(down_ref[...])
    shift = wide(dot(shift_ref[...], down_ref[...], 1, 0, lax.Precision.HIGHEST))
    blocks = jnp.concatenate(
        [down, pltpu.roll(down, nl, 1), pltpu.roll(shift, 2 * nl, 1)], axis=0
    )
    a, low_ref[...] = split(blocks)
    offset = high_ref.shape[0] - 3 * zp
    if carry:
        shape = (offset, width)
        row = lax.broadcasted_iota(jnp.int32, shape, 0)
        to = jnp.where(row < nl, row + nl, row + 2 * nl)
        high_ref[0:offset, :] = jnp.where(
            lax.broadcasted_iota(jnp.int32, shape, 1) == to, 1.0, 0.0
        ).astype(jnp.bfloat16)
    high_ref[offset:, :] = a
    shift_high_ref[...], shift_low_ref[...] = split(shift[:, :nl])

    clear_tail(part_ref, cz)
    most = [jnp.zeros((SUB, LANE), jnp.float32)] * groups
    for k in range(tiles):
        for z in range(cz):
            if z % chunk == 0:
                td_copy(k, z // chunk).wait()
            total = None
            for i in range(groups):
                td = raw_ref[k, z, pl.ds(i, SUB, stride=groups), :]
                total = td if total is None else total + td
                first = (-0.5 * LOG2E) * td
                start_ref[k, z, pl.ds(SUB * i, SUB), :] = first
                most[i] = jnp.maximum(most[i], jnp.abs(first))
            part_ref[k, pl.ds(z * SUB, SUB), :] = total
        mean_ref[:, lanes(k)] = fold(part_ref.at[k], zp, 1.0 / cx)
    most_ref[...] = functools.reduce(jnp.maximum, most)


def cloud_kernel(devices, carry, nl, r_ref, start_ref, td_mean_ref, most_ref, g_high_ref, g_low_ref,
                 shift_high_ref, shift_low_ref, early_high_ref, early_low_ref,
                 late_high_ref, late_low_ref, after_ref, *refs):
    gain_ref, v_ref, ends_ref = (after_ref, *refs[:2]) if carry else (None,) * 3
    out_ref, halo_ref = refs[2:4] if carry else (refs[0], None)
    d_ref, base_ref, east_ref, west_ref, shift_ref, scale_ref, late_ref, value_ref, part_ref = (
        refs[-9:]
    )
    tiles, cz, cx, _ = start_ref.shape
    zp, cols = td_mean_ref.shape
    per = cols // devices
    groups = cx // SUB

    r = split(r_ref[...])
    offset = g_high_ref.shape[0] - 3 * zp
    prof = dot(g_high_ref[...], r[0], 1, 1) + dot(g_high_ref[...], r[1], 1, 1)
    fine = dot(g_low_ref[...], r[0], 1, 1)
    shift = prof[offset + 2 * zp:] + fine[2 * zp:]
    if carry:
        first, second = halves(nl)
        v = prof[0:nl]
        ends = prof[nl:offset]
        flag = ends[second:second + 1] > 0.5
        place = lax.rem(lax.broadcasted_iota(jnp.int32, (1, cols), 1), per)

        def neighbour(end, at):
            step = per if at == 0 else -per
            shift = lambda half: (step + at - row_of(0, half, end)) % cols
            return jnp.concatenate(
                [pltpu.roll(ends, shift(0), 1), pltpu.roll(ends, shift(1), 1)[:second]], axis=0
            )

        behind = neighbour(1, 0) * (loop_diff + 0.5 * v)
        ahead = neighbour(0, per - 1) * (loop_diff - 0.5 * v)
        halo = jnp.where(flag & (place == 0), behind, 0.0) + jnp.where(
            flag & (place == per - 1), ahead, 0.0
        )
        shift = shift + dot3((shift_high_ref[...], shift_low_ref[...]), split(halo), 1, 0)
    d0 = prof[offset:offset + zp] + fine[0:zp]
    speed = max_speed * jnp.tanh(prof[offset + zp:offset + 2 * zp] + fine[zp:2 * zp])
    base = d0 * LOG2E + shift
    base_ref[...] = base
    east_ref[...] = mix_along - 0.5 * speed
    west_ref[...] = mix_along + 0.5 * speed
    shift_ref[...] = shift
    scale_ref[...] = jnp.exp2(shift)
    drain = cond_rate * (1.0 + 0.5 * latent_heat)
    rate = 1.0 - 2.0 * mix_along + max(2.0 * mix_along, max_speed)
    growth = rate**SUBSTEPS
    series = sum(rate**n for n in range(SUBSTEPS))
    bound = growth * (jnp.max(jnp.abs(base)) + jnp.max(most_ref[...])) + series * drain * (
        jnp.max(jnp.abs(shift)) + 1.0
    )
    value_ref[0:zp, :] = td_mean_ref[...]
    value_ref[zp:2 * zp, :] = d0 - 0.5 * td_mean_ref[...]
    value_ref[2 * zp:, :] = shift
    clear_tail(part_ref, cz)

    def row_at(ref, z, k):
        return jnp.broadcast_to(ref[pl.ds(z, 1), lanes(k)], (SUB, LANE))

    slot = [0] + [SUB * (i + 1) for i in range(1, groups)]
    last = slot[-1]

    def get(k, z):
        return [d_ref[k, z, pl.ds(slot[i], SUB), :] for i in range(groups)]

    def put(k, z, i, new):
        d_ref[k, z, pl.ds(slot[i], SUB), :] = new
        if i == 0:
            d_ref[k, z, pl.ds(SUB, SUB), :] = new
        if i == groups - 1:
            d_ref[k, z, pl.ds(last + SUB, SUB), :] = new

    for k in range(tiles):
        for z in range(cz):
            base = row_at(base_ref, z, k)
            for i in range(groups):
                put(k, z, i, base + start_ref[k, z, pl.ds(SUB * i, SUB), :])

    def step(small, _, carry):
        for k in range(tiles):
            below = cur = get(k, 0)
            pair = None
            for z in range(cz):
                above = get(k, z + 1) if z + 1 < cz else cur
                if pair is None:
                    pair = [c + a for c, a in zip(cur, above)]
                    column = [p + b for p, b in zip(pair, below)]
                else:
                    column = [p + a for p, a in zip(pair, above)]
                    pair = None
                ea = row_at(east_ref, z, k)
                we = row_at(west_ref, z, k)
                move = row_at(scale_ref if small else shift_ref, z, k)
                ring = [d_ref[k, z, pl.ds(last + SUB - 1, SUB), :]] + cur
                ring = ring + [d_ref[k, z, pl.ds(1, SUB), :]]
                for i in range(groups):
                    new = (
                        mix_vertical * column[i]
                        + ea * ring[i + 2]
                        + we * ring[i]
                        - drain * moved_softplus2(small, cur[i], move)
                    )
                    put(k, z, i, new)
                below, cur = cur, above
        return carry

    def finish(small):
        lax.fori_loop(0, SUBSTEPS, functools.partial(step, small), 0)
        head, rows = return_shape(cz, per)
        cloud_ref = east_ref
        early = [None] * tiles

        def sums(k):
            for z in range(cz):
                total = cloud = None
                move = row_at(scale_ref if small else shift_ref, z, k)
                for c in moved_sum(small, get(k, z), move):
                    cloud = c if cloud is None else cloud + c
                for f in get(k, z):
                    total = f if total is None else total + f
                part_ref[2 * k, pl.ds(z * SUB, SUB), :] = total
                part_ref[2 * k + 1, pl.ds(z * SUB, SUB), :] = cloud

        def known(k):
            early[k] = dot3(
                split(value_ref[:, lanes(k)]), (early_high_ref[...], early_low_ref[...]), 0, 0
            )

        def ends_part():
            if carry:
                halo = halo_part(devices, r_ref, ends_ref, v_ref)
                halo_ref[...] = halo + dot(gain_ref[...], halo, 1, 0, HI)

        def close(k):
            moved = LN2 * shift_ref[:, lanes(k)]
            end = fold(part_ref.at[2 * k], zp, LN2 / cx) - moved
            cloud = fold(part_ref.at[2 * k + 1], zp, LN2 / cx) - moved
            late_ref[0:zp, lanes(k)] = end
            late_ref[zp:, lanes(k)] = cloud[0:head]
            cloud_ref[:, lanes(k)] = cloud
            late = dot3(split(late_ref[:, lanes(k)]), (late_high_ref[...], late_low_ref[...]), 0, 0)
            main = early[k] + late
            for h in range(LANE // per):
                out_ref[pl.ds((k * (LANE // per) + h) * rows, per), :] = main[h * per:(h + 1) * per]

        for k in range(tiles):
            sums(k)
            if k == 0:
                for n in range(tiles):
                    known(n)
            if k == 1:
                ends_part()
            close(k)
        left = cloud_ref[head:, :]
        left = jnp.concatenate([left, jnp.zeros((SLOT - left.shape[0], cols), jnp.float32)], axis=0) \
            if left.shape[0] < SLOT else left
        place = lax.broadcasted_iota(jnp.int32, (1, cols), 1)
        part = place % per % SLOTS
        spread = jnp.concatenate(
            [jnp.where(part == j, left, 0.0) for j in range(SLOTS)], axis=0
        )
        pick = slot_onehot(place, devices, per, cols)
        a, b = split(spread)
        extra = dot(pick, a, 1, 1) + dot(pick, b, 1, 1)
        for i in range(rows - per):
            out_ref[pl.ds(per + i, devices, stride=rows), :] = extra[i * devices:(i + 1) * devices]

    @pl.when(bound < LARGEST)
    def _():
        finish(True)

    @pl.when(jnp.logical_not(bound < LARGEST))
    def _():
        finish(False)


def base_kernel(devices, carry, *refs):
    pos_ref = refs[6]
    low_ref, high_ref = (None, None) if carry else refs[7:9]
    to_ref, qo_ref, level_high_ref, level_low_ref = refs[-14:-10]
    sel_ref, pick_ref, gain_ref = refs[-10:-7]
    t_ref, q_ref, v_ref, down_ref, up_ref, lin_ref, sem = refs[-7:]
    copies = fetch(refs[:6], refs[-7:-1], sem)
    nl, cols = t_ref.shape
    cz = up_ref.shape[0]
    per = cols // devices
    head, _ = return_shape(cz, per)
    sel_ref[...] = onehot(pos_ref[...], cols)
    pick_ref[...] = slot_onehot(pos_ref[...], devices, per, cols)
    for copy in copies:
        copy.wait()
    up = up_ref[...].T
    wide = jnp.concatenate([up, jnp.zeros((nl, LANE - cz), jnp.float32)], axis=1)
    lane = lax.broadcasted_iota(jnp.int32, wide.shape, 1)
    level = jnp.concatenate(
        [
            wide,
            -pltpu.roll(wide, cz, 1),
            pltpu.roll(jnp.where(lane < head, wide, 0.0), 2 * cz, 1),
        ],
        axis=0,
    )
    rest = jnp.where(lane < SLOT, pltpu.roll(wide, LANE - head, 1), 0.0)[:, 0:SLOT]
    rest = jnp.concatenate([jnp.zeros((2 * nl, SLOT), jnp.float32), rest], axis=0)
    level_high_ref[...], level_low_ref[...] = split(jnp.concatenate([level, rest], axis=1))
    if carry:
        low = high = (jnp.zeros((nl, 1), jnp.float32),) * 2
    else:
        low = (low_ref[0], low_ref[1])
        high = (high_ref[0], high_ref[1])
    v = v_ref[...]
    t = t_ref[...]
    q = q_ref[...]
    advt = advection(t, v, low[0], high[0])
    advq = advection(q, v, low[1], high[1])
    prof = dot(down_ref[...], jnp.concatenate([t, q, advt, advq], axis=1), 1, 0, HI)
    lin = lin_ref[...]
    gain = dot(lin[0], prof[:, :2 * cols], 1, 0, HI) + dot(lin[1], prof[:, 2 * cols:], 1, 0, HI)
    gain = dot(up, gain, 1, 0, HI)
    to_ref[...] = t + advt + gain[:, :cols]
    qo_ref[...] = q + advq + gain[:, cols:]
    gain_ref[...] = dot(up, dot(lin[1], down_ref[...], 1, 0, HI), 1, 0, HI)


def ends_pick():
    pick = np.zeros((2 * SUB, 2 * LANE))
    for r, (field, half, end) in enumerate(CARRIED):
        row = r + (0 if end else SUB)
        place = half * LANE + (0 if end else 1)
        if field:
            pick[row, place] = 1.0
        pick[row, place + 2] = 0.5 if field else 1.0
    return pick


def halo_part(devices, r_ref, ends_ref, v_ref):
    nl, cols = v_ref.shape
    per = cols // devices
    first, second = halves(nl)
    me = lax.axis_index(AXES)

    def block(device):
        start = pl.multiple_of(device * per, SUB)
        return r_ref[pl.ds(start, SUB), :]

    rows = jnp.concatenate(
        [block(lax.rem(me + devices - 1, devices)), block(lax.rem(me + 1, devices))], axis=0
    )
    rows = pltpu.roll(rows, rows.shape[1] - 3 * nl, 1)[:, :LANE]
    a, b = split(rows)
    pick = ends_ref[...]
    part = dot(a, pick, 0, 0) + dot(b, pick, 0, 0)
    ends = jnp.concatenate([part[:first, :LANE], part[:second, LANE:]], axis=0)
    lane = lax.broadcasted_iota(jnp.int32, ends.shape, 1)
    low = v_ref[:, :LANE]
    high = v_ref[:, cols - LANE:]
    v = jnp.where(
        lane == 0, low, jnp.where(lane == 2, pltpu.roll(low, 2, 1), jnp.where(
            lane == 1, -pltpu.roll(high, 2, 1), -pltpu.roll(high, 4, 1)))
    )
    return (loop_diff + 0.5 * v) * ends


def add_ends(field_ref, out_ref, extra, halo, place):
    cols = field_ref.shape[1]
    lane = lax.broadcasted_iota(jnp.int32, halo.shape, 1)
    start = pltpu.roll(halo, LANE - place, 1) if place else halo
    stop = pltpu.roll(halo, LANE - 2 - place, 1)
    parts = [extra[:, k:k + LANE] for k in range(0, cols, LANE)]
    parts[0] = parts[0] + jnp.where(lane == 0, start, 0.0)
    parts[-1] = parts[-1] + jnp.where(lane == LANE - 1, stop, 0.0)
    for k, part in enumerate(parts):
        out_ref[:, lanes(k)] = field_ref[:, lanes(k)] + part


def finish_kernel(devices, carry, *refs):
    r_ref, pos_ref, tb_ref, qb_ref = refs[:4]
    level_high_ref, level_low_ref, sel_ref, pick_ref = refs[4:8]
    to_ref, qo_ref, co_ref = refs[-3:]
    nl, cols = tb_ref.shape
    per = cols // devices
    rows = r_ref.shape[0] // devices
    main = jnp.concatenate([r_ref[pl.ds(h * rows, per), :] for h in range(devices)], axis=0)
    a, b = split(main)
    values = dot(a, sel_ref[...], 0, 0) + dot(b, sel_ref[...], 0, 0)
    extra = jnp.concatenate(
        [r_ref[pl.ds(per + i, devices, stride=rows), :] for i in range(rows - per)], axis=0
    )
    a, b = split(extra)
    extra = dot(a, pick_ref[...], 0, 0) + dot(b, pick_ref[...], 0, 0)
    part = pos_ref[...] % per % SLOTS
    left = jnp.where(part == 0, extra[:SLOT], 0.0)
    for j in range(1, SLOTS):
        left = left + jnp.where(part == j, extra[j * SLOT:(j + 1) * SLOT], 0.0)
    values = split(jnp.concatenate([values, left], axis=0))
    out = dot3((level_high_ref[...], level_low_ref[...]), values, 1, 0)
    if carry:
        halo = refs[8][...]
        add_ends(tb_ref, to_ref, out[0:nl], halo, 0)
        add_ends(qb_ref, qo_ref, out[nl:2 * nl], halo, 2)
    else:
        to_ref[...] = tb_ref[...] + out[0:nl]
        qo_ref[...] = qb_ref[...] + out[nl:2 * nl]
    co_ref[...] = out[2 * nl:3 * nl]


def local(
    thermal_anomaly,
    vapour_anomaly,
    periodic_flow_velocity,
    processor_assignment,
    thermal_disturbance,
    layer_index_downscale,
    layer_index_upscale,
):
    nl, cols = thermal_anomaly.shape
    cz, cx, _ = thermal_disturbance.shape
    devices = lax.axis_size(AXES)
    per = cols // devices
    zp = up_to(cz, SUB)
    f32 = jnp.float32
    width = up_to(3 * nl, LANE)
    head, rows = return_shape(cz, per)
    field = jax.ShapeDtypeStruct((nl, cols), f32)
    carry = carries(nl, per, width)

    fields = (thermal_anomaly, vapour_anomaly, periodic_flow_velocity)
    ends = () if carry else edges(jnp.stack(fields[:2]))
    out, pos = pl.pallas_call(
        functools.partial(pack_kernel, devices, carry),
        out_shape=(
            jax.ShapeDtypeStruct((cols, width), f32),
            jax.ShapeDtypeStruct((1, cols), jnp.int32),
        ),
        in_specs=[HBM] * 4 + [VMEM] * len(ends),
        out_specs=(VMEM,) * 2,
        scratch_shapes=[
            pltpu.VMEM((width, cols), f32),
            pltpu.VMEM((nl, cols), f32),
            pltpu.VMEM((nl, cols), f32),
            pltpu.VMEM((nl, cols), f32),
            pltpu.VMEM((1, cols), jnp.int32),
            pltpu.SemaphoreType.DMA((4,)),
        ],
        compiler_params=pltpu.CompilerParams(vmem_limit_bytes=VMEM_PACK),
        name="pack",
    )(*[in_hbm(f) for f in (*fields, processor_assignment.reshape(1, cols))], *ends)

    def exchange(blocks, *inner):
        shape = blocks.shape
        blocks = blocks.reshape(devices, *inner)
        return lax.all_to_all(blocks, AXES, split_axis=0, concat_axis=0, tiled=True).reshape(shape)

    r1 = exchange(out, per, width)

    power, total = mean_operators(cz)
    release = 1.0 + 0.5 * latent_heat
    shift, unshift = shift_operators(cz)
    mean = np.zeros((4 * zp + head, LANE))
    z_part = np.zeros((4 * zp + head, cz))
    z_part[zp:zp + cz] = power.T / release
    z_part[2 * zp:2 * zp + cz] = (total @ unshift).T / release
    z_part[3 * zp:3 * zp + cz] = -np.eye(cz) / release
    mean[0:cz, 0:cz] = power.T
    mean[:, 0:cz] += latent_heat * z_part
    mean[:, cz:2 * cz] = z_part
    mean[4 * zp:, 2 * cz:2 * cz + head] = np.eye(head)

    tiles = cols // LANE
    groups = cx // SUB
    level_rows = 3 * zp + (nl + halves(nl)[0] if carry else 0)
    bf16 = jnp.bfloat16
    prep = pl.pallas_call(
        functools.partial(prep_kernel, carry),
        out_shape=(
            jax.ShapeDtypeStruct((tiles, cz, cx, LANE), f32),
            jax.ShapeDtypeStruct((zp, cols), f32),
            jax.ShapeDtypeStruct((SUB, LANE), f32),
            jax.ShapeDtypeStruct((level_rows, width), bf16),
            jax.ShapeDtypeStruct((3 * zp, width), bf16),
            jax.ShapeDtypeStruct((zp, nl), bf16),
            jax.ShapeDtypeStruct((zp, nl), bf16),
        ),
        in_specs=[HBM, HBM, HBM, VMEM],
        out_specs=(VMEM,) * 7,
        scratch_shapes=[
            pltpu.VMEM((tiles, cz, cx, LANE), f32),
            pltpu.VMEM((tiles, zp * SUB, LANE), f32),
            pltpu.VMEM((cz, nl), f32),
            pltpu.VMEM((cz, cz), f32),
            pltpu.SemaphoreType.DMA((tiles, 5)),
            pltpu.SemaphoreType.DMA((2,)),
        ],
        compiler_params=pltpu.CompilerParams(vmem_limit_bytes=VMEM_PACK),
        cost_estimate=pl.CostEstimate(flops=10**8, bytes_accessed=4 * 10**6, transcendentals=0),
        name="prep",
    )(
        in_hbm(thermal_disturbance),
        in_hbm(layer_index_downscale),
        in_hbm(jnp.asarray(shift, f32)),
        pos,
    )
    lin = np.stack([power - np.eye(cz), total])
    *base, gain = pl.pallas_call(
        functools.partial(base_kernel, devices, carry),
        out_shape=(
            field,
            field,
            jax.ShapeDtypeStruct((3 * nl, LANE + SLOT), bf16),
            jax.ShapeDtypeStruct((3 * nl, LANE + SLOT), bf16),
            jax.ShapeDtypeStruct((cols, cols), bf16),
            jax.ShapeDtypeStruct((devices * (rows - per), cols), bf16),
            jax.ShapeDtypeStruct((nl, nl), f32),
        ),
        in_specs=[HBM] * 6 + [VMEM] * (1 + len(ends)),
        out_specs=(VMEM,) * 7,
        scratch_shapes=[
            pltpu.VMEM((nl, cols), f32),
            pltpu.VMEM((nl, cols), f32),
            pltpu.VMEM((nl, cols), f32),
            pltpu.VMEM((cz, nl), f32),
            pltpu.VMEM((cz, nl), f32),
            pltpu.VMEM((2, cz, cz), f32),
            pltpu.SemaphoreType.DMA((6,)),
        ],
        compiler_params=pltpu.CompilerParams(vmem_limit_bytes=VMEM_PACK),
        cost_estimate=pl.CostEstimate(flops=10**8, bytes_accessed=10**6, transcendentals=0),
        name="base",
    )(
        *[
            in_hbm(x)
            for x in (
                *fields,
                layer_index_downscale,
                layer_index_upscale.T,
                jnp.asarray(lin, f32),
            )
        ],
        pos,
        *ends,
    )
    halo = (periodic_flow_velocity, jnp.asarray(ends_pick(), bf16)) if carry else ()
    vals, *halo = pl.pallas_call(
        functools.partial(cloud_kernel, devices, carry, nl),
        out_shape=(jax.ShapeDtypeStruct((devices * rows, LANE), f32),)
        + ((jax.ShapeDtypeStruct((nl, LANE), f32),) if carry else ()),
        in_specs=[VMEM] * (13 + len(halo)),
        out_specs=(VMEM,) * (2 if carry else 1),
        scratch_shapes=[
            pltpu.VMEM((tiles, cz, SUB * (groups + 2), LANE), f32),
            pltpu.VMEM((zp, cols), f32),
            pltpu.VMEM((zp, cols), f32),
            pltpu.VMEM((zp, cols), f32),
            pltpu.VMEM((zp, cols), f32),
            pltpu.VMEM((zp, cols), f32),
            pltpu.VMEM((zp + head, cols), f32),
            pltpu.VMEM((3 * zp, cols), f32),
            pltpu.VMEM((2 * tiles, zp * SUB, LANE), f32),
        ],
        compiler_params=pltpu.CompilerParams(vmem_limit_bytes=VMEM_CLOUD),
        name="cloud",
    )(r1, *prep, *halved(mean[:3 * zp]), *halved(mean[3 * zp:]), gain, *halo)
    r2 = exchange(vals, 1, rows * LANE)
    return pl.pallas_call(
        functools.partial(finish_kernel, devices, carry),
        out_shape=(field,) * 3,
        in_specs=[VMEM] * (8 + len(halo)),
        out_specs=(VMEM,) * 3,
        compiler_params=pltpu.CompilerParams(vmem_limit_bytes=VMEM_PACK),
        name="finish",
    )(r2, pos, *base, *halo)


VMEM_PACK = 16 * 2**20
VMEM_CLOUD = 24 * 2**20


def solution(mesh):
    in_specs = (
        P(None, AXES),
        P(None, AXES),
        P(None, AXES),
        P(AXES),
        P(None, None, AXES),
        P(),
        P(),
    )
    out_specs = (P(None, AXES), P(None, AXES), P(None, AXES))
    return jax.shard_map(local, mesh=mesh, in_specs=in_specs, out_specs=out_specs, check_vma=False)
```

```python
import functools

import numpy as np

import jax
import jax.numpy as jnp
from jax import lax
from jax.experimental import pallas as pl
from jax.experimental.pallas import tpu as pltpu
from jax.sharding import PartitionSpec as P

SUBSTEPS = 10

loop_diff = 0.35
mix_along = 0.35
mix_vertical = 0.1
cond_rate = 0.1
latent_heat = 1.5
max_speed = 0.8

AXES = ("tile", "crm")
LOG2E = 1.4426950408889634
LN2 = 0.6931471805599453
SUB = 8
LANE = 128
HI = lax.Precision.HIGH
VMEM = pl.BlockSpec(memory_space=pltpu.VMEM)
HBM = pl.BlockSpec(memory_space=pltpu.HBM)


def in_hbm(x):
    return pltpu.with_memory_space_constraint(x, pltpu.HBM)


def fetch(sources, targets, sem):
    copies = [
        pltpu.make_async_copy(a, b, sem.at[n]) for n, (a, b) in enumerate(zip(sources, targets))
    ]
    for copy in copies:
        copy.start()
    return copies


def up_to(n, m):
    return -(-n // m) * m


def edges(block):
    count = lax.axis_size(AXES)
    forward = [(i, (i + 1) % count) for i in range(count)]
    backward = [(t, s) for s, t in forward]
    low = lax.ppermute(block[:, :, -1:], AXES, forward)
    high = lax.ppermute(block[:, :, :1], AXES, backward)
    return low, high


def ring_mean_operator(levels):
    f = np.eye(levels)
    east = west = f
    above = np.concatenate([f[1:], f[-1:]], axis=0)
    below = np.concatenate([f[:1], f[:-1]], axis=0)
    return (
        f
        + mix_along * (east - 2.0 * f + west)
        + mix_vertical * (above - 2.0 * f + below)
    )


def mean_operators(levels):
    v = ring_mean_operator(levels)
    power = np.eye(levels)
    total = np.zeros((levels, levels))
    for _ in range(SUBSTEPS):
        total = total + power
        power = v @ power
    return power, total / SUBSTEPS


def shift_operators(levels):
    drain = cond_rate * (1.0 + 0.5 * latent_heat)
    rest = (1.0 + drain) * np.eye(levels) - ring_mean_operator(levels)
    scale = LOG2E / SUBSTEPS
    return -np.linalg.inv(rest) * scale, -rest / scale


def halved(x):
    a = np.asarray(x, jnp.bfloat16)
    b = np.asarray(x - a.astype(np.float64), jnp.bfloat16)
    return jnp.asarray(a), jnp.asarray(b)


def split(x):
    a = x.astype(jnp.bfloat16)
    return a, (x - a.astype(jnp.float32)).astype(jnp.bfloat16)


def dot3(a, b, ca, cb):
    return dot(a[0], b[0], ca, cb) + dot(a[0], b[1], ca, cb) + dot(a[1], b[0], ca, cb)


def dot(a, b, ca, cb, precision=None):
    return lax.dot_general(
        a, b, (((ca,), (cb,)), ((), ())), precision=precision, preferred_element_type=jnp.float32
    )


def advection(f, v, low, high):
    cols = f.shape[1]
    lane = lax.broadcasted_iota(jnp.int32, f.shape, 1)
    ahead = jnp.where(lane == cols - 1, high, pltpu.roll(f, cols - 1, 1))
    behind = jnp.where(lane == 0, low, pltpu.roll(f, 1, 1))
    return -v * (ahead - behind) * 0.5 + loop_diff * (ahead - 2.0 * f + behind)


def onehot(pos_row, cols):
    place = lax.broadcasted_iota(jnp.int32, (cols, cols), 0)
    return jnp.where(place == pos_row, 1.0, 0.0).astype(jnp.bfloat16)


SLOT = 32
SLOTS = LANE // SLOT


def return_shape(cz, per):
    head = (LANE - 2 * cz) // SUB * SUB
    assert 0 <= head <= cz and cz - head <= SLOT
    return head, per + -(-per // SLOTS)


def slot_onehot(place_row, devices, per, cols):
    row = place_row % per // SLOTS * devices + place_row // per
    rows = -(-per // SLOTS) * devices
    return jnp.where(
        lax.broadcasted_iota(jnp.int32, (rows, cols), 0) == row, 1.0, 0.0
    ).astype(jnp.bfloat16)


CARRIED = (
    (0, 1, 0), (0, 0, 0), (0, 0, 1), (0, 1, 1),
    (1, 0, 0), (1, 1, 0), (1, 0, 1), (1, 1, 1),
)


def row_of(field, half, end):
    return CARRIED.index((field, half, end))


def halves(levels):
    first = up_to(-(-levels // 2), SUB)
    return first, levels - first


def carries(levels, per, width):
    first, second = halves(levels)
    return per >= len(CARRIED) and 3 * levels + first <= width and second < first


def pack_kernel(devices, carry, *refs):
    low_ref, high_ref = (None, None) if carry else refs[4:6]
    out_ref, pos_ref, s_ref, t_ref, q_ref, v_ref, own_ref, sem = refs[-8:]
    copies = [
        pltpu.make_async_copy(source, target, sem.at[n])
        for n, (source, target) in enumerate(zip(refs[:4], (t_ref, q_ref, v_ref, own_ref)))
    ]
    for n in (3, 0, 1, 2):
        copies[n].start()
    nl, cols = t_ref.shape
    width = s_ref.shape[0]
    per = cols // devices
    copies[3].wait()
    own = own_ref[...]
    who = lax.broadcasted_iota(jnp.int32, (devices, cols), 0)
    mine = jnp.where(who == own, 1.0, 0.0)
    before = lax.broadcasted_iota(jnp.int32, (cols, cols), 0) < lax.broadcasted_iota(
        jnp.int32, (cols, cols), 1
    )
    tri = jnp.where(before, 1.0, 0.0).astype(jnp.bfloat16)
    ranks = dot(mine.astype(jnp.bfloat16), tri, 1, 0)
    rank = jnp.sum(ranks * mine, axis=0, keepdims=True)
    pos = own * per + rank.astype(jnp.int32)
    pos_ref[...] = pos
    sel = onehot(pos, cols)

    for n in range(3):
        copies[n].wait()
    t = t_ref[...]
    x = q_ref[...] - 0.5 * t
    v = v_ref[...]
    if carry:
        low = high = jnp.zeros((nl, 1), jnp.float32)
    else:
        low = low_ref[1] - 0.5 * low_ref[0]
        high = high_ref[1] - 0.5 * high_ref[0]
    s_ref[0:nl, :] = x
    s_ref[nl:2 * nl, :] = v
    s_ref[2 * nl:3 * nl, :] = advection(x, v, low, high)
    rest = width - 3 * nl
    if rest:
        s_ref[3 * nl:, :] = jnp.zeros((rest, cols), jnp.float32)
    if carry:
        first, second = halves(nl)
        lane = lax.broadcasted_iota(jnp.int32, (1, cols), 1)
        s_ref[3 * nl + second:3 * nl + second + 1, :] = jnp.where(
            (lane == 0) | (lane == cols - 1), 1.0, 0.0
        )
    a, b = split(s_ref[...])
    if carry:
        shape = (SUB, cols)
        row = lax.broadcasted_iota(jnp.int32, shape, 0)
        want = jnp.zeros(shape, jnp.int32)
        for r, (_, _, end) in enumerate(CARRIED):
            want = jnp.where(row == r, end * (cols - 1), want)
        pick = jnp.where(lax.broadcasted_iota(jnp.int32, shape, 1) == want, 1.0, 0.0).astype(
            jnp.bfloat16
        )
        row = lax.broadcasted_iota(jnp.int32, (SUB, width), 0)
        lane = lax.broadcasted_iota(jnp.int32, (SUB, width), 1)
        ends = jnp.zeros((SUB, width), jnp.float32)
        for field, terms in enumerate(((a[:nl], b[:nl]), split(t))):
            found = dot(pick, terms[0], 1, 1) + dot(pick, terms[1], 1, 1)
            found = jnp.concatenate([found, jnp.zeros((SUB, width - nl), jnp.float32)], axis=1)
            for half, (start, size) in enumerate(((0, first), (first, second))):
                mine = functools.reduce(
                    jnp.logical_or,
                    [row == r for r, c in enumerate(CARRIED) if c[:2] == (field, half)],
                )
                mine = mine & (lane >= 3 * nl) & (lane < 3 * nl + size)
                ends = jnp.where(mine, pltpu.roll(found, 3 * nl - start, 1), ends)
    out = dot(sel, a, 1, 1) + dot(sel, b, 1, 1)
    if carry:
        out = (out.reshape(devices, per, width) + ends[None]).reshape(cols, width)
    out_ref[...] = out


LARGEST = 60.0


def moved_softplus2(small, g, move):
    if small:
        return jnp.log2(move + jnp.exp2(g))
    return move + softplus2(g - move)


def moved_sum(small, parts, move):
    if not small:
        return [moved_softplus2(small, g, move) for g in parts]
    powers = [move + jnp.exp2(g) for g in parts]
    pairs = [a * b for a, b in zip(powers[::2], powers[1::2])] + powers[len(powers) // 2 * 2:]
    return [jnp.log2(p) for p in pairs]


def softplus2(f):
    return jnp.maximum(f, jnp.log2(1.0 + jnp.exp2(jnp.minimum(f, 100.0))))


def lanes(k):
    return pl.ds(k * LANE, LANE)


def fold(part_ref, levels, scale):
    total = part_ref[pl.ds(0, levels, stride=SUB), :]
    for s in range(1, SUB):
        total = total + part_ref[pl.ds(s, levels, stride=SUB), :]
    return total * scale


def clear_tail(part_ref, cz):
    for n in range(part_ref.shape[0]):
        for z in range(cz * SUB, part_ref.shape[1], SUB):
            part_ref[n, pl.ds(z, SUB), :] = jnp.zeros((SUB, LANE), jnp.float32)


def prep_kernel(carry, td_ref, down_hbm, shift_hbm, after_ref, start_ref, mean_ref, most_ref,
                high_ref, low_ref, shift_high_ref, shift_low_ref, raw_ref, part_ref, down_ref,
                shift_ref, td_sem, sem):
    del after_ref
    cz, cx, cols = td_ref.shape
    nl = down_ref.shape[1]
    zp = mean_ref.shape[0]
    width = high_ref.shape[1]
    groups = cx // SUB
    tiles = cols // LANE
    chunk = -(-cz // td_sem.shape[1])

    def td_copy(k, c):
        levels = pl.ds(c * chunk, min(chunk, cz - c * chunk))
        return pltpu.make_async_copy(
            td_ref.at[levels, :, lanes(k)], raw_ref.at[k, levels], td_sem.at[k, c]
        )

    copies = fetch((down_hbm, shift_hbm), (down_ref, shift_ref), sem)
    for k in range(tiles):
        for c in range(td_sem.shape[1]):
            td_copy(k, c).start()
    for copy in copies:
        copy.wait()

    def wide(rows):
        rows = jnp.concatenate(
            [rows, jnp.zeros((rows.shape[0], width - nl), jnp.float32)], axis=1
        )
        return jnp.concatenate([rows, jnp.zeros((zp - cz, width), jnp.float32)], axis=0)

    down = wide(down_ref[...])
    shift = wide(dot(shift_ref[...], down_ref[...], 1, 0, lax.Precision.HIGHEST))
    blocks = jnp.concatenate(
        [down, pltpu.roll(down, nl, 1), pltpu.roll(shift, 2 * nl, 1)], axis=0
    )
    a, low_ref[...] = split(blocks)
    offset = high_ref.shape[0] - 3 * zp
    if carry:
        shape = (offset, width)
        row = lax.broadcasted_iota(jnp.int32, shape, 0)
        to = jnp.where(row < nl, row + nl, row + 2 * nl)
        high_ref[0:offset, :] = jnp.where(
            lax.broadcasted_iota(jnp.int32, shape, 1) == to, 1.0, 0.0
        ).astype(jnp.bfloat16)
    high_ref[offset:, :] = a
    shift_high_ref[...], shift_low_ref[...] = split(shift[:, :nl])

    clear_tail(part_ref, cz)
    most = [jnp.zeros((SUB, LANE), jnp.float32)] * groups
    for k in range(tiles):
        for z in range(cz):
            if z % chunk == 0:
                td_copy(k, z // chunk).wait()
            total = None
            for i in range(groups):
                td = raw_ref[k, z, pl.ds(i, SUB, stride=groups), :]
                total = td if total is None else total + td
                first = (-0.5 * LOG2E) * td
                start_ref[k, z, pl.ds(SUB * i, SUB), :] = first
                most[i] = jnp.maximum(most[i], jnp.abs(first))
            part_ref[k, pl.ds(z * SUB, SUB), :] = total
        mean_ref[:, lanes(k)] = fold(part_ref.at[k], zp, 1.0 / cx)
    most_ref[...] = functools.reduce(jnp.maximum, most)


def cloud_kernel(devices, carry, nl, r_ref, start_ref, td_mean_ref, most_ref, g_high_ref, g_low_ref,
                 shift_high_ref, shift_low_ref, early_high_ref, early_low_ref,
                 late_high_ref, late_low_ref, after_ref, *refs):
    gain_ref, v_ref, ends_ref = (after_ref, *refs[:2]) if carry else (None,) * 3
    out_ref, halo_ref = refs[2:4] if carry else (refs[0], None)
    d_ref, base_ref, east_ref, west_ref, shift_ref, scale_ref, late_ref, value_ref, part_ref = (
        refs[-9:]
    )
    tiles, cz, cx, _ = start_ref.shape
    zp, cols = td_mean_ref.shape
    per = cols // devices
    groups = cx // SUB

    r = split(r_ref[...])
    offset = g_high_ref.shape[0] - 3 * zp
    prof = dot(g_high_ref[...], r[0], 1, 1) + dot(g_high_ref[...], r[1], 1, 1)
    fine = dot(g_low_ref[...], r[0], 1, 1)
    shift = prof[offset + 2 * zp:] + fine[2 * zp:]
    if carry:
        first, second = halves(nl)
        v = prof[0:nl]
        ends = prof[nl:offset]
        flag = ends[second:second + 1] > 0.5
        place = lax.rem(lax.broadcasted_iota(jnp.int32, (1, cols), 1), per)

        def neighbour(end, at):
            step = per if at == 0 else -per
            shift = lambda half: (step + at - row_of(0, half, end)) % cols
            return jnp.concatenate(
                [pltpu.roll(ends, shift(0), 1), pltpu.roll(ends, shift(1), 1)[:second]], axis=0
            )

        behind = neighbour(1, 0) * (loop_diff + 0.5 * v)
        ahead = neighbour(0, per - 1) * (loop_diff - 0.5 * v)
        halo = jnp.where(flag & (place == 0), behind, 0.0) + jnp.where(
            flag & (place == per - 1), ahead, 0.0
        )
        shift = shift + dot3((shift_high_ref[...], shift_low_ref[...]), split(halo), 1, 0)
    d0 = prof[offset:offset + zp] + fine[0:zp]
    speed = max_speed * jnp.tanh(prof[offset + zp:offset + 2 * zp] + fine[zp:2 * zp])
    base = d0 * LOG2E + shift
    base_ref[...] = base
    east_ref[...] = mix_along - 0.5 * speed
    west_ref[...] = mix_along + 0.5 * speed
    shift_ref[...] = shift
    scale_ref[...] = jnp.exp2(shift)
    drain = cond_rate * (1.0 + 0.5 * latent_heat)
    rate = 1.0 - 2.0 * mix_along + max(2.0 * mix_along, max_speed)
    growth = rate**SUBSTEPS
    series = sum(rate**n for n in range(SUBSTEPS))
    bound = growth * (jnp.max(jnp.abs(base)) + jnp.max(most_ref[...])) + series * drain * (
        jnp.max(jnp.abs(shift)) + 1.0
    )
    value_ref[0:zp, :] = td_mean_ref[...]
    value_ref[zp:2 * zp, :] = d0 - 0.5 * td_mean_ref[...]
    value_ref[2 * zp:, :] = shift
    clear_tail(part_ref, cz)

    def row_at(ref, z, k):
        return jnp.broadcast_to(ref[pl.ds(z, 1), lanes(k)], (SUB, LANE))

    slot = [0] + [SUB * (i + 1) for i in range(1, groups)]
    last = slot[-1]

    def get(k, z):
        return [d_ref[k, z, pl.ds(slot[i], SUB), :] for i in range(groups)]

    def put(k, z, i, new):
        d_ref[k, z, pl.ds(slot[i], SUB), :] = new
        if i == 0:
            d_ref[k, z, pl.ds(SUB, SUB), :] = new
        if i == groups - 1:
            d_ref[k, z, pl.ds(last + SUB, SUB), :] = new

    for k in range(tiles):
        for z in range(cz):
            base = row_at(base_ref, z, k)
            for i in range(groups):
                put(k, z, i, base + start_ref[k, z, pl.ds(SUB * i, SUB), :])

    def step(small, _, carry):
        for k in range(tiles):
            below = cur = get(k, 0)
            pair = None
            for z in range(cz):
                above = get(k, z + 1) if z + 1 < cz else cur
                if pair is None:
                    pair = [c + a for c, a in zip(cur, above)]
                    column = [p + b for p, b in zip(pair, below)]
                else:
                    column = [p + a for p, a in zip(pair, above)]
                    pair = None
                ea = row_at(east_ref, z, k)
                we = row_at(west_ref, z, k)
                move = row_at(scale_ref if small else shift_ref, z, k)
                ring = [d_ref[k, z, pl.ds(last + SUB - 1, SUB), :]] + cur
                ring = ring + [d_ref[k, z, pl.ds(1, SUB), :]]
                for i in range(groups):
                    new = (
                        mix_vertical * column[i]
                        + ea * ring[i + 2]
                        + we * ring[i]
                        - drain * moved_softplus2(small, cur[i], move)
                    )
                    put(k, z, i, new)
                below, cur = cur, above
        return carry

    def finish(small):
        lax.fori_loop(0, SUBSTEPS, functools.partial(step, small), 0)
        head, rows = return_shape(cz, per)
        cloud_ref = east_ref
        early = [None] * tiles

        def sums(k):
            for z in range(cz):
                total = cloud = None
                move = row_at(scale_ref if small else shift_ref, z, k)
                for c in moved_sum(small, get(k, z), move):
                    cloud = c if cloud is None else cloud + c
                for f in get(k, z):
                    total = f if total is None else total + f
                part_ref[2 * k, pl.ds(z * SUB, SUB), :] = total
                part_ref[2 * k + 1, pl.ds(z * SUB, SUB), :] = cloud

        def known(k):
            early[k] = dot3(
                split(value_ref[:, lanes(k)]), (early_high_ref[...], early_low_ref[...]), 0, 0
            )

        def ends_part():
            if carry:
                halo = halo_part(devices, r_ref, ends_ref, v_ref)
                halo_ref[...] = halo + dot(gain_ref[...], halo, 1, 0, HI)

        def close(k):
            moved = LN2 * shift_ref[:, lanes(k)]
            end = fold(part_ref.at[2 * k], zp, LN2 / cx) - moved
            cloud = fold(part_ref.at[2 * k + 1], zp, LN2 / cx) - moved
            late_ref[0:zp, lanes(k)] = end
            late_ref[zp:, lanes(k)] = cloud[0:head]
            cloud_ref[:, lanes(k)] = cloud
            late = dot3(split(late_ref[:, lanes(k)]), (late_high_ref[...], late_low_ref[...]), 0, 0)
            main = early[k] + late
            for h in range(LANE // per):
                out_ref[pl.ds((k * (LANE // per) + h) * rows, per), :] = main[h * per:(h + 1) * per]

        for k in range(tiles):
            sums(k)
            if k == 0:
                for n in range(tiles):
                    known(n)
            if k == 1:
                ends_part()
            close(k)
        left = cloud_ref[head:, :]
        left = jnp.concatenate([left, jnp.zeros((SLOT - left.shape[0], cols), jnp.float32)], axis=0) \
            if left.shape[0] < SLOT else left
        place = lax.broadcasted_iota(jnp.int32, (1, cols), 1)
        part = place % per % SLOTS
        spread = jnp.concatenate(
            [jnp.where(part == j, left, 0.0) for j in range(SLOTS)], axis=0
        )
        pick = slot_onehot(place, devices, per, cols)
        a, b = split(spread)
        extra = dot(pick, a, 1, 1) + dot(pick, b, 1, 1)
        for i in range(rows - per):
            out_ref[pl.ds(per + i, devices, stride=rows), :] = extra[i * devices:(i + 1) * devices]

    @pl.when(bound < LARGEST)
    def _():
        finish(True)

    @pl.when(jnp.logical_not(bound < LARGEST))
    def _():
        finish(False)


def base_kernel(devices, carry, *refs):
    pos_ref = refs[6]
    low_ref, high_ref = (None, None) if carry else refs[7:9]
    to_ref, qo_ref, level_high_ref, level_low_ref = refs[-14:-10]
    sel_ref, pick_ref, gain_ref = refs[-10:-7]
    t_ref, q_ref, v_ref, down_ref, up_ref, lin_ref, sem = refs[-7:]
    copies = fetch(refs[:6], refs[-7:-1], sem)
    nl, cols = t_ref.shape
    cz = up_ref.shape[0]
    per = cols // devices
    head, _ = return_shape(cz, per)
    sel_ref[...] = onehot(pos_ref[...], cols)
    pick_ref[...] = slot_onehot(pos_ref[...], devices, per, cols)
    for copy in copies:
        copy.wait()
    up = up_ref[...].T
    wide = jnp.concatenate([up, jnp.zeros((nl, LANE - cz), jnp.float32)], axis=1)
    lane = lax.broadcasted_iota(jnp.int32, wide.shape, 1)
    level = jnp.concatenate(
        [
            wide,
            -pltpu.roll(wide, cz, 1),
            pltpu.roll(jnp.where(lane < head, wide, 0.0), 2 * cz, 1),
        ],
        axis=0,
    )
    rest = jnp.where(lane < SLOT, pltpu.roll(wide, LANE - head, 1), 0.0)[:, 0:SLOT]
    rest = jnp.concatenate([jnp.zeros((2 * nl, SLOT), jnp.float32), rest], axis=0)
    level_high_ref[...], level_low_ref[...] = split(jnp.concatenate([level, rest], axis=1))
    if carry:
        low = high = (jnp.zeros((nl, 1), jnp.float32),) * 2
    else:
        low = (low_ref[0], low_ref[1])
        high = (high_ref[0], high_ref[1])
    v = v_ref[...]
    t = t_ref[...]
    q = q_ref[...]
    advt = advection(t, v, low[0], high[0])
    advq = advection(q, v, low[1], high[1])
    prof = dot(down_ref[...], jnp.concatenate([t, q, advt, advq], axis=1), 1, 0, HI)
    lin = lin_ref[...]
    gain = dot(lin[0], prof[:, :2 * cols], 1, 0, HI) + dot(lin[1], prof[:, 2 * cols:], 1, 0, HI)
    gain = dot(up, gain, 1, 0, HI)
    to_ref[...] = t + advt + gain[:, :cols]
    qo_ref[...] = q + advq + gain[:, cols:]
    gain_ref[...] = dot(up, dot(lin[1], down_ref[...], 1, 0, HI), 1, 0, HI)


def ends_pick():
    pick = np.zeros((2 * SUB, 2 * LANE))
    for r, (field, half, end) in enumerate(CARRIED):
        row = r + (0 if end else SUB)
        place = half * LANE + (0 if end else 1)
        if field:
            pick[row, place] = 1.0
        pick[row, place + 2] = 0.5 if field else 1.0
    return pick


def halo_part(devices, r_ref, ends_ref, v_ref):
    nl, cols = v_ref.shape
    per = cols // devices
    first, second = halves(nl)
    me = lax.axis_index(AXES)

    def block(device):
        start = pl.multiple_of(device * per, SUB)
        return r_ref[pl.ds(start, SUB), :]

    rows = jnp.concatenate(
        [block(lax.rem(me + devices - 1, devices)), block(lax.rem(me + 1, devices))], axis=0
    )
    rows = pltpu.roll(rows, rows.shape[1] - 3 * nl, 1)[:, :LANE]
    a, b = split(rows)
    pick = ends_ref[...]
    part = dot(a, pick, 0, 0) + dot(b, pick, 0, 0)
    ends = jnp.concatenate([part[:first, :LANE], part[:second, LANE:]], axis=0)
    lane = lax.broadcasted_iota(jnp.int32, ends.shape, 1)
    low = v_ref[:, :LANE]
    high = v_ref[:, cols - LANE:]
    v = jnp.where(
        lane == 0, low, jnp.where(lane == 2, pltpu.roll(low, 2, 1), jnp.where(
            lane == 1, -pltpu.roll(high, 2, 1), -pltpu.roll(high, 4, 1)))
    )
    return (loop_diff + 0.5 * v) * ends


def add_ends(field_ref, out_ref, extra, halo, place):
    cols = field_ref.shape[1]
    lane = lax.broadcasted_iota(jnp.int32, halo.shape, 1)
    start = pltpu.roll(halo, LANE - place, 1) if place else halo
    stop = pltpu.roll(halo, LANE - 2 - place, 1)
    parts = [extra[:, k:k + LANE] for k in range(0, cols, LANE)]
    parts[0] = parts[0] + jnp.where(lane == 0, start, 0.0)
    parts[-1] = parts[-1] + jnp.where(lane == LANE - 1, stop, 0.0)
    for k, part in enumerate(parts):
        out_ref[:, lanes(k)] = field_ref[:, lanes(k)] + part


def finish_kernel(devices, carry, *refs):
    r_ref, pos_ref, tb_ref, qb_ref = refs[:4]
    level_high_ref, level_low_ref, sel_ref, pick_ref = refs[4:8]
    to_ref, qo_ref, co_ref = refs[-3:]
    nl, cols = tb_ref.shape
    per = cols // devices
    rows = r_ref.shape[0] // devices
    main = jnp.concatenate([r_ref[pl.ds(h * rows, per), :] for h in range(devices)], axis=0)
    a, b = split(main)
    values = dot(a, sel_ref[...], 0, 0) + dot(b, sel_ref[...], 0, 0)
    extra = jnp.concatenate(
        [r_ref[pl.ds(per + i, devices, stride=rows), :] for i in range(rows - per)], axis=0
    )
    a, b = split(extra)
    extra = dot(a, pick_ref[...], 0, 0) + dot(b, pick_ref[...], 0, 0)
    part = pos_ref[...] % per % SLOTS
    left = jnp.where(part == 0, extra[:SLOT], 0.0)
    for j in range(1, SLOTS):
        left = left + jnp.where(part == j, extra[j * SLOT:(j + 1) * SLOT], 0.0)
    values = split(jnp.concatenate([values, left], axis=0))
    out = dot3((level_high_ref[...], level_low_ref[...]), values, 1, 0)
    if carry:
        halo = refs[8][...]
        add_ends(tb_ref, to_ref, out[0:nl], halo, 0)
        add_ends(qb_ref, qo_ref, out[nl:2 * nl], halo, 2)
    else:
        to_ref[...] = tb_ref[...] + out[0:nl]
        qo_ref[...] = qb_ref[...] + out[nl:2 * nl]
    co_ref[...] = out[2 * nl:3 * nl]


def local(
    thermal_anomaly,
    vapour_anomaly,
    periodic_flow_velocity,
    processor_assignment,
    thermal_disturbance,
    layer_index_downscale,
    layer_index_upscale,
):
    nl, cols = thermal_anomaly.shape
    cz, cx, _ = thermal_disturbance.shape
    devices = lax.axis_size(AXES)
    per = cols // devices
    zp = up_to(cz, SUB)
    f32 = jnp.float32
    width = up_to(3 * nl, LANE)
    head, rows = return_shape(cz, per)
    field = jax.ShapeDtypeStruct((nl, cols), f32)
    carry = carries(nl, per, width)

    fields = (thermal_anomaly, vapour_anomaly, periodic_flow_velocity)
    ends = () if carry else edges(jnp.stack(fields[:2]))
    out, pos = pl.pallas_call(
        functools.partial(pack_kernel, devices, carry),
        out_shape=(
            jax.ShapeDtypeStruct((cols, width), f32),
            jax.ShapeDtypeStruct((1, cols), jnp.int32),
        ),
        in_specs=[HBM] * 4 + [VMEM] * len(ends),
        out_specs=(VMEM,) * 2,
        scratch_shapes=[
            pltpu.VMEM((width, cols), f32),
            pltpu.VMEM((nl, cols), f32),
            pltpu.VMEM((nl, cols), f32),
            pltpu.VMEM((nl, cols), f32),
            pltpu.VMEM((1, cols), jnp.int32),
            pltpu.SemaphoreType.DMA((4,)),
        ],
        compiler_params=pltpu.CompilerParams(vmem_limit_bytes=VMEM_PACK),
        name="pack",
    )(*[in_hbm(f) for f in (*fields, processor_assignment.reshape(1, cols))], *ends)

    def exchange(blocks, *inner):
        shape = blocks.shape
        blocks = blocks.reshape(devices, *inner)
        return lax.all_to_all(blocks, AXES, split_axis=0, concat_axis=0, tiled=True).reshape(shape)

    r1 = exchange(out, per, width)

    power, total = mean_operators(cz)
    release = 1.0 + 0.5 * latent_heat
    shift, unshift = shift_operators(cz)
    mean = np.zeros((4 * zp + head, LANE))
    z_part = np.zeros((4 * zp + head, cz))
    z_part[zp:zp + cz] = power.T / release
    z_part[2 * zp:2 * zp + cz] = (total @ unshift).T / release
    z_part[3 * zp:3 * zp + cz] = -np.eye(cz) / release
    mean[0:cz, 0:cz] = power.T
    mean[:, 0:cz] += latent_heat * z_part
    mean[:, cz:2 * cz] = z_part
    mean[4 * zp:, 2 * cz:2 * cz + head] = np.eye(head)

    tiles = cols // LANE
    groups = cx // SUB
    level_rows = 3 * zp + (nl + halves(nl)[0] if carry else 0)
    bf16 = jnp.bfloat16
    prep = pl.pallas_call(
        functools.partial(prep_kernel, carry),
        out_shape=(
            jax.ShapeDtypeStruct((tiles, cz, cx, LANE), f32),
            jax.ShapeDtypeStruct((zp, cols), f32),
            jax.ShapeDtypeStruct((SUB, LANE), f32),
            jax.ShapeDtypeStruct((level_rows, width), bf16),
            jax.ShapeDtypeStruct((3 * zp, width), bf16),
            jax.ShapeDtypeStruct((zp, nl), bf16),
            jax.ShapeDtypeStruct((zp, nl), bf16),
        ),
        in_specs=[HBM, HBM, HBM, VMEM],
        out_specs=(VMEM,) * 7,
        scratch_shapes=[
            pltpu.VMEM((tiles, cz, cx, LANE), f32),
            pltpu.VMEM((tiles, zp * SUB, LANE), f32),
            pltpu.VMEM((cz, nl), f32),
            pltpu.VMEM((cz, cz), f32),
            pltpu.SemaphoreType.DMA((tiles, 5)),
            pltpu.SemaphoreType.DMA((2,)),
        ],
        compiler_params=pltpu.CompilerParams(vmem_limit_bytes=VMEM_PACK),
        cost_estimate=pl.CostEstimate(flops=10**8, bytes_accessed=4 * 10**6, transcendentals=0),
        name="prep",
    )(
        in_hbm(thermal_disturbance),
        in_hbm(layer_index_downscale),
        in_hbm(jnp.asarray(shift, f32)),
        pos,
    )
    lin = np.stack([power - np.eye(cz), total])
    *base, gain = pl.pallas_call(
        functools.partial(base_kernel, devices, carry),
        out_shape=(
            field,
            field,
            jax.ShapeDtypeStruct((3 * nl, LANE + SLOT), bf16),
            jax.ShapeDtypeStruct((3 * nl, LANE + SLOT), bf16),
            jax.ShapeDtypeStruct((cols, cols), bf16),
            jax.ShapeDtypeStruct((devices * (rows - per), cols), bf16),
            jax.ShapeDtypeStruct((nl, nl), f32),
        ),
        in_specs=[HBM] * 6 + [VMEM] * (1 + len(ends)),
        out_specs=(VMEM,) * 7,
        scratch_shapes=[
            pltpu.VMEM((nl, cols), f32),
            pltpu.VMEM((nl, cols), f32),
            pltpu.VMEM((nl, cols), f32),
            pltpu.VMEM((cz, nl), f32),
            pltpu.VMEM((cz, nl), f32),
            pltpu.VMEM((2, cz, cz), f32),
            pltpu.SemaphoreType.DMA((6,)),
        ],
        compiler_params=pltpu.CompilerParams(vmem_limit_bytes=VMEM_PACK),
        cost_estimate=pl.CostEstimate(flops=10**8, bytes_accessed=10**6, transcendentals=0),
        name="base",
    )(
        *[
            in_hbm(x)
            for x in (
                *fields,
                layer_index_downscale,
                layer_index_upscale.T,
                jnp.asarray(lin, f32),
            )
        ],
        pos,
        *ends,
    )
    halo = (periodic_flow_velocity, jnp.asarray(ends_pick(), bf16)) if carry else ()
    vals, *halo = pl.pallas_call(
        functools.partial(cloud_kernel, devices, carry, nl),
        out_shape=(jax.ShapeDtypeStruct((devices * rows, LANE), f32),)
        + ((jax.ShapeDtypeStruct((nl, LANE), f32),) if carry else ()),
        in_specs=[VMEM] * (13 + len(halo)),
        out_specs=(VMEM,) * (2 if carry else 1),
        scratch_shapes=[
            pltpu.VMEM((tiles, cz, SUB * (groups + 2), LANE), f32),
            pltpu.VMEM((zp, cols), f32),
            pltpu.VMEM((zp, cols), f32),
            pltpu.VMEM((zp, cols), f32),
            pltpu.VMEM((zp, cols), f32),
            pltpu.VMEM((zp, cols), f32),
            pltpu.VMEM((zp + head, cols), f32),
            pltpu.VMEM((3 * zp, cols), f32),
            pltpu.VMEM((2 * tiles, zp * SUB, LANE), f32),
        ],
        compiler_params=pltpu.CompilerParams(vmem_limit_bytes=VMEM_CLOUD),
        name="cloud",
    )(r1, *prep, *halved(mean[:3 * zp]), *halved(mean[3 * zp:]), gain, *halo)
    r2 = exchange(vals, 1, rows * LANE)
    return pl.pallas_call(
        functools.partial(finish_kernel, devices, carry),
        out_shape=(field,) * 3,
        in_specs=[VMEM] * (8 + len(halo)),
        out_specs=(VMEM,) * 3,
        compiler_params=pltpu.CompilerParams(vmem_limit_bytes=VMEM_PACK),
        name="finish",
    )(r2, pos, *base, *halo)


VMEM_PACK = 16 * 2**20
VMEM_CLOUD = 24 * 2**20


def solution(mesh):
    in_specs = (
        P(None, AXES),
        P(None, AXES),
        P(None, AXES),
        P(AXES),
        P(None, None, AXES),
        P(),
        P(),
    )
    out_specs = (P(None, AXES), P(None, AXES), P(None, AXES))
    return jax.shard_map(local, mesh=mesh, in_specs=in_specs, out_specs=out_specs, check_vma=False)
```
